32 devices in a mesh: fsdp: 8 (over z, core), tp: 4 (over y, x).
Axes of the slice: x: 2, y: 2, z: 4, core: 2. Of those that a mesh axis runs over, the one named last changes fastest.
Arguments:
- block_in: bfloat16 [12288, 2560], P(('fsdp', 'tp')), may hold values from -6 to 6
- cotangent: bfloat16 [12288, 2560], P(('fsdp', 'tp')), may hold values from -6 to 6
- segment_ids: int32 [8, 1536], P('fsdp'), may hold values from 0 to 3, never falling along the last dimension, each value on 1 to 1152 neighbouring positions
- group_fill: int32 [8], P('fsdp'), may hold values from 1 to 1536, 7680 in all
- input_gain: bfloat16 [2560], P('fsdp'), may hold values from 0.5 to 1.5
- proj_inner: bfloat16 [2560, 2, 5120], P('fsdp', None, 'tp'), may hold values from -0.125 to 0.125
- proj_step: bfloat16 [2560, 80], P('fsdp', 'tp'), may hold values from -0.125 to 0.125
- proj_state: bfloat16 [2560, 256], P('fsdp', 'tp'), may hold values from -0.125 to 0.125
- conv_inner: bfloat16 [5, 5120], P(None, ('tp', 'fsdp')), may hold values from -0.5 to 0.5
- conv_state: bfloat16 [5, 256], P(None, ('tp', 'fsdp')), may hold values from -0.5 to 0.5
- head_params: float32 [3, 80], P(None, 'tp'), may hold values from -7 to 3, as said below
- mixer_gain: bfloat16 [5120], P(('tp', 'fsdp')), may hold values from 0.5 to 1.5
- proj_output: bfloat16 [5120, 2560], P('tp', 'fsdp'), may hold values from -0.078125 to 0.078125
- first_input_gain: float32 [2560], P('fsdp'), may hold values from -32 to 32
- first_proj_inner: float32 [2560, 2, 5120], P('fsdp', None, 'tp'), may hold values from -32 to 32
- first_proj_step: float32 [2560, 80], P('fsdp', 'tp'), may hold values from -32 to 32
- first_proj_state: float32 [2560, 256], P('fsdp', 'tp'), may hold values from -32 to 32
- first_conv_inner: float32 [5, 5120], P(None, ('tp', 'fsdp')), may hold values from -32 to 32
- first_conv_state: float32 [5, 256], P(None, ('tp', 'fsdp')), may hold values from -32 to 32
- first_head_params: float32 [3, 80], P(None, 'tp'), may hold values from -32 to 32
- first_mixer_gain: float32 [5120], P(('tp', 'fsdp')), may hold values from -32 to 32
- first_proj_output: float32 [5120, 2560], P('tp', 'fsdp'), may hold values from -32 to 32
- second_input_gain: float32 [2560], P('fsdp'), may hold values from 30.72 to 122.88
- second_proj_inner: float32 [2560, 2, 5120], P('fsdp', None, 'tp'), may hold values from 30.72 to 122.88
- second_proj_step: float32 [2560, 80], P('fsdp', 'tp'), may hold values from 30.72 to 122.88
- second_proj_state: float32 [2560, 256], P('fsdp', 'tp'), may hold values from 30.72 to 122.88
- second_conv_inner: float32 [5, 5120], P(None, ('tp', 'fsdp')), may hold values from 30.72 to 122.88
- second_conv_state: float32 [5, 256], P(None, ('tp', 'fsdp')), may hold values from 30.72 to 122.88
- second_head_params: float32 [3, 80], P(None, 'tp'), may hold values from 30.72 to 122.88
- second_mixer_gain: float32 [5120], P(('tp', 'fsdp')), may hold values from 30.72 to 122.88
- second_proj_output: float32 [5120, 2560], P('tp', 'fsdp'), may hold values from 30.72 to 122.88
Outputs:
- block_out: bfloat16 [12288, 2560], P(('fsdp', 'tp'))
- d_input: bfloat16 [12288, 2560], P(('fsdp', 'tp'))
- grad_input_gain: float32 [2560], P('fsdp')
- grad_proj_inner: float32 [2560, 2, 5120], P('fsdp', None, 'tp')
- grad_proj_step: float32 [2560, 80], P('fsdp', 'tp')
- grad_proj_state: float32 [2560, 256], P('fsdp', 'tp')
- grad_conv_inner: float32 [5, 5120], P(None, ('tp', 'fsdp'))
- grad_conv_state: float32 [5, 256], P(None, ('tp', 'fsdp'))
- grad_head_params: float32 [3, 80], P(None, 'tp')
- grad_mixer_gain: float32 [5120], P(('tp', 'fsdp'))
- grad_proj_output: float32 [5120, 2560], P('tp', 'fsdp')
- new_input_gain: bfloat16 [2560], P('fsdp')
- new_proj_inner: bfloat16 [2560, 2, 5120], P('fsdp', None, 'tp')
- new_proj_step: bfloat16 [2560, 80], P('fsdp', 'tp')
- new_proj_state: bfloat16 [2560, 256], P('fsdp', 'tp')
- new_conv_inner: bfloat16 [5, 5120], P(None, ('tp', 'fsdp'))
- new_conv_state: bfloat16 [5, 256], P(None, ('tp', 'fsdp'))
- new_head_params: float32 [3, 80], P(None, 'tp')
- new_mixer_gain: bfloat16 [5120], P(('tp', 'fsdp'))
- new_proj_output: bfloat16 [5120, 2560], P('tp', 'fsdp')
- new_first_input_gain: float32 [2560], P('fsdp')
- new_first_proj_inner: float32 [2560, 2, 5120], P('fsdp', None, 'tp')
- new_first_proj_step: float32 [2560, 80], P('fsdp', 'tp')
- new_first_proj_state: float32 [2560, 256], P('fsdp', 'tp')
- new_first_conv_inner: float32 [5, 5120], P(None, ('tp', 'fsdp'))
- new_first_conv_state: float32 [5, 256], P(None, ('tp', 'fsdp'))
- new_first_head_params: float32 [3, 80], P(None, 'tp')
- new_first_mixer_gain: float32 [5120], P(('tp', 'fsdp'))
- new_first_proj_output: float32 [5120, 2560], P('tp', 'fsdp')
- new_second_input_gain: float32 [2560], P('fsdp')
- new_second_proj_inner: float32 [2560, 2, 5120], P('fsdp', None, 'tp')
- new_second_proj_step: float32 [2560, 80], P('fsdp', 'tp')
- new_second_proj_state: float32 [2560, 256], P('fsdp', 'tp')
- new_second_conv_inner: float32 [5, 5120], P(None, ('tp', 'fsdp'))
- new_second_conv_state: float32 [5, 256], P(None, ('tp', 'fsdp'))
- new_second_head_params: float32 [3, 80], P(None, 'tp')
- new_second_mixer_gain: float32 [5120], P(('tp', 'fsdp'))
- new_second_proj_output: float32 [5120, 2560], P('tp', 'fsdp')
The draws below stay inside these ranges and needn't reach their ends.
Inputs may be any that keep to these rules, and one draw needn't show every extreme that they name: `segment_ids`: within each group the numbers never fall; each packed sequence has at most 1152 slots, and some has exactly 1152. `group_fill`: the live slots of a group are its leading slots; the counts sum to 7680, and the largest is exactly 1536. `head_params`: row 0 lies in [-7, -2.3], row 1 in [0, 2.8], row 2 in [0.25, 2].
All inputs are finite; a program needn't handle non-finite values.
Results may differ from the reference program's by a relative error of at most 0.0076.
The reference program's roundings to bfloat16 on the way count: a program that leaves them out, or rounds other values in their place, can miss the bound.
Values may be sent and summed in bfloat16 or wider, within the bound.
A program may use at most 576 MiB of HBM per device.

```python
import math
import jax
import jax.numpy as jnp
import numpy as np
from jax import lax

D = 2560
DI = 5120
H = 80
N = 128
K = 4
Q = 256
STEP = 3
GROUP_TOK = 1536
TOKENS = 12288
SEQ_MOST = 1152
SEGS = 4
FILL_TOTAL = 7680
N_FSDP = 8


def draw_head_params(key, part):
    first_key, second_key, third_key = jax.random.split(key, 3)
    bias_row = jax.random.uniform(first_key, (H,), jnp.float32, -6.5, -2.5)
    rate_row = jax.random.uniform(second_key, (H,), jnp.float32, 0.0, 2.7)
    skip_row = jax.random.uniform(third_key, (H,), jnp.float32, 0.5, 1.5)
    return jnp.stack([bias_row, rate_row, skip_row], axis=0)


def block_scale(rng, extent, cuts, low, high):
    def one(axis_at, parts):
        draws = jax.random.uniform(jax.random.fold_in(jax.random.fold_in(rng, 6), axis_at), (parts,), jnp.float32, low / len(cuts), high / len(cuts))
        return jnp.repeat(jnp.exp(draws), extent[axis_at] // parts).reshape((-1,) + (1,) * (len(extent) - axis_at - 1))

    level = one(*cuts[0])
    for cut in cuts[1:]:
        level = level * one(*cut)
    return level


def length_profile(amount, total, most, skew):
    loads = [(1 << 20) // math.isqrt(rank ** skew) + 1 for rank in range(2, amount + 1)]
    surplus, holding = total - most - (amount - 1), [1] * (amount - 1)
    while surplus > 0:
        candidates = [i for i in range(amount - 1) if holding[i] < most]
        whole, budget = sum([loads[i] for i in candidates]), surplus
        for i in candidates:
            more = min(most - holding[i], max(1, budget * loads[i] // whole), surplus)
            holding[i] = holding[i] + more
            surplus = surplus - more
    return np.array([most] + holding)


def ragged_sizes(rng, count, total, bound, lean):
    if count == 2:
        one = jax.random.randint(rng, (), max(1, total - bound), min(bound, total - 1) + 1)
        return jnp.stack([one, total - one])
    lengths = jnp.asarray(length_profile(count, total, bound, lean), jnp.int32)
    pairs = (count - 1) // 2
    giver, taker = lengths[1:1 + 2 * pairs:2], lengths[2:2 + 2 * pairs:2]
    slack = jnp.minimum(giver - 1, bound - taker)
    moved = jax.random.randint(jax.random.fold_in(rng, 1), (pairs,), 0, 1 << 20) % (slack + 1)
    lengths = lengths.at[1:1 + 2 * pairs:2].set(giver - moved).at[2:2 + 2 * pairs:2].set(taker + moved)
    return lengths[jax.random.permutation(jax.random.fold_in(rng, 2), count)]


def noise(key, shape, width, limit, cuts=(), kind=jnp.bfloat16):
    entries = jax.random.normal(key, shape, jnp.float32) * width
    if len(cuts) > 0:
        entries = block_scale(key, shape, cuts, -0.22, 0.18) * entries
    return jnp.clip(entries, min=-limit, max=limit).astype(kind)


def setup_inputs(seed: int = 0) -> dict:
    seeds = jax.random.split(jax.random.key(seed), 32)
    block_in = noise(seeds[0], (TOKENS, D), 1.0, 6.0, ((0, 32),))
    cotangent = noise(seeds[1], (TOKENS, D), 1.0, 6.0, ((0, 32),))
    segment_ids = jax.vmap(lambda own: jnp.searchsorted(jnp.cumsum(ragged_sizes(own, SEGS, GROUP_TOK, SEQ_MOST, 2)), jnp.arange(GROUP_TOK), side="right"))(jax.random.split(seeds[2], N_FSDP)).reshape((N_FSDP, GROUP_TOK)).astype(jnp.int32)
    group_fill = ragged_sizes(seeds[3], N_FSDP, FILL_TOTAL, GROUP_TOK, 2).astype(jnp.int32)
    input_gain = jnp.clip(1.0 + 0.1 * jax.random.normal(seeds[4], (D,), jnp.float32), 0.5, 1.5).astype(jnp.bfloat16)
    proj_inner = noise(seeds[5], (D, 2, DI), D ** -0.5, 0.125, ((0, 8), (2, 4)))
    proj_step = noise(seeds[6], (D, H), D ** -0.5, 0.125, ((0, 8), (1, 4)))
    proj_state = noise(seeds[7], (D, 2 * N), D ** -0.5, 0.125, ((0, 8), (1, 4)))
    conv_inner = jnp.clip(jax.random.uniform(seeds[8], (K + 1, DI), jnp.float32, -0.5, 0.5) * block_scale(seeds[8], (K + 1, DI), ((1, 32),), -0.4, 0.0), -0.5, 0.5).astype(jnp.bfloat16)
    conv_state = jnp.clip(jax.random.uniform(seeds[9], (K + 1, 2 * N), jnp.float32, -0.5, 0.5) * block_scale(seeds[9], (K + 1, 2 * N), ((1, 32),), -0.4, 0.0), -0.5, 0.5).astype(jnp.bfloat16)
    head_params = draw_head_params(jax.random.fold_in(seeds[31], 71), 0)
    mixer_gain = jnp.clip(1.0 + 0.1 * jax.random.normal(seeds[11], (DI,), jnp.float32), 0.5, 1.5).astype(jnp.bfloat16)
    proj_output = noise(seeds[12], (DI, D), DI ** -0.5, 0.078125, ((0, 4), (1, 8)))
    first_input_gain = noise(seeds[13], (D,), (0.05 * TOKENS ** 0.5), 32.0, ((0, 8),), jnp.float32)
    first_proj_inner = noise(seeds[14], (D, 2, DI), (0.05 * TOKENS ** 0.5), 32.0, ((0, 8), (2, 4)), jnp.float32)
    first_proj_step = noise(seeds[15], (D, H), (0.05 * TOKENS ** 0.5), 32.0, ((0, 8), (1, 4)), jnp.float32)
    first_proj_state = noise(seeds[16], (D, 2 * N), (0.05 * TOKENS ** 0.5), 32.0, ((0, 8), (1, 4)), jnp.float32)
    first_conv_inner = noise(seeds[17], (K + 1, DI), (0.05 * TOKENS ** 0.5), 32.0, ((1, 32),), jnp.float32)
    first_conv_state = noise(seeds[18], (K + 1, 2 * N), (0.05 * TOKENS ** 0.5), 32.0, ((1, 32),), jnp.float32)
    first_head_params = noise(seeds[19], (3, H), (0.05 * TOKENS ** 0.5), 32.0, ((1, 4),), jnp.float32)
    first_mixer_gain = noise(seeds[20], (DI,), (0.05 * TOKENS ** 0.5), 32.0, ((0, 32),), jnp.float32)
    first_proj_output = noise(seeds[21], (DI, D), (0.05 * TOKENS ** 0.5), 32.0, ((0, 4), (1, 8)), jnp.float32)
    second_input_gain = jnp.clip(jnp.exp(math.log(122.88) - 1.3862944 * jax.random.uniform(seeds[22], (D,), jnp.float32) ** block_scale(seeds[22], (D,), ((0, 8),), -0.2, 0.2)), 30.72, 122.88)
    second_proj_inner = jnp.clip(jnp.exp(math.log(122.88) - 1.3862944 * jax.random.uniform(seeds[23], (D, 2, DI), jnp.float32) ** block_scale(seeds[23], (D, 2, DI), ((0, 8), (2, 4)), -0.2, 0.2)), 30.72, 122.88)
    second_proj_step = jnp.clip(jnp.exp(math.log(122.88) - 1.3862944 * jax.random.uniform(seeds[24], (D, H), jnp.float32) ** block_scale(seeds[24], (D, H), ((0, 8), (1, 4)), -0.2, 0.2)), 30.72, 122.88)
    second_proj_state = jnp.clip(jnp.exp(math.log(122.88) - 1.3862944 * jax.random.uniform(seeds[25], (D, 2 * N), jnp.float32) ** block_scale(seeds[25], (D, 2 * N), ((0, 8), (1, 4)), -0.2, 0.2)), 30.72, 122.88)
    second_conv_inner = jnp.clip(jnp.exp(math.log(122.88) - 1.3862944 * jax.random.uniform(seeds[26], (K + 1, DI), jnp.float32) ** block_scale(seeds[26], (K + 1, DI), ((1, 32),), -0.2, 0.2)), 30.72, 122.88)
    second_conv_state = jnp.clip(jnp.exp(math.log(122.88) - 1.3862944 * jax.random.uniform(seeds[27], (K + 1, 2 * N), jnp.float32) ** block_scale(seeds[27], (K + 1, 2 * N), ((1, 32),), -0.2, 0.2)), 30.72, 122.88)
    second_head_params = jnp.clip(jnp.exp(math.log(122.88) - 1.3862944 * jax.random.uniform(seeds[28], (3, H), jnp.float32) ** block_scale(seeds[28], (3, H), ((1, 4),), -0.2, 0.2)), 30.72, 122.88)
    second_mixer_gain = jnp.clip(jnp.exp(math.log(122.88) - 1.3862944 * jax.random.uniform(seeds[29], (DI,), jnp.float32) ** block_scale(seeds[29], (DI,), ((0, 32),), -0.2, 0.2)), 30.72, 122.88)
    second_proj_output = jnp.clip(jnp.exp(math.log(122.88) - 1.3862944 * jax.random.uniform(seeds[30], (DI, D), jnp.float32) ** block_scale(seeds[30], (DI, D), ((0, 4), (1, 8)), -0.2, 0.2)), 30.72, 122.88)
    return {"block_in": block_in, "cotangent": cotangent, "segment_ids": segment_ids, "group_fill": group_fill, "input_gain": input_gain, "proj_inner": proj_inner, "proj_step": proj_step, "proj_state": proj_state, "conv_inner": conv_inner, "conv_state": conv_state, "head_params": head_params, "mixer_gain": mixer_gain, "proj_output": proj_output, "first_input_gain": first_input_gain, "first_proj_inner": first_proj_inner, "first_proj_step": first_proj_step, "first_proj_state": first_proj_state, "first_conv_inner": first_conv_inner, "first_conv_state": first_conv_state, "first_head_params": first_head_params, "first_mixer_gain": first_mixer_gain, "first_proj_output": first_proj_output, "second_input_gain": second_input_gain, "second_proj_inner": second_proj_inner, "second_proj_step": second_proj_step, "second_proj_state": second_proj_state, "second_conv_inner": second_conv_inner, "second_conv_state": second_conv_state, "second_head_params": second_head_params, "second_mixer_gain": second_mixer_gain, "second_proj_output": second_proj_output}


NORM_EPS = 1e-05
BETA_ONE = 0.9
BETA_TWO = 0.95
LEARN_RATE = 0.004
LEARN_SMALL = 0.15
WEIGHT_DECAY = 0.1
ADAM_EPS = 1e-08
PRECISE = lax.Precision.HIGHEST

def silu_act(values):
    return values * jax.nn.sigmoid(values)

def causal_conv(inputs, conv_taps, segment):
    tap_count = conv_taps.shape[0] - 1
    length = inputs.shape[0]
    summed = conv_taps[tap_count][None, :] + conv_taps[tap_count - 1][None, :] * inputs
    for offset in range(1, tap_count):
        shifted = jnp.concatenate([jnp.zeros_like(inputs[:offset]), inputs[:length - offset]], axis=0)
        earlier = jnp.concatenate([jnp.full((offset,), -1, jnp.int32), segment[:length - offset]], axis=0)
        same_doc = (earlier == segment)[:, None]
        summed = summed + conv_taps[tap_count - 1 - offset][None, :] * jnp.where(same_doc, shifted, 0.0)
    return summed

def ssd_block(carry_state, previous, inner_vals, step_sizes, b_rows, c_rows, labels, decay_rates, skip_weights):
    block_len = inner_vals.shape[0]
    lower_mask = jnp.arange(block_len)[:, None] >= jnp.arange(block_len)[None, :]
    log_steps = step_sizes * decay_rates[None, :]
    cumulative = jnp.cumsum(log_steps, axis=0)
    keep_mask = (lower_mask & (labels[:, None] == labels[None, :]))[:, :, None]
    spread = cumulative[:, None, :] - cumulative[None, :, :]
    decays = jnp.where(keep_mask, jnp.exp(jnp.where(keep_mask, spread, 0.0)), 0.0)
    scores = jnp.dot(c_rows, b_rows.T, precision=PRECISE)
    mixing = decays * scores[:, :, None] * step_sizes[None, :, :]
    inside = jnp.einsum('ijh,jhp->ihp', mixing, inner_vals, precision=PRECISE)
    carried = jnp.where((labels == previous)[:, None], jnp.exp(cumulative), 0.0)
    from_state = jnp.einsum('in,hnp->ihp', c_rows, carry_state, precision=PRECISE) * carried[:, :, None]
    output = inside + from_state + skip_weights[None, :, None] * inner_vals
    final_label = labels[block_len - 1]
    tail_weights = jnp.where((labels == final_label)[:, None], jnp.exp(cumulative[block_len - 1][None, :] - cumulative), 0.0) * step_sizes
    kept_share = jnp.where(previous == final_label, jnp.exp(cumulative[block_len - 1]), 0.0)
    new_state = jnp.einsum('jn,jh,jhp->hnp', b_rows, tail_weights, inner_vals, precision=PRECISE) + carry_state * kept_share[:, None, None]
    return (new_state, output)

def ssd_scan(inner_vals, step_sizes, decay_rates, b_rows, c_rows, segment, skip_weights, filled, skip_empty):
    row_count, head_count, head_width = inner_vals.shape
    blocks = row_count // Q
    state_width = b_rows.shape[1]
    stacked = (inner_vals.reshape(blocks, Q, head_count, head_width), step_sizes.reshape(blocks, Q, head_count), b_rows.reshape(blocks, Q, state_width), c_rows.reshape(blocks, Q, state_width), segment.reshape(blocks, Q), jnp.arange(blocks, dtype=jnp.int32) * Q)

    def advance(carried_in, pieces):
        carry_state, previous = carried_in
        block_vals, block_steps, block_b, block_c, block_labels, block_start = pieces

        def compute():
            return ssd_block(carry_state, previous, block_vals, block_steps, block_b, block_c, block_labels, decay_rates, skip_weights)

        def empty_block():
            return (carry_state, jnp.zeros_like(block_vals))
        if skip_empty:
            new_state, output = lax.cond(block_start < filled, compute, empty_block)
        else:
            new_state, output = compute()
        return ((new_state, block_labels[Q - 1]), output)
    start_state = jnp.zeros((head_count, state_width, head_width), inner_vals.dtype)
    final_carry, outputs = lax.scan(advance, (start_state, jnp.int32(-1)), stacked)
    return outputs.reshape(row_count, head_count, head_width)

def mixer_core(x_raw, dt_raw, b_rows, c_rows, conv_taps, head_params, segment, filled, skip_empty):
    head_count = head_params.shape[1]
    activated = silu_act(causal_conv(x_raw, conv_taps, segment))
    step_sizes = jax.nn.softplus(dt_raw + head_params[0][None, :])
    decay_rates = -jnp.exp(head_params[1])
    shaped = activated.reshape(activated.shape[0], head_count, -1)
    output = ssd_scan(shaped, step_sizes, decay_rates, b_rows, c_rows, segment, head_params[2], filled, skip_empty)
    return output.reshape(activated.shape[0], -1)

def state_act(raw_rows, conv_taps, segment):
    return silu_act(causal_conv(raw_rows, conv_taps, segment))

def contract_rows(left_mat, right_mat):
    return lax.dot_general(left_mat, right_mat, (((0,), (0,)), ((), ())), preferred_element_type=jnp.float32)

def contract_cols(left_mat, right_mat):
    return lax.dot_general(left_mat, right_mat, (((1,), (1,)), ((), ())), preferred_element_type=jnp.float32)

def adamw_step(weight, gradient, first_moment, second_moment, decay_factor, learn_rate):
    new_first = BETA_ONE * first_moment + (1.0 - BETA_ONE) * gradient
    new_second = BETA_TWO * second_moment + (1.0 - BETA_TWO) * gradient * gradient
    first_hat = new_first / (1.0 - BETA_ONE ** STEP)
    second_hat = new_second / (1.0 - BETA_TWO ** STEP)
    weight_f = weight.astype(jnp.float32)
    updated = weight_f - learn_rate * (first_hat / (jnp.sqrt(second_hat) + ADAM_EPS) + decay_factor * weight_f)
    return (updated.astype(weight.dtype), new_first, new_second)

def group_pass(block_rows, cot_rows, segment, filled, input_gain, proj_inner, proj_step, proj_state, conv_inner, conv_state, head_params, mixer_gain, proj_output):
    row_count = block_rows.shape[0]
    live_rows = (jnp.arange(row_count, dtype=jnp.int32) < filled)[:, None]
    block_f = block_rows.astype(jnp.float32)
    inv_rms = lax.rsqrt(lax.optimization_barrier(jnp.mean(block_f * block_f, axis=1, keepdims=True)) + NORM_EPS)
    unit_rows = block_f * inv_rms
    gain_f = input_gain.astype(jnp.float32)
    normed = (unit_rows * gain_f[None, :]).astype(jnp.bfloat16)
    gate_proj = proj_inner[:, 0, :]
    inner_proj = proj_inner[:, 1, :]
    z_raw = jnp.dot(normed, gate_proj, preferred_element_type=jnp.float32)
    x_raw = jnp.dot(normed, inner_proj, preferred_element_type=jnp.float32)
    dt_raw = jnp.dot(normed, proj_step, preferred_element_type=jnp.float32)
    state_raw = jnp.dot(normed, proj_state, preferred_element_type=jnp.float32)
    state_vals, state_back = jax.vjp(lambda raw_rows, conv_taps: state_act(raw_rows, conv_taps, segment), state_raw, conv_state.astype(jnp.float32))
    state_b = lax.optimization_barrier(state_vals.astype(jnp.bfloat16))
    state_f = state_b.astype(jnp.float32)
    b_rows = state_f[:, :N]
    c_rows = state_f[:, N:]
    mixed_inner, core_back = jax.vjp(lambda x_in_raw, dt_in_raw, b_in, c_in, conv_taps, head_in: mixer_core(x_in_raw, dt_in_raw, b_in, c_in, conv_taps, head_in, segment, filled, False), x_raw, dt_raw, b_rows, c_rows, conv_inner.astype(jnp.float32), head_params)
    gate_act = silu_act(z_raw)
    gated_rows = mixed_inner * gate_act
    inv_gate = lax.rsqrt(lax.optimization_barrier(jnp.mean(gated_rows * gated_rows, axis=1, keepdims=True)) + NORM_EPS)
    unit_gated = gated_rows * inv_gate
    mixer_f = mixer_gain.astype(jnp.float32)
    normed_gated = (unit_gated * mixer_f[None, :]).astype(jnp.bfloat16)
    mixed_rows = jnp.dot(normed_gated, proj_output, preferred_element_type=jnp.float32)
    block_out = (block_f + jnp.where(live_rows, mixed_rows, 0.0)).astype(jnp.bfloat16)
    cot_f = cot_rows.astype(jnp.float32)
    own_grad = jnp.where(live_rows, cot_f, 0.0).astype(jnp.bfloat16)
    grad_output = contract_rows(normed_gated, own_grad)
    d_normed_gated = contract_cols(own_grad, proj_output)
    grad_mixer = lax.optimization_barrier(jnp.sum(d_normed_gated * unit_gated, axis=0))
    d_unit = d_normed_gated * mixer_f[None, :]
    inner_mean = lax.optimization_barrier(jnp.mean(d_unit * unit_gated, axis=1, keepdims=True))
    d_gated = inv_gate * (d_unit - unit_gated * inner_mean)
    d_mixed_inner = d_gated * gate_act
    sigmoid_z = jax.nn.sigmoid(z_raw)
    d_z = d_gated * mixed_inner * sigmoid_z * (1.0 + z_raw * (1.0 - sigmoid_z))
    d_x, d_dt, d_b, d_c, grad_conv_inner, grad_head = core_back(d_mixed_inner)
    d_state_raw, grad_conv_state = state_back(jnp.concatenate([d_b, d_c], axis=1))
    d_z_b = d_z.astype(jnp.bfloat16)
    d_x_b = d_x.astype(jnp.bfloat16)
    d_step = d_dt.astype(jnp.bfloat16)
    d_state_b = d_state_raw.astype(jnp.bfloat16)
    grad_inner = jnp.stack([contract_rows(normed, d_z_b), contract_rows(normed, d_x_b)], axis=1)
    grad_step = contract_rows(normed, d_step)
    grad_state = contract_rows(normed, d_state_b)
    d_normed = contract_cols(d_z_b, gate_proj) + contract_cols(d_x_b, inner_proj) + contract_cols(d_step, proj_step) + contract_cols(d_state_b, proj_state)
    grad_gain = lax.optimization_barrier(jnp.sum(d_normed * unit_rows, axis=0))
    scaled = d_normed * gain_f[None, :]
    d_block = inv_rms * (scaled - unit_rows * lax.optimization_barrier(jnp.mean(scaled * unit_rows, axis=1, keepdims=True)))
    d_input = (cot_f + d_block).astype(jnp.bfloat16)
    grads = (grad_gain, grad_inner, grad_step, grad_state, grad_conv_inner, grad_conv_state, grad_head, grad_mixer, grad_output)
    return (block_out, d_input, grads)

def reference(block_in, cotangent, segment_ids, group_fill, input_gain, proj_inner, proj_step, proj_state, conv_inner, conv_state, head_params, mixer_gain, proj_output, first_input_gain, first_proj_inner, first_proj_step, first_proj_state, first_conv_inner, first_conv_state, first_head_params, first_mixer_gain, first_proj_output, second_input_gain, second_proj_inner, second_proj_step, second_proj_state, second_conv_inner, second_conv_state, second_head_params, second_mixer_gain, second_proj_output):
    groups = segment_ids.shape[0]
    group_len = segment_ids.shape[1]
    model_width = block_in.shape[1]
    weights = (input_gain, proj_inner, proj_step, proj_state, conv_inner, conv_state, head_params, mixer_gain, proj_output)
    start_grads = tuple((jnp.zeros(weight.shape, jnp.float32) for weight in weights))

    def advance(summed, pieces):
        block_rows, cot_rows, segment, filled = pieces
        block_out, d_input, grads = group_pass(block_rows, cot_rows, segment, filled, *weights)
        return (tuple((total_grad + new_grad for total_grad, new_grad in zip(summed, grads))), (block_out, d_input))
    grads, (blocks_out, blocks_din) = lax.scan(advance, start_grads, (block_in.reshape(groups, group_len, model_width), cotangent.reshape(groups, group_len, model_width), segment_ids, group_fill))
    block_out = blocks_out.reshape(-1, model_width)
    d_input = blocks_din.reshape(-1, model_width)
    decays = (0.0, WEIGHT_DECAY, WEIGHT_DECAY, WEIGHT_DECAY, 0.0, 0.0, 0.0, 0.0, WEIGHT_DECAY)
    rates = (LEARN_SMALL, LEARN_RATE, LEARN_RATE, LEARN_RATE, LEARN_SMALL, LEARN_SMALL, LEARN_SMALL, LEARN_SMALL, LEARN_RATE)
    firsts = (first_input_gain, first_proj_inner, first_proj_step, first_proj_state, first_conv_inner, first_conv_state, first_head_params, first_mixer_gain, first_proj_output)
    seconds = (second_input_gain, second_proj_inner, second_proj_step, second_proj_state, second_conv_inner, second_conv_state, second_head_params, second_mixer_gain, second_proj_output)
    updated = [adamw_step(weights[index], grads[index], firsts[index], seconds[index], decays[index], rates[index]) for index in range(9)]
    return (block_out, d_input, grads[0], grads[1], grads[2], grads[3], grads[4], grads[5], grads[6], grads[7], grads[8], updated[0][0], updated[1][0], updated[2][0], updated[3][0], updated[4][0], updated[5][0], updated[6][0], updated[7][0], updated[8][0], updated[0][1], updated[1][1], updated[2][1], updated[3][1], updated[4][1], updated[5][1], updated[6][1], updated[7][1], updated[8][1], updated[0][2], updated[1][2], updated[2][2], updated[3][2], updated[4][2], updated[5][2], updated[6][2], updated[7][2], updated[8][2])
```

```python
import functools
import jax
import jax.numpy as jnp
from jax import lax
from jax.experimental import pallas as pl
from jax.experimental.layout import Layout, with_layout_constraint
from jax.experimental.pallas import tpu as pltpu
from jax.sharding import PartitionSpec as P

N = 128
Q = 256
LANE = 128
BLK = 128
NEG = -1e30
F32 = jnp.float32
BF16 = jnp.bfloat16
VMEM_CAP = 56 << 20


def mm(left, right):
    return lax.dot_general(left, right, (((1,), (0,)), ((), ())), preferred_element_type=F32)


def mm_nt(left, right):
    return lax.dot_general(left, right, (((1,), (1,)), ((), ())), preferred_element_type=F32)


def mm_exact(left, right):
    return lax.dot_general(
        left,
        right,
        (((1,), (0,)), ((), ())),
        precision=lax.Precision.HIGHEST,
        preferred_element_type=F32,
    )


def split_two(value):
    high = value.astype(BF16)
    low = (value - high.astype(F32)).astype(BF16)
    return high, low


def spread_heads(value, expand):
    high = value.astype(BF16).astype(F32)
    rest = value - high
    mid = rest.astype(BF16).astype(F32)
    low = rest - mid
    packed = high + pltpu.roll(mid, 32, 1) + pltpu.roll(low, 64, 1)
    return mm(packed.astype(BF16), expand)


def iota2(shape, axis):
    return lax.broadcasted_iota(jnp.int32, shape, axis)


def step_terms(small_ref, meta_ref, hp_ref):
    lane_on = hp_ref[2:3, :]
    pre = small_ref[...] + hp_ref[0:1, :]
    pre = pre * lane_on
    steps = (jnp.maximum(pre, 0.0) + jnp.log1p(jnp.exp(-jnp.abs(pre)))) * lane_on
    logs = steps * hp_ref[1:2, :]
    size = logs.shape[0]
    lower = (iota2((size, size), 0) >= iota2((size, size), 1)).astype(F32)
    cum = mm_exact(lower, logs)
    last = cum[size - 1 : size, :]
    into = jnp.exp(cum) * meta_ref[:, 4:5] * lane_on
    tail = jnp.exp(last - cum) * meta_ref[:, 5:6] * lane_on
    keep = jnp.exp(last) * meta_ref[size - 1 : size, 4:5] * lane_on
    return pre, steps, cum, into, tail, keep


def ssd_fwd_kernel(
    heads,
    raw_ref,
    small_ref,
    bc_raw_ref,
    meta_ref,
    metar_ref,
    taps_ref,
    taps_bc_ref,
    hp_ref,
    skip_ref,
    expand_ref,
    y_ref,
    st_ref,
    bc_ref,
    state,
    tail_rows,
    tail_bc,
    window,
    col_cum,
    row_cum,
    bias,
    scores,
    step_x,
    into_x,
    tail_x,
    keep_x,
    masks,
    b_turned,
):
    chunk = pl.program_id(0)

    @pl.when(chunk == 0)
    def _():
        state[...] = jnp.zeros_like(state)
        tail_rows[...] = jnp.zeros_like(tail_rows)
        tail_bc[...] = jnp.zeros_like(tail_bc)

    st_ref[0] = state[...]
    _, steps, cum, into, tail, keep = step_terms(small_ref, meta_ref, hp_ref)
    row_cum[...] = cum.T
    for head in range(heads):
        col_cum[:, head * LANE : (head + 1) * LANE] = jnp.broadcast_to(
            cum[:, head : head + 1], (Q, LANE)
        )
    expand = expand_ref[...]
    step_x[...] = spread_heads(steps, expand)
    into_x[...] = spread_heads(into, expand)
    tail_x[...] = spread_heads(tail, expand)
    keep_x[...] = spread_heads(jnp.broadcast_to(keep, (8, LANE)), expand)
    for offset in range(1, 4):
        masks[offset - 1] = jnp.broadcast_to(meta_ref[:, offset : offset + 1], (Q, LANE))
    same = (meta_ref[:, 0:1] == metar_ref[0, 0:1, :]) & (
        iota2((Q, Q), 0) >= iota2((Q, Q), 1)
    )
    bias[...] = jnp.where(same, 0.0, NEG)
    for at in range(0, 2 * N, LANE):
        lanes = slice(at, at + LANE)
        window[0:8, :] = tail_bc[:, lanes]
        current = bc_raw_ref[:, lanes]
        window[8 : 8 + Q, :] = current
        conv = taps_bc_ref[4:5, lanes] + taps_bc_ref[3:4, lanes] * current
        for offset in range(1, 4):
            conv = conv + taps_bc_ref[3 - offset : 4 - offset, lanes] * (
                masks[offset - 1] * window[8 - offset : 8 - offset + Q, :]
            )
        bc_ref[:, lanes] = (conv * jax.nn.sigmoid(conv)).astype(BF16)
    tail_bc[...] = bc_raw_ref[Q - 8 : Q, :]
    b_rows = bc_ref[:, :N]
    c_rows = bc_ref[:, N:]
    scores[...] = mm_nt(c_rows, b_rows)
    b_turned[...] = b_rows.astype(F32).T.astype(BF16)
    first = iota2((Q, LANE), 1) < LANE // 2

    def pair(index, _):
        lanes = pl.ds(pl.multiple_of(index * LANE, LANE), LANE)
        window[0:8, :] = tail_rows[:, lanes]
        current = raw_ref[:, lanes]
        window[8 : 8 + Q, :] = current
        conv = taps_ref[4:5, lanes] + taps_ref[3:4, lanes] * current
        for offset in range(1, 4):
            conv = conv + taps_ref[3 - offset : 4 - offset, lanes] * (
                masks[offset - 1] * window[8 - offset : 8 - offset + Q, :]
            )
        vals = conv * jax.nn.sigmoid(conv)
        scaled = (vals * step_x[:, lanes]).astype(BF16)
        zero = jnp.zeros_like(scaled)
        own = (jnp.where(first, scaled, zero), jnp.where(first, zero, scaled))
        held = state[:, lanes]
        base = into_x[:, lanes] * mm(c_rows, held.astype(BF16)) + skip_ref[0:1, lanes] * vals
        for low in range(0, Q, BLK):
            width = low + BLK
            total = base[low:width, :]
            for which in range(2):
                head = index * 2 + which
                across = row_cum[pl.ds(head, 1), :][:, :width]
                down = col_cum[low:width, pl.ds(pl.multiple_of(head * LANE, LANE), LANE)]
                down = jnp.concatenate([down] * (width // LANE), axis=1)
                decays = jnp.exp(down - across + bias[low:width, :width])
                mixing = (decays * scores[low:width, :width]).astype(BF16)
                total = total + mm(mixing, own[which][:width, :])
            y_ref[low:width, lanes] = total
        weighted = (tail_x[:, lanes] * scaled.astype(F32)).astype(BF16)
        state[:, lanes] = held * keep_x[0:1, lanes] + mm(b_turned[...], weighted)
        return 0

    lax.fori_loop(0, heads // 2, pair, 0)
    tail_rows[...] = raw_ref[Q - 8 : Q, :]


def ssd_bwd_kernel(
    heads,
    raw_ref,
    halo_ref,
    small_ref,
    bc_ref,
    meta_ref,
    meta_next_ref,
    metar_ref,
    taps_ref,
    hp_ref,
    skip_ref,
    expand_ref,
    gather_ref,
    y_ref,
    dy_ref,
    st_ref,
    dx_ref,
    ddt_ref,
    dbc_ref,
    dtaps_ref,
    dhp_ref,
    dskip_ref,
    small_turned_ref,
    dstate,
    next_rows,
    carried,
    window,
    dwindow,
    col_cum,
    row_cum,
    bias,
    scores,
    dscores,
    step_x,
    into_x,
    tail_x,
    keep_x,
    masks,
    c_turned,
    sums,
    dbc,
):
    chunk = pl.program_id(0)

    @pl.when(chunk == 0)
    def _():
        dstate[...] = jnp.zeros_like(dstate)
        next_rows[...] = jnp.zeros_like(next_rows)
        carried[...] = jnp.zeros_like(carried)
        dtaps_ref[...] = jnp.zeros_like(dtaps_ref)
        dhp_ref[...] = jnp.zeros_like(dhp_ref)
        dskip_ref[...] = jnp.zeros_like(dskip_ref)

    small_turned_ref[...] = small_ref[...].T
    pre, steps, cum, into, tail, keep = step_terms(small_ref, meta_ref, hp_ref)
    row_cum[...] = cum.T
    for head in range(heads):
        col_cum[:, head * LANE : (head + 1) * LANE] = jnp.broadcast_to(
            cum[:, head : head + 1], (Q, LANE)
        )
    expand = expand_ref[...]
    step_x[...] = spread_heads(steps, expand)
    into_x[...] = spread_heads(into, expand)
    tail_x[...] = spread_heads(tail, expand)
    keep_x[...] = spread_heads(jnp.broadcast_to(keep, (8, LANE)), expand)
    for offset in range(1, 4):
        masks[offset - 1, :Q] = jnp.broadcast_to(meta_ref[:, offset : offset + 1], (Q, LANE))
        masks[offset - 1, Q:] = jnp.broadcast_to(meta_next_ref[:, offset : offset + 1], (8, LANE))
    same = (meta_ref[:, 0:1] == metar_ref[0, 0:1, :]) & (
        iota2((Q, Q), 0) <= iota2((Q, Q), 1)
    )
    bias[...] = jnp.where(same, 0.0, NEG)
    b_rows = bc_ref[:, :N]
    c_rows = bc_ref[:, N:]
    scores[...] = mm_nt(b_rows, c_rows)
    dscores[...] = jnp.zeros_like(dscores)
    c_turned[...] = c_rows.astype(F32).T.astype(BF16)
    sums[...] = jnp.zeros_like(sums)
    dbc[...] = jnp.zeros_like(dbc)
    carry_high, carry_low = split_two(carried[...])
    gather_all = gather_ref[...]
    from_next = mm(carry_high, gather_all) + mm(carry_low, gather_all)
    first = iota2((Q, LANE), 1) < LANE // 2

    def pair(index, _):
        lanes = pl.ds(pl.multiple_of(index * LANE, LANE), LANE)
        window[0:8, :] = halo_ref[:, lanes]
        current = raw_ref[:, lanes]
        window[8 : 8 + Q, :] = current
        conv = taps_ref[4:5, lanes] + taps_ref[3:4, lanes] * current
        for offset in range(1, 4):
            conv = conv + taps_ref[3 - offset : 4 - offset, lanes] * (
                masks[offset - 1, :Q] * window[8 - offset : 8 - offset + Q, :]
            )
        gate = jax.nn.sigmoid(conv)
        vals = conv * gate
        step_here = step_x[:, lanes]
        scaled = (vals * step_here).astype(BF16)
        skip = skip_ref[0:1, lanes]
        dy = dy_ref[:, lanes]
        dy_half = dy.astype(BF16)
        zero = jnp.zeros_like(scaled)
        own = (jnp.where(first, scaled, zero), jnp.where(first, zero, scaled))
        own_dy = (jnp.where(first, dy_half, zero), jnp.where(first, zero, dy_half))
        dheld = dstate[:, lanes]
        dheld_half = dheld.astype(BF16)
        tail_here = tail_x[:, lanes]
        base = tail_here * mm(b_rows, dheld_half)
        pieces = []
        for low in range(0, Q, BLK):
            high = low + BLK
            total = base[low:high, :]
            for which in range(2):
                head = index * 2 + which
                across = row_cum[pl.ds(head, 1), :][:, low:]
                down = col_cum[low:high, pl.ds(pl.multiple_of(head * LANE, LANE), LANE)]
                down = jnp.concatenate([down] * ((Q - low) // LANE), axis=1)
                decays = jnp.exp(across - down + bias[low:high, low:])
                mixing = (decays * scores[low:high, low:]).astype(BF16)
                total = total + mm(mixing, own_dy[which][low:, :])
                dmix = mm_nt(own[which][low:high, :], dy_half[low:, :])
                dscores[low:high, low:] += dmix * decays
            pieces.append(total)
        dscaled = jnp.concatenate(pieces, axis=0)
        held = st_ref[0, :, lanes]
        edy = (into_x[:, lanes] * dy).astype(BF16)
        weighted = (tail_here * scaled.astype(F32)).astype(BF16)
        dbc[:, :N] += mm_nt(weighted, dheld_half)
        dbc[:, N:] += mm_nt(edy, held.astype(BF16))
        gather = gather_ref[lanes, :]
        balance = dy_half.astype(F32) * (y_ref[:, lanes] - skip * vals) - scaled.astype(
            F32
        ) * dscaled
        part_high, part_low = split_two(balance)
        sums[0] += mm(part_high, gather) + mm(part_low, gather)
        part_high, part_low = split_two(vals * dscaled)
        sums[1] += mm(part_high, gather) + mm(part_low, gather)
        dskip_ref[0:1, lanes] += jnp.sum(dy * vals, axis=0, keepdims=True)
        dheld_new = keep_x[0:1, lanes] * dheld + mm(c_turned[...], edy)
        dstate[:, lanes] = dheld_new
        carried[0:1, lanes] = jnp.sum(dheld_new * held, axis=0, keepdims=True)
        dvals = step_here * dscaled + skip * dy
        dconv = dvals * (gate * (1.0 + conv * (1.0 - gate)))
        dwindow[0:Q, :] = dconv
        dwindow[Q : Q + 8, :] = next_rows[:, lanes]
        next_rows[:, lanes] = dconv[0:8, :]
        dtaps_ref[4:5, lanes] += jnp.sum(dconv, axis=0, keepdims=True)
        dtaps_ref[3:4, lanes] += jnp.sum(dconv * current, axis=0, keepdims=True)
        draw = taps_ref[3:4, lanes] * dconv
        for offset in range(1, 4):
            shifted = masks[offset - 1, :Q] * window[8 - offset : 8 - offset + Q, :]
            dtaps_ref[3 - offset : 4 - offset, lanes] += jnp.sum(
                dconv * shifted, axis=0, keepdims=True
            )
            draw = draw + taps_ref[3 - offset : 4 - offset, lanes] * (
                masks[offset - 1, offset : offset + Q] * dwindow[offset : offset + Q, :]
            )
        dx_ref[:, lanes] = draw.astype(BF16)
        return 0

    lax.fori_loop(0, heads // 2, pair, 0)
    dscores_now = dscores[...]
    d_b = dbc[:, :N] + mm(dscores_now.astype(BF16), c_rows)
    d_c = dbc[:, N:] + mm(dscores_now.T.astype(BF16), b_rows)
    dbc_ref[:N, :] = d_b.T
    dbc_ref[N:, :] = d_c.T
    dcum = sums[0] + jnp.where(iota2((Q, LANE), 0) == Q - 1, from_next[0:1, :], 0.0)
    upper = (iota2((Q, Q), 0) <= iota2((Q, Q), 1)).astype(F32)
    dlogs = mm_exact(upper, dcum)
    dsteps = (dlogs * hp_ref[1:2, :] + sums[1]) * jax.nn.sigmoid(pre) * hp_ref[2:3, :]
    ddt_ref[...] = dsteps.T
    dhp_ref[0:1, :] += jnp.sum(dsteps, axis=0, keepdims=True)
    dhp_ref[1:2, :] += jnp.sum(dlogs * steps, axis=0, keepdims=True)


def head_tables(heads):
    width = heads * (LANE // 2)
    owner = jnp.arange(width) // (LANE // 2)
    slot = jnp.arange(LANE)
    expand = ((slot % 32)[:, None] == owner[None, :]) & (slot < 96)[:, None]
    gather = owner[:, None] == slot[None, :]
    return expand.astype(BF16), gather.astype(BF16)


def segment_tables(segment):
    length = segment.shape[0]
    chunks = length // Q
    columns = [segment.astype(F32)]
    for offset in range(1, 4):
        earlier = jnp.concatenate(
            [jnp.full((offset,), -1, jnp.int32), segment[: length - offset]], axis=0
        )
        columns.append((earlier == segment).astype(F32))
    by_chunk = segment.reshape(chunks, Q)
    last = by_chunk[:, Q - 1]
    before = jnp.concatenate([jnp.full((1,), -1, jnp.int32), last[: chunks - 1]], axis=0)
    columns.append((by_chunk == before[:, None]).astype(F32).reshape(length))
    columns.append((by_chunk == last[:, None]).astype(F32).reshape(length))
    meta = jnp.pad(jnp.stack(columns, axis=1), ((0, 0), (0, LANE - len(columns))))
    meta_rows = jnp.broadcast_to(by_chunk.astype(F32)[:, None, :], (chunks, 8, Q))
    return meta, meta_rows


def head_rows(head_params):
    heads = head_params.shape[1]
    rates = -jnp.exp(head_params[1])
    table = jnp.stack([head_params[0], rates, jnp.ones_like(rates)], axis=0)
    return jnp.pad(table, ((0, 5), (0, LANE - heads)))


def time_like(seconds):
    return pl.CostEstimate(
        flops=int(seconds * 1.1e15), bytes_accessed=int(seconds * 3.4e12), transcendentals=0
    )


def full_spec(shape):
    return pl.BlockSpec(shape, lambda c: (0,) * len(shape))


def ssd_forward(raw, bc_raw, meta, meta_rows, taps, taps_bc, hp, skip, expand, heads):
    length = raw.shape[0]
    width = heads * (LANE // 2)
    chunks = length // Q
    small_at = width // LANE
    return pl.pallas_call(
        functools.partial(ssd_fwd_kernel, heads),
        grid=(chunks,),
        out_shape=(
            jax.ShapeDtypeStruct((length, width), F32),
            jax.ShapeDtypeStruct((chunks, N, width), F32),
            jax.ShapeDtypeStruct((length, 2 * N), BF16),
        ),
        in_specs=[
            pl.BlockSpec((Q, width), lambda c: (c, 0)),
            pl.BlockSpec((Q, LANE), lambda c: (c, small_at)),
            pl.BlockSpec((Q, 2 * N), lambda c: (c, 0)),
            pl.BlockSpec((Q, LANE), lambda c: (c, 0)),
            pl.BlockSpec((1, 8, Q), lambda c: (c, 0, 0)),
            full_spec((8, width)),
            full_spec((8, 2 * N)),
            full_spec((8, LANE)),
            full_spec((8, width)),
            full_spec((LANE, width)),
        ],
        out_specs=(
            pl.BlockSpec((Q, width), lambda c: (c, 0)),
            pl.BlockSpec((1, N, width), lambda c: (c, 0, 0)),
            pl.BlockSpec((Q, 2 * N), lambda c: (c, 0)),
        ),
        scratch_shapes=[
            pltpu.VMEM((N, width), F32),
            pltpu.VMEM((8, width), F32),
            pltpu.VMEM((8, 2 * N), F32),
            pltpu.VMEM((Q + 8, LANE), F32),
            pltpu.VMEM((Q, heads * LANE), F32),
            pltpu.VMEM((LANE, Q), F32),
            pltpu.VMEM((Q, Q), F32),
            pltpu.VMEM((Q, Q), F32),
            pltpu.VMEM((Q, width), F32),
            pltpu.VMEM((Q, width), F32),
            pltpu.VMEM((Q, width), F32),
            pltpu.VMEM((8, width), F32),
            pltpu.VMEM((3, Q, LANE), F32),
            pltpu.VMEM((N, Q), BF16),
        ],
        compiler_params=pltpu.CompilerParams(vmem_limit_bytes=VMEM_CAP),
        cost_estimate=time_like(37e-6 * length * heads / 30720),
        name="ssd_fwd",
    )(raw, raw, bc_raw, meta, meta_rows, taps, taps_bc, hp, skip, expand)


def ssd_backward(raw, bc, meta, meta_rows, taps, hp, skip, expand, gather, y, dy, states, heads):
    length = raw.shape[0]
    width = heads * (LANE // 2)
    chunks = length // Q
    small_at = width // LANE
    per = Q // 8

    def at(c):
        return chunks - 1 - c

    return pl.pallas_call(
        functools.partial(ssd_bwd_kernel, heads),
        grid=(chunks,),
        out_shape=(
            jax.ShapeDtypeStruct((length, width), BF16),
            jax.ShapeDtypeStruct((LANE, length), F32),
            jax.ShapeDtypeStruct((2 * N, length), F32),
            jax.ShapeDtypeStruct((8, width), F32),
            jax.ShapeDtypeStruct((8, LANE), F32),
            jax.ShapeDtypeStruct((8, width), F32),
            jax.ShapeDtypeStruct((LANE, length), F32),
        ),
        in_specs=[
            pl.BlockSpec((Q, width), lambda c: (at(c), 0)),
            pl.BlockSpec((8, width), lambda c: (jnp.maximum(at(c) * per - 1, 0), 0)),
            pl.BlockSpec((Q, LANE), lambda c: (at(c), small_at)),
            pl.BlockSpec((Q, 2 * N), lambda c: (at(c), 0)),
            pl.BlockSpec((Q, LANE), lambda c: (at(c), 0)),
            pl.BlockSpec(
                (8, LANE), lambda c: (jnp.minimum((at(c) + 1) * per, chunks * per - 1), 0)
            ),
            pl.BlockSpec((1, 8, Q), lambda c: (at(c), 0, 0)),
            full_spec((8, width)),
            full_spec((8, LANE)),
            full_spec((8, width)),
            full_spec((LANE, width)),
            full_spec((width, LANE)),
            pl.BlockSpec((Q, width), lambda c: (at(c), 0)),
            pl.BlockSpec((Q, width), lambda c: (at(c), 0)),
            pl.BlockSpec((1, N, width), lambda c: (at(c), 0, 0)),
        ],
        out_specs=(
            pl.BlockSpec((Q, width), lambda c: (at(c), 0)),
            pl.BlockSpec((LANE, Q), lambda c: (0, at(c))),
            pl.BlockSpec((2 * N, Q), lambda c: (0, at(c))),
            full_spec((8, width)),
            full_spec((8, LANE)),
            full_spec((8, width)),
            pl.BlockSpec((LANE, Q), lambda c: (0, at(c))),
        ),
        scratch_shapes=[
            pltpu.VMEM((N, width), F32),
            pltpu.VMEM((8, width), F32),
            pltpu.VMEM((8, width), F32),
            pltpu.VMEM((Q + 8, LANE), F32),
            pltpu.VMEM((Q + 8, LANE), F32),
            pltpu.VMEM((Q, heads * LANE), F32),
            pltpu.VMEM((LANE, Q), F32),
            pltpu.VMEM((Q, Q), F32),
            pltpu.VMEM((Q, Q), F32),
            pltpu.VMEM((Q, Q), F32),
            pltpu.VMEM((Q, width), F32),
            pltpu.VMEM((Q, width), F32),
            pltpu.VMEM((Q, width), F32),
            pltpu.VMEM((8, width), F32),
            pltpu.VMEM((3, Q + 8, LANE), F32),
            pltpu.VMEM((N, Q), BF16),
            pltpu.VMEM((2, Q, LANE), F32),
            pltpu.VMEM((Q, 2 * N), F32),
        ],
        compiler_params=pltpu.CompilerParams(vmem_limit_bytes=VMEM_CAP),
        cost_estimate=time_like(69e-6 * length * heads / 30720),
        name="ssd_bwd",
    )(
        raw, raw, raw, bc, meta, meta, meta_rows, taps, hp, skip, expand, gather, y, dy, states
    )


def dn_kernel(step, dz_ref, dx_ref, side_ref, gate_ref, inner_ref, normed_ref, out_ref, sums_ref, turned):
    width = dz_ref.shape[1]

    @pl.when(pl.program_id(0) == 0)
    def _():
        turned[...] = side_ref[...].T.astype(BF16)

    gate = gate_ref[...]
    inner = inner_ref[:, :width]
    side = inner_ref[:, width:]
    sums_ref[...] = jnp.zeros_like(sums_ref)

    def rows(index, _):
        at = pl.ds(pl.multiple_of(index * step, step), step)
        total = mm_nt(dz_ref[at, :], gate) + mm_nt(dx_ref[at, :], inner)
        total = total + mm_nt(turned[at, :], side)
        out_ref[at, :] = total.astype(BF16)
        sums_ref[0:1, :] += jnp.sum(total * normed_ref[at, :].astype(F32), axis=0, keepdims=True)
        return 0

    lax.fori_loop(0, dz_ref.shape[0] // step, rows, 0)


def d_normed_half(d_z, d_x, d_side, gate_all, x_all, normed, which, step=768, tile=256):
    length, width = d_z.shape
    model = gate_all.shape[0]
    half = model // 2
    first = which * half // tile
    return pl.pallas_call(
        functools.partial(dn_kernel, step),
        grid=(half // tile,),
        out_shape=(
            jax.ShapeDtypeStruct((length, half), BF16),
            jax.ShapeDtypeStruct((8, half), F32),
        ),
        in_specs=[
            full_spec((length, width)),
            full_spec((length, width)),
            full_spec((LANE, length)),
            pl.BlockSpec((tile, width), lambda n: (n + first, 0)),
            pl.BlockSpec((tile, width + LANE), lambda n: (n + first, 0)),
            pl.BlockSpec((length, tile), lambda n: (0, n + first)),
        ],
        out_specs=(
            pl.BlockSpec((length, tile), lambda n: (0, n)),
            pl.BlockSpec((8, tile), lambda n: (0, n)),
        ),
        scratch_shapes=[pltpu.VMEM((length, LANE), BF16)],
        compiler_params=pltpu.CompilerParams(vmem_limit_bytes=VMEM_CAP),
        cost_estimate=time_like(12e-6),
        name="d_normed",
    )(d_z, d_x, d_side, gate_all, x_all, normed)

DI = 5120
STEP = 3
NORM_EPS = 1e-05
BETA_ONE = 0.9
BETA_TWO = 0.95
LEARN_RATE = 0.004
LEARN_SMALL = 0.15
WEIGHT_DECAY = 0.1
ADAM_EPS = 1e-08


def by_rows(value):
    return with_layout_constraint(value, Layout(major_to_minor=(0, 1)))


def silu_act(values):
    return values * jax.nn.sigmoid(values)


def later(row, offset):
    return jnp.pad(row, ((0, 0), (offset, 0)))[:, : row.shape[1]]


def state_act(raw_cols, conv_taps, doc_masks):
    conv = conv_taps[4][:, None] + conv_taps[3][:, None] * raw_cols
    for offset in range(1, 4):
        conv = conv + conv_taps[3 - offset][:, None] * (
            doc_masks[offset - 1][None, :] * later(raw_cols, offset)
        )
    return silu_act(conv)


def contract_rows(left_mat, right_mat):
    return lax.dot_general(
        left_mat, right_mat, (((0,), (0,)), ((), ())), preferred_element_type=F32
    )


def adamw_step(weight, gradient, first_moment, second_moment, decay_factor, learn_rate):
    new_first = BETA_ONE * first_moment + (1.0 - BETA_ONE) * gradient
    new_second = BETA_TWO * second_moment + (1.0 - BETA_TWO) * gradient * gradient
    first_hat = new_first / (1.0 - BETA_ONE**STEP)
    second_hat = new_second / (1.0 - BETA_TWO**STEP)
    weight_f = weight.astype(F32)
    updated = weight_f - learn_rate * (
        first_hat / (jnp.sqrt(second_hat) + ADAM_EPS) + decay_factor * weight_f
    )
    return (updated.astype(weight.dtype), new_first, new_second)


def swap(value, distance, size):
    return lax.ppermute(value, "tp", [(at, at ^ distance) for at in range(size)])


def tied(*values):
    return lax.optimization_barrier(values)


def gather_parts(value, size):
    if size != 4:
        return [value] + [swap(value, k, size) for k in range(1, size)]
    half = value.shape[0] // 2
    one, two = swap(value, 1, size), swap(value, 2, size)
    far = jnp.concatenate([swap(two[:half], 1, size), swap(one[half:], 2, size)], axis=0)
    return [value, one, two, far]


def scatter_start(left, right, rows, index, size):
    def block(value, distance):
        return lax.dynamic_slice_in_dim(value, (index ^ distance) * rows, rows, 0)

    sent, kept = [], []
    for half, near in ((left, 1), (right, 2)):
        if size == 4:
            pair = jnp.concatenate([block(half, 3), block(half, near)], axis=0)
            sent.append(swap(pair, near, size))
            kept.append((block(half, 3 - near), block(half, 0)))
        else:
            sent.append([swap(block(half, k), k, size) for k in range(1, size)])
            kept.append(block(half, 0))
    return sent, kept


def scatter_middle(sent, kept, rows, size):
    if size != 4:
        return sent, kept
    passed = [
        (kept[at][0].astype(F32) + sent[at][:rows].astype(F32)).astype(BF16) for at in range(2)
    ]
    own = [kept[at][1].astype(F32) + sent[at][rows:].astype(F32) for at in range(2)]
    return passed, own


def scatter_last(passed, size):
    if size != 4:
        return passed[0] + passed[1]
    return [swap(passed[0], 2, size), swap(passed[1], 1, size)]


def scatter_end(own, last):
    each = len(last) // 2
    totals = []
    for at in range(2):
        total = own[at].astype(F32)
        for piece in last[at * each : (at + 1) * each]:
            total = total + piece.astype(F32)
        totals.append(total)
    return jnp.concatenate(totals, axis=1)


def all_sum(value, size):
    distance = 1
    while distance < size:
        value = value + swap(value, distance, size)
        distance *= 2
    return value


def fsdp_swap(value, distance, size):
    return lax.ppermute(value, "fsdp", [(at, at ^ distance) for at in range(size)])


def gather_by_swaps(value, index, size):
    whole = jnp.zeros((size,) + value.shape, value.dtype)
    for distance in range(size):
        piece = value if distance == 0 else fsdp_swap(value, distance, size)
        whole = lax.dynamic_update_slice(
            whole, piece[None], (index ^ distance, jnp.int32(0), jnp.int32(0))
        )
    return whole


def pair_sum(value, index, size):
    blocks = value.reshape(size // 2, 2, value.shape[0] // size, value.shape[1])
    core = index % 2
    away = lax.dynamic_slice_in_dim(blocks, 1 - core, 1, 1)[:, 0]
    own = lax.dynamic_slice_in_dim(blocks, core, 1, 1)[:, 0]
    return (own.astype(F32) + fsdp_swap(away, 1, size).astype(F32)).astype(value.dtype)


def chip_scatter(value, size):
    groups = [list(range(core, size, 2)) for core in range(2)]
    flat = value.reshape(value.shape[0] * value.shape[1], value.shape[2])
    return lax.psum_scatter(
        flat, "fsdp", scatter_dimension=0, axis_index_groups=groups, tiled=True
    ).astype(F32)


def chip_sum(value, index, size):
    chip = index // 2

    def block(distance):
        return lax.dynamic_slice_in_dim(value, chip ^ distance, 1, 0)[0]

    total = block(0).astype(F32)
    for distance in range(1, size // 2):
        total = total + fsdp_swap(block(distance), 2 * distance, size).astype(F32)
    return total


def pad_cols(value, width):
    return jnp.pad(value, ((0, 0), (0, width - value.shape[1])))


def body(
    block_in,
    cotangent,
    segment_ids,
    group_fill,
    input_gain,
    proj_inner,
    proj_step,
    proj_state,
    conv_inner,
    conv_state,
    head_params,
    mixer_gain,
    proj_output,
    *moments,
):
    tp_size = lax.axis_size("tp")
    fsdp_size = lax.axis_size("fsdp")
    tp_index = lax.axis_index("tp")
    fsdp_index = lax.axis_index("fsdp")
    own_rows, model = block_in.shape
    group_rows = own_rows * tp_size
    shard, _, width = proj_inner.shape
    heads = proj_step.shape[1]
    state_cols = proj_state.shape[1]
    segment = segment_ids[0]
    filled = group_fill[0]

    small_values = jnp.concatenate(
        [conv_inner.reshape(-1), conv_state.reshape(-1), mixer_gain], axis=0
    )
    small_count = small_values.shape[0]
    inner_n, state_n = conv_inner.size, conv_state.size
    small_cols = -(-(small_count + 3 * heads) // shard)
    small_block = jnp.pad(small_values, (0, small_cols * shard - small_count)).reshape(
        shard, small_cols
    )
    used = heads + state_cols
    side = pad_cols(
        jnp.concatenate([proj_step, proj_state, input_gain[:, None], small_block], axis=1), LANE
    )
    x_local = jnp.concatenate([proj_inner[:, 1, :], side], axis=1)
    x_all = lax.all_gather(x_local, "fsdp", axis=0, tiled=True)
    turned = jnp.concatenate(
        [proj_state.T, jnp.pad(conv_state.reshape(1, -1), ((0, 15), (0, shard - state_n)))], axis=0
    )
    turned = lax.all_gather(turned, "tp", axis=0, tiled=False)
    state_local = turned[:, :state_cols].reshape(tp_size * state_cols, shard).T
    conv_row = jnp.pad(
        turned[:, state_cols, :state_n].reshape(1, tp_size * state_n),
        ((0, 15), (0, tp_size * (state_cols - state_n))),
    )
    gate_all = lax.all_gather(proj_inner[:, 0, :], "fsdp", axis=0, tiled=True)
    block_sent, state_local = tied(block_in, state_local)
    row_parts = [by_rows(part) for part in gather_parts(block_sent, tp_size)]
    state_packed = gather_by_swaps(
        jnp.concatenate([state_local, conv_row], axis=0), fsdp_index, fsdp_size
    )
    out_local, *row_parts = tied(proj_output.T, *row_parts)
    out_all = lax.all_gather(out_local, "fsdp", axis=0, tiled=True)
    state_all = state_packed[:, :shard].reshape(model, tp_size * state_cols)
    taps_bc = (
        state_packed[:, shard, : tp_size * state_n]
        .reshape(fsdp_size, tp_size, 5, -1)
        .transpose(2, 1, 0, 3)
        .reshape(5, tp_size * state_cols)
        .astype(F32)
    )
    positions = tp_index * own_rows + jnp.arange(own_rows, dtype=jnp.int32)
    live_rows = (positions < filled)[:, None]
    block_f = block_in.astype(F32)
    cot_f = cotangent.astype(F32)
    own_grad, *row_parts = tied(
        jnp.where(live_rows, cot_f, 0.0).astype(BF16), *row_parts
    )
    grad_parts = [by_rows(own_grad)] + [swap(own_grad, k, tp_size) for k in range(1, tp_size)]

    side_all = x_all[:, width:]
    gain_f = side_all[:, used].astype(F32)
    extras = side_all[:, used + 1 : used + 1 + small_cols].reshape(fsdp_size, shard * small_cols)

    def from_owners(flat, rows):
        return flat.reshape(fsdp_size, rows, -1).transpose(1, 0, 2).reshape(rows, -1).astype(F32)

    taps_inner = from_owners(extras[:, :inner_n], 5)
    taps_state = from_owners(extras[:, inner_n : inner_n + state_n], 5)
    mixer_f = from_owners(extras[:, inner_n + state_n : small_count], 1)[0]

    def unit_of(rows):
        rows_f = rows.astype(F32)
        scale = lax.rsqrt(jnp.mean(rows_f * rows_f, axis=1, keepdims=True) + NORM_EPS)
        return rows_f * scale, scale

    def place(parts):
        whole = jnp.zeros((group_rows, model), BF16)
        for distance in range(tp_size):
            whole = lax.dynamic_update_slice(
                whole, parts[distance], ((tp_index ^ distance) * own_rows, jnp.int32(0))
            )
        return whole

    normed = by_rows(
        place([(unit_of(rows)[0] * gain_f[None, :]).astype(BF16) for rows in row_parts])
    )

    raw = mm(normed, x_all)
    bc_raw = mm(normed, state_all)
    meta, meta_rows = segment_tables(segment)
    expand, gather = head_tables(heads)
    taps8 = jnp.pad(taps_inner, ((0, 3), (0, 0)))
    taps_bc8 = jnp.pad(taps_bc, ((0, 3), (0, 0)))
    hp8 = head_rows(head_params)
    skip8 = jnp.broadcast_to(jnp.repeat(head_params[2], LANE // 2)[None, :], (8, width))
    mixed, states, bc = ssd_forward(
        raw, bc_raw, meta, meta_rows, taps8, taps_bc8, hp8, skip8, expand, heads
    )

    mixed, *grad_parts = tied(mixed, *grad_parts)
    group_grad = by_rows(place(grad_parts))

    z_raw = mm(normed, gate_all)
    sig = jax.nn.sigmoid(z_raw)
    gate_act = z_raw * sig
    gated = mixed * gate_act
    square_sum = lax.psum(jnp.sum(gated * gated, axis=1), "tp")
    inv_gate = lax.rsqrt(square_sum / DI + NORM_EPS)[:, None]
    unit_gated = gated * inv_gate
    normed_gated = (unit_gated * mixer_f[None, :]).astype(BF16)
    sum_out = pair_sum(
        contract_rows(group_grad, normed_gated).astype(BF16), fsdp_index, fsdp_size
    )
    group_grad, sum_out = tied(group_grad, sum_out)
    grad_out = chip_scatter(sum_out, fsdp_size)

    d_ng = mm(group_grad, out_all)
    d_unit = d_ng * mixer_f[None, :]
    inner_mean = lax.psum(jnp.sum(d_unit * unit_gated, axis=1), "tp")[:, None] / DI
    grad_mixer = jnp.sum(d_ng * unit_gated, axis=0)
    d_gated = inv_gate * (d_unit - unit_gated * inner_mean)
    d_mixed = d_gated * gate_act
    d_z = (d_gated * mixed * sig * (1.0 + z_raw * (1.0 - sig))).astype(BF16)
    part_gate, grad_out = tied(contract_rows(normed, d_z).astype(BF16), grad_out)
    sum_gate = pair_sum(part_gate, fsdp_index, fsdp_size)

    half = model // 2
    mixed_left = mm_nt(normed_gated, out_all[:half]).astype(BF16)
    mixed_right = mm_nt(normed_gated, out_all[half:]).astype(BF16)
    mixed_sent, mixed_kept = scatter_start(mixed_left, mixed_right, own_rows, tp_index, tp_size)
    d_mixed, sum_gate, mixed_left, mixed_right = tied(d_mixed, sum_gate, mixed_left, mixed_right)
    grad_gate = chip_scatter(sum_gate, fsdp_size)
    d_x, d_dt, d_bc, d_taps, d_heads, d_skip, small_turned = ssd_backward(
        raw,
        bc,
        meta,
        meta_rows,
        taps8,
        hp8,
        skip8,
        expand,
        gather,
        mixed,
        d_mixed,
        states,
        heads,
    )
    d_x, mixed_sent = tied(d_x, mixed_sent)
    mixed_passed, mixed_kept = scatter_middle(mixed_sent, mixed_kept, own_rows, tp_size)
    mixed_last = scatter_last(mixed_passed, tp_size)
    d_x, grad_gate = tied(d_x, grad_gate)
    sum_x = pair_sum(contract_rows(normed, d_x).astype(BF16), fsdp_index, fsdp_size)
    sum_x, d_z = tied(sum_x, d_z)
    grad_x = chip_scatter(sum_x, fsdp_size)

    def state_block(distance):
        return lax.dynamic_slice_in_dim(d_bc, (tp_index ^ distance) * state_cols, state_cols, 0)

    d_state_act = state_block(0)
    for k in range(1, tp_size):
        d_state_act = d_state_act + swap(state_block(k), k, tp_size)
    doc_masks = [meta[:, k] for k in range(1, 4)]
    _, state_back = jax.vjp(
        lambda raw_cols, conv_taps: state_act(raw_cols, conv_taps, doc_masks),
        small_turned[heads:used],
        taps_state,
    )
    d_state_raw, grad_conv_state = state_back(d_state_act)
    d_side = jnp.concatenate([d_dt[:heads], d_state_raw], axis=0)
    d_side = jnp.pad(d_side, ((0, LANE - used), (0, 0)))

    d_normed_left, gains_left = d_normed_half(d_z, d_x, d_side, gate_all, x_all, normed, 0)
    d_normed_right, gains_right = d_normed_half(d_z, d_x, d_side, gate_all, x_all, normed, 1)
    d_normed_left, *mixed_last = tied(d_normed_left, *mixed_last)
    mixed_rows = scatter_end(mixed_kept, mixed_last)
    block_out = (block_f + jnp.where(live_rows, mixed_rows, 0.0)).astype(BF16)
    sent, kept = scatter_start(d_normed_left, d_normed_right, own_rows, tp_index, tp_size)
    passed, kept = scatter_middle(sent, kept, own_rows, tp_size)
    grad_x, passed = tied(grad_x, passed)
    d_normed = scatter_end(kept, scatter_last(passed, tp_size))
    gain_sums = jnp.concatenate([gains_left[0], gains_right[0]], axis=0)

    grad_head = jnp.stack(
        [
            d_heads[0, :heads],
            hp8[1, :heads] * d_heads[1, :heads],
            jnp.sum(d_skip[0].reshape(heads, LANE // 2), axis=1),
        ],
        axis=0,
    )

    def by_owner(value):
        rows = value.shape[0]
        return value.reshape(rows, fsdp_size, -1).transpose(1, 0, 2).reshape(fsdp_size, -1)

    grad_extras = jnp.concatenate(
        [
            by_owner(d_taps[:5]),
            by_owner(grad_conv_state),
            by_owner(grad_mixer[None, :]),
            jnp.broadcast_to(grad_head.reshape(1, -1), (fsdp_size, 3 * heads)),
        ],
        axis=1,
    )
    grad_extras = pad_cols(grad_extras, small_cols * shard).reshape(fsdp_size * shard, small_cols)
    grad_extras = jnp.concatenate([gain_sums[:, None], grad_extras], axis=1)
    side_part = lax.dot_general(
        normed, d_side.astype(BF16), (((0,), (1,)), ((), ())), preferred_element_type=F32
    ) + jnp.pad(grad_extras, ((0, 0), (used, LANE - used - 1 - small_cols)))
    grad_side = chip_sum(pair_sum(side_part, fsdp_index, fsdp_size), fsdp_index, fsdp_size)
    grad_input_gain = all_sum(grad_side[:, used], tp_size) / input_gain.astype(F32)

    unit_rows, inv_rms = unit_of(block_in)
    scaled = d_normed * gain_f[None, :]
    d_block = inv_rms * (scaled - unit_rows * jnp.mean(scaled * unit_rows, axis=1, keepdims=True))
    d_input = (cot_f + d_block).astype(BF16)

    own_extras = grad_side[:, used + 1 : used + 1 + small_cols].reshape(-1)
    grads = (
        grad_input_gain,
        jnp.stack([grad_gate, grad_x], axis=1),
        grad_side[:, :heads],
        grad_side[:, heads:used],
        own_extras[:inner_n].reshape(conv_inner.shape),
        own_extras[inner_n : inner_n + state_n].reshape(conv_state.shape),
        own_extras[small_count : small_count + 3 * heads].reshape(3, heads),
        own_extras[inner_n + state_n : small_count],
        grad_out.T,
    )
    weights = (
        input_gain,
        proj_inner,
        proj_step,
        proj_state,
        conv_inner,
        conv_state,
        head_params,
        mixer_gain,
        proj_output,
    )
    large = (1, 2, 3, 8)
    updated = [
        adamw_step(
            weights[at],
            grads[at],
            moments[at],
            moments[9 + at],
            WEIGHT_DECAY if at in large else 0.0,
            LEARN_RATE if at in large else LEARN_SMALL,
        )
        for at in range(9)
    ]
    return (
        block_out,
        d_input,
        *grads,
        *[entry[0] for entry in updated],
        *[entry[1] for entry in updated],
        *[entry[2] for entry in updated],
    )


def weight_specs():
    return (
        P("fsdp"),
        P("fsdp", None, "tp"),
        P("fsdp", "tp"),
        P("fsdp", "tp"),
        P(None, ("tp", "fsdp")),
        P(None, ("tp", "fsdp")),
        P(None, "tp"),
        P(("tp", "fsdp")),
        P("tp", "fsdp"),
    )


def solution(mesh):
    rows = P(("fsdp", "tp"), None)
    return jax.shard_map(
        body,
        mesh=mesh,
        in_specs=(rows, rows, P("fsdp", None), P("fsdp")) + weight_specs() * 3,
        out_specs=(rows, rows) + weight_specs() * 4,
        check_vma=False,
    )
```

```python
import functools
import jax
import jax.numpy as jnp
from jax import lax
from jax.experimental import pallas as pl
from jax.experimental.layout import Layout, with_layout_constraint
from jax.experimental.pallas import tpu as pltpu
from jax.sharding import PartitionSpec as P

N = 128
Q = 256
LANE = 128
BLK = 128
SLOTS = 32
UNROLL = 10
LOG2E = 1.4426950408889634
F32 = jnp.float32
BF16 = jnp.bfloat16
VMEM_CAP = 56 << 20


def mm(left, right):
    return lax.dot_general(left, right, (((1,), (0,)), ((), ())), preferred_element_type=F32)


def mm_nt(left, right):
    return lax.dot_general(left, right, (((1,), (1,)), ((), ())), preferred_element_type=F32)


def split_two(value):
    high = value.astype(BF16)
    low = (value - high.astype(F32)).astype(BF16)
    return high, low


def split_three(value):
    high = value.astype(BF16).astype(F32)
    rest = value - high
    mid = rest.astype(BF16).astype(F32)
    return high, mid, rest - mid


def as_columns(value):
    parts = split_three(value)
    stacked = jnp.concatenate(list(parts) + [jnp.zeros_like(value)], axis=0)
    return stacked.T.astype(BF16)


def lane_sums(value, table):
    parts = jnp.concatenate(split_three(value), axis=0).astype(BF16)
    sums = mm(parts, table)
    return sums[:SLOTS] + sums[SLOTS : 2 * SLOTS] + sums[2 * SLOTS :]


def iota2(shape, axis):
    return lax.broadcasted_iota(jnp.int32, shape, axis)


def step_terms(small_ref, meta_ref, hp_ref):
    on = hp_ref[:, 2:3]
    pre = (small_ref[...] + hp_ref[:, 0:1]) * on
    steps = (jnp.maximum(pre, 0.0) + jnp.log1p(jnp.exp(-jnp.abs(pre)))) * on
    upto = (iota2((Q, Q), 0) <= iota2((Q, Q), 1)).astype(BF16)
    cum = lane_sums(steps * hp_ref[:, 1:2], upto) * LOG2E
    into = jnp.exp2(cum) * meta_ref[0, 1:2, :] * on
    tail = jnp.exp2(cum[:, Q - 1 : Q] - cum) * meta_ref[0, 2:3, :] * on
    return pre, steps, cum, into, tail


def ssd_fwd_kernel(
    heads,
    raw_ref,
    small_ref,
    bc_ref,
    masks_ref,
    meta_ref,
    seg_ref,
    taps_ref,
    hp_ref,
    skip_ref,
    expand_ref,
    widen_ref,
    y_ref,
    st_ref,
    state,
    tail_rows,
    window,
    row_cum,
    scores,
    columns,
    spreads,
    wide_cum,
):
    chunk = pl.program_id(0)

    @pl.when(chunk == 0)
    def _():
        state[...] = jnp.zeros_like(state)
        tail_rows[...] = jnp.zeros_like(tail_rows)

    st_ref[0] = state[...]
    _, steps, cum, into, tail = step_terms(small_ref, meta_ref, hp_ref)
    row_cum[...] = cum
    for at, value in enumerate((cum, steps, into, tail)):
        columns[at] = as_columns(value)
    for at in range(3):
        spreads[at] = mm(columns[at + 1], expand_ref[...])
    cum_cols = jnp.concatenate([cum] * 4, axis=0).T
    for head in range(heads):
        wide_cum[:, head * LANE : (head + 1) * LANE] = jnp.broadcast_to(
            cum_cols[:, head : head + 1], (Q, LANE)
        )
    same = (seg_ref[:, 0:1] == meta_ref[0, 0:1, :]) & (iota2((Q, Q), 0) >= iota2((Q, Q), 1))
    b_turned = bc_ref[:N, :]
    c_rows = bc_ref[N:, :].astype(F32).T.astype(BF16)
    scores[...] = jnp.where(same, mm(c_rows, b_turned), 0.0)
    first = iota2((Q, LANE), 1) < LANE // 2

    def pair(index, _):
        lanes = pl.ds(pl.multiple_of(index * LANE, LANE), LANE)
        both = pl.ds(pl.multiple_of(index * 2 * LANE, 2 * LANE), 2 * LANE)
        window[0:8, :] = tail_rows[:, lanes]
        current = raw_ref[:, lanes]
        window[8 : 8 + Q, :] = current
        conv = taps_ref[4:5, lanes] + taps_ref[3:4, lanes] * current
        for offset in range(1, 4):
            conv = conv + taps_ref[3 - offset : 4 - offset, lanes] * (
                masks_ref[:, (offset - 1) * LANE : offset * LANE]
                * window[8 - offset : 8 - offset + Q, :]
            )
        vals = conv * jax.nn.sigmoid(conv)
        scaled = (vals * spreads[0, :, lanes]).astype(BF16)
        zero = jnp.zeros_like(scaled)
        own = (jnp.where(first, scaled, zero), jnp.where(first, zero, scaled))
        held = state[:, lanes]
        into_here = spreads[1, :, lanes]
        base = into_here * mm(c_rows, held.astype(BF16)) + skip_ref[0:1, lanes] * vals
        cum_cols = wide_cum[:, both]
        for low in range(0, Q, BLK):
            width = low + BLK
            total = base[low:width, :]
            for which in range(2):
                across = row_cum[pl.ds(index * 2 + which, 1), :][:, :width]
                down = cum_cols[low:width, which * LANE : (which + 1) * LANE]
                down = jnp.concatenate([down] * (width // LANE), axis=1)
                decays = jnp.exp2(jnp.minimum(down - across, 0.0))
                mixing = (decays * scores[low:width, :width]).astype(BF16)
                total = total + mm(mixing, own[which][:width, :])
            y_ref[low:width, lanes] = total
        weighted = (spreads[2, :, lanes] * scaled.astype(F32)).astype(BF16)
        state[:, lanes] = held * into_here[Q - 1 : Q, :] + mm(b_turned, weighted)
        return 0

    lax.fori_loop(0, heads // 2, pair, 0, unroll=UNROLL)
    tail_rows[...] = raw_ref[Q - 8 : Q, :]


def ssd_bwd_kernel(
    heads,
    raw_ref,
    halo_ref,
    small_ref,
    bc_ref,
    masks_ref,
    masks_next_ref,
    meta_ref,
    seg_ref,
    taps_ref,
    hp_ref,
    skip_ref,
    expand_ref,
    widen_ref,
    gather_ref,
    y_ref,
    dy_ref,
    st_ref,
    dx_ref,
    ddt_ref,
    dbc_ref,
    dtaps_ref,
    dhp_ref,
    dskip_ref,
    dstate,
    next_rows,
    carried,
    window,
    dwindow,
    row_cum,
    scores,
    dscores,
    columns,
    into_dy,
    tail_vals,
    balance_parts,
    direct_parts,
    wide_cum,
):
    chunk = pl.program_id(0)

    @pl.when(chunk == 0)
    def _():
        dstate[...] = jnp.zeros_like(dstate)
        next_rows[...] = jnp.zeros_like(next_rows)
        carried[...] = jnp.zeros_like(carried)
        dtaps_ref[...] = jnp.zeros_like(dtaps_ref)
        dhp_ref[...] = jnp.zeros_like(dhp_ref)
        dskip_ref[...] = jnp.zeros_like(dskip_ref)

    pre, steps, cum, into, tail = step_terms(small_ref, meta_ref, hp_ref)
    row_cum[...] = cum
    for at, value in enumerate((cum, steps, into, tail)):
        columns[at] = as_columns(value)
    cum_cols = jnp.concatenate([cum] * 4, axis=0).T
    for head in range(heads):
        wide_cum[:, head * LANE : (head + 1) * LANE] = jnp.broadcast_to(
            cum_cols[:, head : head + 1], (Q, LANE)
        )
    same = (seg_ref[:, 0:1] == meta_ref[0, 0:1, :]) & (iota2((Q, Q), 0) <= iota2((Q, Q), 1))
    b_rows = bc_ref[:N, :].astype(F32).T.astype(BF16)
    c_turned = bc_ref[N:, :]
    scores[...] = jnp.where(same, mm(b_rows, c_turned), 0.0)
    dscores[...] = jnp.zeros_like(dscores)
    carry_high, carry_low = split_two(carried[...])
    gather_all = gather_ref[...]
    from_next = mm(carry_high, gather_all) + mm(carry_low, gather_all)
    dstate_half = dstate[...].astype(BF16)
    first = iota2((Q, LANE), 1) < LANE // 2

    def pair(index, _):
        lanes = pl.ds(pl.multiple_of(index * LANE, LANE), LANE)
        both = pl.ds(pl.multiple_of(index * 2 * LANE, 2 * LANE), 2 * LANE)
        window[0:8, :] = halo_ref[:, lanes]
        current = raw_ref[:, lanes]
        window[8 : 8 + Q, :] = current
        conv = taps_ref[4:5, lanes] + taps_ref[3:4, lanes] * current
        for offset in range(1, 4):
            conv = conv + taps_ref[3 - offset : 4 - offset, lanes] * (
                masks_ref[:, (offset - 1) * LANE : offset * LANE]
                * window[8 - offset : 8 - offset + Q, :]
            )
        gate = jax.nn.sigmoid(conv)
        vals = conv * gate
        expand = expand_ref[:, lanes]
        step_here = mm(columns[1], expand)
        scaled = (vals * step_here).astype(BF16)
        skip = skip_ref[0:1, lanes]
        dy = dy_ref[:, lanes]
        dy_half = dy.astype(BF16)
        zero = jnp.zeros_like(scaled)
        own = (jnp.where(first, scaled, zero), jnp.where(first, zero, scaled))
        own_dy = (jnp.where(first, dy_half, zero), jnp.where(first, zero, dy_half))
        dheld = dstate[:, lanes]
        tail_here = mm(columns[3], expand)
        into_here = mm(columns[2], expand)
        base = tail_here * mm(b_rows, dheld.astype(BF16))
        cum_cols = wide_cum[:, both]
        pieces = []
        for low in range(0, Q, BLK):
            high = low + BLK
            total = base[low:high, :]
            for which in range(2):
                across = row_cum[pl.ds(index * 2 + which, 1), :][:, low:]
                down = cum_cols[low:high, which * LANE : (which + 1) * LANE]
                down = jnp.concatenate([down] * ((Q - low) // LANE), axis=1)
                decays = jnp.exp2(jnp.minimum(across - down, 0.0))
                mixing = (decays * scores[low:high, low:]).astype(BF16)
                total = total + mm(mixing, own_dy[which][low:, :])
                dmix = mm_nt(own[which][low:high, :], dy_half[low:, :])
                dscores[low:high, low:] += dmix * decays
            pieces.append(total)
        dscaled = jnp.concatenate(pieces, axis=0)
        held = st_ref[0, :, lanes]
        edy = (into_here * dy).astype(BF16)
        scaled_f = scaled.astype(F32)
        into_dy[:, lanes] = edy
        tail_vals[:, lanes] = (tail_here * scaled_f).astype(BF16)
        balance = dy_half.astype(F32) * (y_ref[:, lanes] - skip * vals) - scaled_f * dscaled
        part_high, part_low = split_two(balance)
        balance_parts[0, :, lanes] = part_high
        balance_parts[1, :, lanes] = part_low
        part_high, part_low = split_two(vals * dscaled)
        direct_parts[0, :, lanes] = part_high
        direct_parts[1, :, lanes] = part_low
        dskip_ref[0:1, lanes] += jnp.sum(dy * vals, axis=0, keepdims=True)
        dheld_new = into_here[Q - 1 : Q, :] * dheld + mm(c_turned, edy)
        dstate[:, lanes] = dheld_new
        carried[0:1, lanes] = jnp.sum(dheld_new * held, axis=0, keepdims=True)
        dvals = step_here * dscaled + skip * dy
        dconv = dvals * (gate * (1.0 + conv * (1.0 - gate)))
        dwindow[0:Q, :] = dconv
        dwindow[Q : Q + 8, :] = next_rows[:, lanes]
        next_rows[:, lanes] = dconv[0:8, :]
        dtaps_ref[4:5, lanes] += jnp.sum(dconv, axis=0, keepdims=True)
        dtaps_ref[3:4, lanes] += jnp.sum(dconv * current, axis=0, keepdims=True)
        draw = taps_ref[3:4, lanes] * dconv
        for offset in range(1, 4):
            mask = masks_ref[:, (offset - 1) * LANE : offset * LANE]
            mask_next = masks_next_ref[:, (offset - 1) * LANE : offset * LANE]
            mask_later = jnp.concatenate([mask, mask_next], axis=0)[offset : offset + Q, :]
            shifted = mask * window[8 - offset : 8 - offset + Q, :]
            dtaps_ref[3 - offset : 4 - offset, lanes] += jnp.sum(
                dconv * shifted, axis=0, keepdims=True
            )
            draw = draw + taps_ref[3 - offset : 4 - offset, lanes] * (
                mask_later * dwindow[offset : offset + Q, :]
            )
        dx_ref[:, lanes] = draw.astype(BF16)
        return 0

    lax.fori_loop(0, heads // 2, pair, 0, unroll=UNROLL)
    dscores_now = jnp.where(same, dscores[...], 0.0)
    d_b = mm_nt(tail_vals[...], dstate_half) + mm_nt(dscores_now.astype(BF16), c_turned)
    d_c = mm_nt(into_dy[...], st_ref[0].astype(BF16)) + mm(dscores_now.T.astype(BF16), b_rows)
    dbc_ref[:N, :] = d_b.T
    dbc_ref[N:, :] = d_c.T
    balance = mm(balance_parts[0], gather_all) + mm(balance_parts[1], gather_all)
    balance = balance + jnp.where(iota2((Q, LANE), 0) == Q - 1, from_next[0:1, :], 0.0)
    direct = mm(direct_parts[0], gather_all) + mm(direct_parts[1], gather_all)
    since = (iota2((Q, Q), 0) >= iota2((Q, Q), 1)).astype(BF16)
    dlogs = lane_sums(balance.T[:SLOTS], since)
    dsteps = dlogs * hp_ref[:, 1:2] + direct.T[:SLOTS]
    dsteps = dsteps * jax.nn.sigmoid(pre) * hp_ref[:, 2:3]
    ddt_ref[...] = dsteps
    dhp_ref[:, 0:1] += jnp.sum(dsteps, axis=1, keepdims=True)
    dhp_ref[:, 1:2] += jnp.sum(dlogs * steps, axis=1, keepdims=True)


def head_tables(heads):
    width = heads * (LANE // 2)
    owner = jnp.arange(width) // (LANE // 2)
    wide_owner = jnp.arange(heads * LANE) // LANE
    slot = jnp.arange(LANE)
    real = (slot < 3 * SLOTS)[:, None]
    expand = ((slot % SLOTS)[:, None] == owner[None, :]) & real
    widen = ((slot % SLOTS)[:, None] == wide_owner[None, :]) & real
    gather = owner[:, None] == slot[None, :]
    return expand.astype(BF16), widen.astype(BF16), gather.astype(BF16)


def segment_tables(segment):
    length = segment.shape[0]
    chunks = length // Q
    doc_masks = []
    for offset in range(1, 4):
        earlier = jnp.concatenate(
            [jnp.full((offset,), -1, jnp.int32), segment[: length - offset]], axis=0
        )
        doc_masks.append((earlier == segment).astype(F32))
    masks = jnp.concatenate(
        [jnp.broadcast_to(mask[:, None], (length, LANE)) for mask in doc_masks], axis=1
    )
    by_chunk = segment.reshape(chunks, Q)
    last = by_chunk[:, Q - 1]
    before = jnp.concatenate([jnp.full((1,), -1, jnp.int32), last[: chunks - 1]], axis=0)
    rows = [
        by_chunk.astype(F32),
        (by_chunk == before[:, None]).astype(F32),
        (by_chunk == last[:, None]).astype(F32),
    ]
    meta = jnp.pad(jnp.stack(rows, axis=1), ((0, 0), (0, 5), (0, 0)))
    seg_cols = jnp.broadcast_to(segment.astype(F32)[:, None], (length, LANE))
    return doc_masks, masks, meta, seg_cols


def head_columns(head_params):
    heads = head_params.shape[1]
    rates = -jnp.exp(head_params[1])
    table = jnp.stack([head_params[0], rates, jnp.ones_like(rates)], axis=1)
    return jnp.pad(table, ((0, SLOTS - heads), (0, LANE - 3)))


def time_like(seconds):
    return pl.CostEstimate(
        flops=int(seconds * 1.1e15), bytes_accessed=int(seconds * 3.4e12), transcendentals=0
    )


def full_spec(shape):
    return pl.BlockSpec(shape, lambda c: (0,) * len(shape))


def ssd_forward(raw, small, bc, tables, taps, hp, skip, spread, heads):
    length = raw.shape[0]
    width = heads * (LANE // 2)
    chunks = length // Q
    _, masks, meta, seg_cols = tables
    expand, widen, _ = spread
    return pl.pallas_call(
        functools.partial(ssd_fwd_kernel, heads),
        grid=(chunks,),
        out_shape=(
            jax.ShapeDtypeStruct((length, width), F32),
            jax.ShapeDtypeStruct((chunks, N, width), F32),
        ),
        in_specs=[
            pl.BlockSpec((Q, width), lambda c: (c, 0)),
            pl.BlockSpec((SLOTS, Q), lambda c: (0, c)),
            pl.BlockSpec((2 * N, Q), lambda c: (0, c)),
            pl.BlockSpec((Q, 3 * LANE), lambda c: (c, 0)),
            pl.BlockSpec((1, 8, Q), lambda c: (c, 0, 0)),
            pl.BlockSpec((Q, LANE), lambda c: (c, 0)),
            full_spec((8, width)),
            full_spec((SLOTS, LANE)),
            full_spec((8, width)),
            full_spec((LANE, width)),
            full_spec((LANE, heads * LANE)),
        ],
        out_specs=(
            pl.BlockSpec((Q, width), lambda c: (c, 0)),
            pl.BlockSpec((1, N, width), lambda c: (c, 0, 0)),
        ),
        scratch_shapes=[
            pltpu.VMEM((N, width), F32),
            pltpu.VMEM((8, width), F32),
            pltpu.VMEM((Q + 8, LANE), F32),
            pltpu.VMEM((SLOTS, Q), F32),
            pltpu.VMEM((Q, Q), F32),
            pltpu.VMEM((4, Q, LANE), BF16),
            pltpu.VMEM((3, Q, width), F32),
            pltpu.VMEM((Q, heads * LANE), F32),
        ],
        compiler_params=pltpu.CompilerParams(vmem_limit_bytes=VMEM_CAP),
        cost_estimate=time_like(37e-6 * length * heads / 30720),
        name="ssd_fwd",
    )(raw, small, bc, masks, meta, seg_cols, taps, hp, skip, expand, widen)


def ssd_backward(raw, small, bc, tables, taps, hp, skip, spread, y, dy, states, heads):
    length = raw.shape[0]
    width = heads * (LANE // 2)
    chunks = length // Q
    per = Q // 8
    _, masks, meta, seg_cols = tables

    def at(c):
        return chunks - 1 - c

    return pl.pallas_call(
        functools.partial(ssd_bwd_kernel, heads),
        grid=(chunks,),
        out_shape=(
            jax.ShapeDtypeStruct((length, width), BF16),
            jax.ShapeDtypeStruct((SLOTS, length), F32),
            jax.ShapeDtypeStruct((2 * N, length), F32),
            jax.ShapeDtypeStruct((8, width), F32),
            jax.ShapeDtypeStruct((SLOTS, LANE), F32),
            jax.ShapeDtypeStruct((8, width), F32),
        ),
        in_specs=[
            pl.BlockSpec((Q, width), lambda c: (at(c), 0)),
            pl.BlockSpec((8, width), lambda c: (jnp.maximum(at(c) * per - 1, 0), 0)),
            pl.BlockSpec((SLOTS, Q), lambda c: (0, at(c))),
            pl.BlockSpec((2 * N, Q), lambda c: (0, at(c))),
            pl.BlockSpec((Q, 3 * LANE), lambda c: (at(c), 0)),
            pl.BlockSpec(
                (8, 3 * LANE), lambda c: (jnp.minimum((at(c) + 1) * per, chunks * per - 1), 0)
            ),
            pl.BlockSpec((1, 8, Q), lambda c: (at(c), 0, 0)),
            pl.BlockSpec((Q, LANE), lambda c: (at(c), 0)),
            full_spec((8, width)),
            full_spec((SLOTS, LANE)),
            full_spec((8, width)),
            full_spec((LANE, width)),
            full_spec((LANE, heads * LANE)),
            full_spec((width, LANE)),
            pl.BlockSpec((Q, width), lambda c: (at(c), 0)),
            pl.BlockSpec((Q, width), lambda c: (at(c), 0)),
            pl.BlockSpec((1, N, width), lambda c: (at(c), 0, 0)),
        ],
        out_specs=(
            pl.BlockSpec((Q, width), lambda c: (at(c), 0)),
            pl.BlockSpec((SLOTS, Q), lambda c: (0, at(c))),
            pl.BlockSpec((2 * N, Q), lambda c: (0, at(c))),
            full_spec((8, width)),
            full_spec((SLOTS, LANE)),
            full_spec((8, width)),
        ),
        scratch_shapes=[
            pltpu.VMEM((N, width), F32),
            pltpu.VMEM((8, width), F32),
            pltpu.VMEM((8, width), F32),
            pltpu.VMEM((Q + 8, LANE), F32),
            pltpu.VMEM((Q + 8, LANE), F32),
            pltpu.VMEM((SLOTS, Q), F32),
            pltpu.VMEM((Q, Q), F32),
            pltpu.VMEM((Q, Q), F32),
            pltpu.VMEM((4, Q, LANE), BF16),
            pltpu.VMEM((Q, width), BF16),
            pltpu.VMEM((Q, width), BF16),
            pltpu.VMEM((2, Q, width), BF16),
            pltpu.VMEM((2, Q, width), BF16),
            pltpu.VMEM((Q, heads * LANE), F32),
        ],
        compiler_params=pltpu.CompilerParams(vmem_limit_bytes=VMEM_CAP),
        cost_estimate=time_like(69e-6 * length * heads / 30720),
        name="ssd_bwd",
    )(
        raw,
        raw,
        small,
        bc,
        masks,
        masks,
        meta,
        seg_cols,
        taps,
        hp,
        skip,
        *spread,
        y,
        dy,
        states,
    )


def dn_kernel(count, rows, at_ref, *refs):
    dz, dx, side, normed = (refs[k * count : (k + 1) * count] for k in range(4))
    gate_ref, inner_ref, out_ref, sums_ref = refs[4 * count : 4 * count + 4]
    turned = refs[4 * count + 4]
    width = dz[0].shape[1]

    @pl.when(pl.program_id(0) == 0)
    def _():
        for k in range(count):
            turned[k * rows : (k + 1) * rows, :] = side[k][...].T.astype(BF16)

    gate = gate_ref[...]
    inner = inner_ref[:, :width]
    last = inner_ref[:, width:]
    sums = None
    for k in range(count):
        at = slice(k * rows, (k + 1) * rows)
        total = mm_nt(dz[k][...], gate) + mm_nt(dx[k][...], inner) + mm_nt(turned[at, :], last)
        out_ref[at, :] = total.astype(BF16)
        part = jnp.sum(total * normed[k][...].astype(F32), axis=0, keepdims=True)
        sums = part if sums is None else sums + part
    sums_ref[0:1, :] = sums


def d_normed_blocks(d_z, d_x, d_side, gate_all, x_all, normed, blocks, which, rows, tile=256):
    length, width = d_z.shape
    count = blocks.shape[0]
    half = gate_all.shape[0] // 2
    first = which * half // tile

    def rows_of(k):
        return pl.BlockSpec((rows, width), lambda n, at, k=k: (at[k], 0))

    def cols_of(k):
        return pl.BlockSpec((LANE, rows), lambda n, at, k=k: (0, at[k]))

    def tile_of(k):
        return pl.BlockSpec((rows, tile), lambda n, at, k=k: (at[k], n + first))

    each = range(count)
    return pl.pallas_call(
        functools.partial(dn_kernel, count, rows),
        grid_spec=pltpu.PrefetchScalarGridSpec(
            num_scalar_prefetch=1,
            grid=(half // tile,),
            in_specs=[rows_of(k) for k in each]
            + [rows_of(k) for k in each]
            + [cols_of(k) for k in each]
            + [tile_of(k) for k in each]
            + [
                pl.BlockSpec((tile, width), lambda n, at: (n + first, 0)),
                pl.BlockSpec((tile, width + LANE), lambda n, at: (n + first, 0)),
            ],
            out_specs=(
                pl.BlockSpec((count * rows, tile), lambda n, at: (0, n)),
                pl.BlockSpec((8, tile), lambda n, at: (0, n)),
            ),
            scratch_shapes=[pltpu.VMEM((count * rows, LANE), BF16)],
        ),
        out_shape=(
            jax.ShapeDtypeStruct((count * rows, half), BF16),
            jax.ShapeDtypeStruct((8, half), F32),
        ),
        compiler_params=pltpu.CompilerParams(vmem_limit_bytes=VMEM_CAP),
        cost_estimate=time_like(1e-7),
        name="d_normed",
    )(
        blocks,
        *([d_z] * count),
        *([d_x] * count),
        *([d_side] * count),
        *([normed] * count),
        gate_all,
        x_all,
    )


def adam_kernel(step, gate_ref, inner_ref, weight_ref, first_ref, second_ref, *outs):
    grad_out, weight_out, first_out, second_out = outs
    for part, grad_ref in ((0, gate_ref), (1, inner_ref)):
        grad = grad_ref[...].astype(F32)
        new_weight, new_first, new_second = step(
            weight_ref[:, part, :], grad, first_ref[:, part, :], second_ref[:, part, :]
        )
        grad_out[:, part, :] = grad
        weight_out[:, part, :] = new_weight
        first_out[:, part, :] = new_first
        second_out[:, part, :] = new_second


def adam_pair(step, grad_gate, grad_inner, weight, first, second, rows=40):
    shard, _, width = weight.shape
    deep = pl.BlockSpec((rows, 2, width), lambda n: (n, 0, 0))
    flat = pl.BlockSpec((rows, width), lambda n: (n, 0))
    like = jax.ShapeDtypeStruct(weight.shape, F32)
    return pl.pallas_call(
        functools.partial(adam_kernel, step),
        grid=(shard // rows,),
        out_shape=(like, jax.ShapeDtypeStruct(weight.shape, weight.dtype), like, like),
        in_specs=[flat, flat, deep, deep, deep],
        out_specs=(deep,) * 4,
        compiler_params=pltpu.CompilerParams(vmem_limit_bytes=VMEM_CAP),
        cost_estimate=pl.CostEstimate(flops=1000, bytes_accessed=1000, transcendentals=0),
        name="adam_pair",
    )(grad_gate, grad_inner, weight, first, second)

DI = 5120
STEP = 3
NORM_EPS = 1e-05
BETA_ONE = 0.9
BETA_TWO = 0.95
LEARN_RATE = 0.004
LEARN_SMALL = 0.15
WEIGHT_DECAY = 0.1
ADAM_EPS = 1e-08


def by_rows(value):
    return with_layout_constraint(value, Layout(major_to_minor=(0, 1)))


def silu_act(values):
    return values * jax.nn.sigmoid(values)


def later(row, offset):
    return jnp.pad(row, ((0, 0), (offset, 0)))[:, : row.shape[1]]


def state_act(raw_cols, conv_taps, doc_masks):
    conv = conv_taps[4][:, None] + conv_taps[3][:, None] * raw_cols
    for offset in range(1, 4):
        conv = conv + conv_taps[3 - offset][:, None] * (
            doc_masks[offset - 1][None, :] * later(raw_cols, offset)
        )
    return silu_act(conv)


def contract_rows(left_mat, right_mat):
    return lax.dot_general(
        left_mat, right_mat, (((0,), (0,)), ((), ())), preferred_element_type=F32
    )


def adamw_step(weight, gradient, first_moment, second_moment, decay_factor, learn_rate):
    new_first = BETA_ONE * first_moment + (1.0 - BETA_ONE) * gradient
    new_second = BETA_TWO * second_moment + (1.0 - BETA_TWO) * gradient * gradient
    first_hat = new_first / (1.0 - BETA_ONE**STEP)
    second_hat = new_second / (1.0 - BETA_TWO**STEP)
    weight_f = weight.astype(F32)
    updated = weight_f - learn_rate * (
        first_hat / (jnp.sqrt(second_hat) + ADAM_EPS) + decay_factor * weight_f
    )
    return (updated.astype(weight.dtype), new_first, new_second)


def swap(value, distance, size):
    return lax.ppermute(value, "tp", [(at, at ^ distance) for at in range(size)])


def tied(*values):
    return lax.optimization_barrier(values)


def gather_parts(value, size, near_done):
    if size != 4:
        one, *others = near_done(swap(value, 1, size))
        return [value, one] + [swap(value, k, size) for k in range(2, size)], *others
    half = value.shape[0] // 2
    one, two = swap(value, 1, size), swap(value, 2, size)
    one, *others = near_done(one)
    far = jnp.concatenate([swap(two[:half], 1, size), swap(one[half:], 2, size)], axis=0)
    return [value, one, two, far], *others


def scatter_start(left, right, rows, index, size):
    def block(value, distance):
        return lax.dynamic_slice_in_dim(value, (index ^ distance) * rows, rows, 0)

    sent, kept = [], []
    for half, near in ((left, 1), (right, 2)):
        if size == 4:
            pair = jnp.concatenate([block(half, 3), block(half, near)], axis=0)
            sent.append(swap(pair, near, size))
            kept.append((block(half, 3 - near), block(half, 0)))
        else:
            sent.append([swap(block(half, k), k, size) for k in range(1, size)])
            kept.append(block(half, 0))
    return sent, kept


def scatter_middle(sent, kept, rows, size):
    if size != 4:
        return sent, [(one,) for one in kept]
    passed = [
        (kept[at][0].astype(F32) + sent[at][:rows].astype(F32)).astype(BF16) for at in range(2)
    ]
    return passed, [(kept[at][1], sent[at][rows:]) for at in range(2)]


def scatter_last(passed, size):
    if size != 4:
        return passed[0] + passed[1]
    return [swap(passed[0], 2, size), swap(passed[1], 1, size)]


def scatter_end(own, last):
    each = len(last) // 2
    totals = []
    for at in range(2):
        total = own[at][0].astype(F32)
        for piece in own[at][1:]:
            total = total + piece.astype(F32)
        for piece in last[at * each : (at + 1) * each]:
            total = total + piece.astype(F32)
        totals.append(total)
    return jnp.concatenate(totals, axis=1)


def all_sum(value, size):
    distance = 1
    while distance < size:
        value = value + swap(value, distance, size)
        distance *= 2
    return value


def fsdp_swap(value, distance, size):
    return lax.ppermute(value, "fsdp", [(at, at ^ distance) for at in range(size)])


def gather_by_swaps(value, index, size):
    whole = jnp.zeros((size,) + value.shape, value.dtype)
    for distance in range(size):
        piece = value if distance == 0 else fsdp_swap(value, distance, size)
        whole = lax.dynamic_update_slice(whole, piece[None], (index ^ distance, jnp.int32(0)))
    return whole


def pair_sum(value, index, size):
    blocks = value.reshape(size // 2, 2, value.shape[0] // size, value.shape[1])
    core = index % 2
    away = lax.dynamic_slice_in_dim(blocks, 1 - core, 1, 1)[:, 0]
    own = lax.dynamic_slice_in_dim(blocks, core, 1, 1)[:, 0]
    return (own.astype(F32) + fsdp_swap(away, 1, size).astype(F32)).astype(value.dtype)


def chip_scatter(value, size):
    groups = [list(range(core, size, 2)) for core in range(2)]
    flat = value.reshape(value.shape[0] * value.shape[1], value.shape[2])
    return lax.psum_scatter(
        flat, "fsdp", scatter_dimension=0, axis_index_groups=groups, tiled=True
    )


def chip_sum(value, index, size):
    chip = index // 2

    def block(distance):
        return lax.dynamic_slice_in_dim(value, chip ^ distance, 1, 0)[0]

    total = block(0).astype(F32)
    for distance in range(1, size // 2):
        total = total + fsdp_swap(block(distance), 2 * distance, size).astype(F32)
    return total


def pad_cols(value, width):
    return jnp.pad(value, ((0, 0), (0, width - value.shape[1])))


def body(
    block_in,
    cotangent,
    segment_ids,
    group_fill,
    input_gain,
    proj_inner,
    proj_step,
    proj_state,
    conv_inner,
    conv_state,
    head_params,
    mixer_gain,
    proj_output,
    *moments,
):
    tp_size = lax.axis_size("tp")
    fsdp_size = lax.axis_size("fsdp")
    tp_index = lax.axis_index("tp")
    fsdp_index = lax.axis_index("fsdp")
    own_rows, model = block_in.shape
    group_rows = own_rows * tp_size
    shard, _, width = proj_inner.shape
    heads = proj_step.shape[1]
    state_cols = proj_state.shape[1]
    segment = segment_ids[0]
    filled = group_fill[0]

    small_values = jnp.concatenate(
        [conv_inner.reshape(-1), conv_state.reshape(-1), mixer_gain], axis=0
    )
    small_count = small_values.shape[0]
    inner_n, state_n = conv_inner.size, conv_state.size
    small_cols = -(-(small_count + 3 * heads) // shard)
    small_block = jnp.pad(small_values, (0, small_cols * shard - small_count)).reshape(
        shard, small_cols
    )
    used = heads + state_cols
    side = pad_cols(
        jnp.concatenate([proj_step, proj_state, input_gain[:, None], small_block], axis=1), LANE
    )
    x_local = jnp.concatenate([proj_inner[:, 1, :], side], axis=1)
    x_all = lax.all_gather(x_local, "fsdp", axis=0, tiled=True)
    gate_all = lax.all_gather(proj_inner[:, 0, :], "fsdp", axis=0, tiled=True)
    gain_all = lax.dynamic_update_slice(
        jnp.zeros((fsdp_size, shard), BF16), input_gain[None], (fsdp_index, jnp.int32(0))
    )
    distance = 1
    while distance < fsdp_size:
        gain_all = gain_all + fsdp_swap(gain_all, distance, fsdp_size)
        distance *= 2
    gain_f = gain_all.reshape(model).astype(F32)
    positions = tp_index * own_rows + jnp.arange(own_rows, dtype=jnp.int32)
    live_rows = (positions < filled)[:, None]
    block_f = block_in.astype(F32)
    cot_f = cotangent.astype(F32)
    own_grad = jnp.where(live_rows, cot_f, 0.0).astype(BF16)
    blank = jnp.zeros((group_rows, model), BF16)

    def unit_of(rows):
        rows_f = rows.astype(F32)
        scale = lax.rsqrt(jnp.mean(rows_f * rows_f, axis=1, keepdims=True) + NORM_EPS)
        return rows_f * scale, scale

    def normed_of(rows):
        return (unit_of(rows)[0] * gain_f[None, :]).astype(BF16)

    def put(whole, part, distance):
        return lax.dynamic_update_slice(
            whole, part, ((tp_index ^ distance) * own_rows, jnp.int32(0))
        )

    started = put(blank, normed_of(block_in), 0)

    def near_done(one):
        return tied(one, started, own_grad)

    row_parts, started, own_grad = gather_parts(block_in, tp_size, near_done)
    row_parts = [by_rows(part) for part in row_parts]
    out_local, *row_parts = tied(proj_output.T, *row_parts)
    out_all = lax.all_gather(out_local, "fsdp", axis=0, tiled=True)
    own_grad, *row_parts = tied(own_grad, *row_parts)
    near = min(3, tp_size)
    grad_parts = [by_rows(own_grad)] + [swap(own_grad, k, tp_size) for k in range(1, near)]

    side_all = x_all[:, width:]
    extras = side_all[:, used + 1 : used + 1 + small_cols].reshape(fsdp_size, shard * small_cols)

    def from_owners(flat, rows):
        return flat.reshape(fsdp_size, rows, -1).transpose(1, 0, 2).reshape(rows, -1).astype(F32)

    taps_inner = from_owners(extras[:, :inner_n], 5)
    taps_state = from_owners(extras[:, inner_n : inner_n + state_n], 5)
    mixer_f = from_owners(extras[:, inner_n + state_n : small_count], 1)[0]

    normed = started
    for distance in range(1, tp_size - 1):
        normed = put(normed, normed_of(row_parts[distance]), distance)
    far_rows, normed = tied(row_parts[-1], normed)
    normed = by_rows(put(normed, normed_of(far_rows), tp_size - 1))
    small = lax.dot_general(
        side_all, normed, (((0,), (1,)), ((), ())), preferred_element_type=F32
    )
    raw = mm(normed, x_all)
    tables = segment_tables(segment)
    doc_masks = tables[0]
    state_vals, state_back = jax.vjp(
        lambda raw_cols, conv_taps: state_act(raw_cols, conv_taps, doc_masks),
        small[heads:used],
        taps_state,
    )
    state_local = state_vals.astype(BF16)
    bc = jnp.zeros((tp_size * state_cols, group_rows), BF16)
    for k in range(tp_size):
        piece = state_local if k == 0 else swap(state_local, k, tp_size)
        bc = lax.dynamic_update_slice(bc, piece, ((tp_index ^ k) * state_cols, jnp.int32(0)))
    own_grad, bc = tied(own_grad, bc)
    grad_parts += [swap(own_grad, k, tp_size) for k in range(near, tp_size)]
    spread = head_tables(heads)
    taps8 = jnp.pad(taps_inner, ((0, 3), (0, 0)))
    hp8 = head_columns(head_params)
    skip8 = jnp.broadcast_to(jnp.repeat(head_params[2], LANE // 2)[None, :], (8, width))
    mixed, states = ssd_forward(raw, small, bc, tables, taps8, hp8, skip8, spread, heads)

    z_raw = mm(normed, gate_all)
    sig = jax.nn.sigmoid(z_raw)
    gate_act = z_raw * sig
    gated = mixed * gate_act
    square_sum, *grad_parts = tied(jnp.sum(gated * gated, axis=1), *grad_parts)
    square_sum = all_sum(square_sum, tp_size)
    group_grad = jnp.zeros((group_rows, model), BF16)
    for distance in range(tp_size):
        group_grad = put(group_grad, grad_parts[distance], distance)
    group_grad = by_rows(group_grad)
    inv_gate = lax.rsqrt(square_sum / DI + NORM_EPS)[:, None]
    unit_gated = gated * inv_gate
    normed_gated = (unit_gated * mixer_f[None, :]).astype(BF16)
    sum_out = pair_sum(
        contract_rows(group_grad, normed_gated).astype(BF16), fsdp_index, fsdp_size
    )
    half = model // 2
    mixed_halves = [mm_nt(normed_gated, out_all[:half])]
    normed_gated, sum_out = tied(normed_gated, sum_out)
    grad_out = chip_scatter(sum_out, fsdp_size)
    mixed_halves.append(mm_nt(normed_gated, out_all[half:]))
    inner_sum = jnp.sum(mixed_halves[0] * group_grad[:, :half].astype(F32), axis=1) + jnp.sum(
        mixed_halves[1] * group_grad[:, half:].astype(F32), axis=1
    )
    inner_sum = all_sum(inner_sum, tp_size)
    mixed_left, mixed_right = (part.astype(BF16) for part in mixed_halves)
    mixed_sent, mixed_kept = scatter_start(mixed_left, mixed_right, own_rows, tp_index, tp_size)

    inner_mean = inner_sum[:, None] / DI
    d_ng = mm(group_grad, out_all)
    grad_mixer = jnp.sum(d_ng * unit_gated, axis=0)
    d_gated = inv_gate * (d_ng * mixer_f[None, :] - unit_gated * inner_mean)
    d_mixed = d_gated * gate_act
    d_z = (d_gated * mixed * sig * (1.0 + z_raw * (1.0 - sig))).astype(BF16)
    part_gate, mixed_sent = tied(contract_rows(normed, d_z).astype(BF16), mixed_sent)
    sum_gate = pair_sum(part_gate, fsdp_index, fsdp_size)
    mixed_passed, mixed_kept = scatter_middle(mixed_sent, mixed_kept, own_rows, tp_size)
    sum_gate, grad_out = tied(sum_gate, grad_out)

    d_mixed, sum_gate, mixed_passed = tied(d_mixed, sum_gate, mixed_passed)
    mixed_last = scatter_last(mixed_passed, tp_size)
    grad_gate = chip_scatter(sum_gate, fsdp_size)
    d_x, d_dt, d_bc, d_taps, d_heads, d_skip = ssd_backward(
        raw, small, bc, tables, taps8, hp8, skip8, spread, mixed, d_mixed, states, heads
    )
    def state_block(distance):
        return lax.dynamic_slice_in_dim(d_bc, (tp_index ^ distance) * state_cols, state_cols, 0)

    state_parts = [state_block(0)]
    state_parts += [swap(state_block(k), k, tp_size) for k in range(1, tp_size)]
    part_x, mixed_last, grad_gate, *state_parts = tied(
        contract_rows(normed, d_x).astype(BF16), mixed_last, grad_gate, *state_parts
    )
    sum_x = pair_sum(part_x, fsdp_index, fsdp_size)

    d_state_raw, grad_conv_state = state_back(sum(state_parts[1:], state_parts[0]).astype(F32))
    d_side = jnp.concatenate([d_dt[:heads], d_state_raw], axis=0)
    d_side = jnp.pad(d_side, ((0, LANE - used), (0, 0)))

    four = tp_size == 4
    side_part = lax.dot_general(
        normed, d_side.astype(BF16), (((0,), (1,)), ((), ())), preferred_element_type=F32
    )

    def side_gradient(side_part, d_taps, d_skip, d_heads, grad_conv_state, gain_sums):
        grad_head = jnp.stack(
            [
                d_heads[:heads, 0],
                hp8[:heads, 1] * d_heads[:heads, 1],
                jnp.sum(d_skip[0].reshape(heads, LANE // 2), axis=1),
            ],
            axis=0,
        )

        def by_owner(value):
            rows = value.shape[0]
            return value.reshape(rows, fsdp_size, -1).transpose(1, 0, 2).reshape(fsdp_size, -1)

        grad_extras = jnp.concatenate(
            [
                by_owner(d_taps[:5]),
                by_owner(grad_conv_state),
                by_owner(grad_mixer[None, :]),
                jnp.broadcast_to(grad_head.reshape(1, -1), (fsdp_size, 3 * heads)),
            ],
            axis=1,
        )
        grad_extras = pad_cols(grad_extras, small_cols * shard).reshape(fsdp_size * shard, small_cols)
        grad_extras = jnp.concatenate([gain_sums[:, None], grad_extras], axis=1)
        side_part = side_part + jnp.pad(
            grad_extras, ((0, 0), (used, LANE - used - 1 - small_cols))
        )
        side_part = pair_sum(side_part, fsdp_index, fsdp_size)
        return chip_sum(side_part, fsdp_index, fsdp_size)

    def d_normed_of(distances, which):
        return d_normed_blocks(
            d_z, d_x, d_side, gate_all, x_all, normed, tp_index ^ jnp.array(distances), which, own_rows
        )

    if four:
        left_away, gains_one = d_normed_of([3, 1], 0)
        gains_one, sum_x = tied(gains_one, sum_x)
        right_away, gains_two = d_normed_of([3, 2], 1)
        gains_two, mixed_last, d_taps, d_skip, d_heads, grad_conv_state = tied(
            gains_two, mixed_last, d_taps, d_skip, d_heads, grad_conv_state
        )
        sent = [swap(left_away, 1, 4), swap(right_away, 2, 4)]
        left_kept, gains_three = d_normed_of([2, 0], 0)
        sent[0], d_side_late, side_part = tied(sent[0], d_side, side_part)
        right_kept, gains_four = d_normed_blocks(
            d_z, d_x, d_side_late, gate_all, x_all, normed, tp_index ^ jnp.array([1, 0]), 1, own_rows
        )
        kept = [
            (left_kept[:own_rows], left_kept[own_rows:]),
            (right_kept[:own_rows], right_kept[own_rows:]),
        ]
        gain_sums = jnp.concatenate([gains_one + gains_three, gains_two + gains_four], axis=1)[0]
    else:
        left, gains_one = d_normed_of(list(range(tp_size)), 0)
        right, gains_two = d_normed_of(list(range(tp_size)), 1)
        sent = [
            [
                swap(part[k * own_rows : (k + 1) * own_rows], k, tp_size)
                for k in range(1, tp_size)
            ]
            for part in (left, right)
        ]
        kept = [left[:own_rows], right[:own_rows]]
        gain_sums = jnp.concatenate([gains_one, gains_two], axis=1)[0]
    grad_x = chip_scatter(sum_x, fsdp_size)
    passed, kept = scatter_middle(sent, kept, own_rows, tp_size)
    passed, mixed_last = tied(passed, mixed_last)
    mixed_rows = scatter_end(mixed_kept, mixed_last)
    block_out = (block_f + jnp.where(live_rows, mixed_rows, 0.0)).astype(BF16)
    grad_x, passed = tied(grad_x, passed)
    last = scatter_last(passed, tp_size)
    grad_side = side_gradient(side_part, d_taps, d_skip, d_heads, grad_conv_state, gain_sums)
    gain_part, last[0] = tied(grad_side[:, used], last[0])
    grad_input_gain = all_sum(gain_part, tp_size) / input_gain.astype(F32)
    d_normed = scatter_end(kept, last)

    unit_rows, inv_rms = unit_of(block_in)
    scaled = d_normed * gain_f[None, :]
    d_block = inv_rms * (scaled - unit_rows * jnp.mean(scaled * unit_rows, axis=1, keepdims=True))
    d_input = (cot_f + d_block).astype(BF16)

    own_extras = grad_side[:, used + 1 : used + 1 + small_cols].reshape(-1)
    grads = (
        grad_input_gain,
        None,
        grad_side[:, :heads],
        grad_side[:, heads:used],
        own_extras[:inner_n].reshape(conv_inner.shape),
        own_extras[inner_n : inner_n + state_n].reshape(conv_state.shape),
        own_extras[small_count : small_count + 3 * heads].reshape(3, heads),
        own_extras[inner_n + state_n : small_count],
        grad_out.astype(F32).T,
    )
    weights = (
        input_gain,
        proj_inner,
        proj_step,
        proj_state,
        conv_inner,
        conv_state,
        head_params,
        mixer_gain,
        proj_output,
    )
    large = (1, 2, 3, 8)
    grads = list(grads)
    updated = [None] * 9
    for at in range(9):
        decay = WEIGHT_DECAY if at in large else 0.0
        rate = LEARN_RATE if at in large else LEARN_SMALL
        if at == 1:
            grads[1], *updated[1] = adam_pair(
                lambda w, g, m, v: adamw_step(w, g, m, v, WEIGHT_DECAY, LEARN_RATE),
                grad_gate,
                grad_x,
                proj_inner,
                moments[1],
                moments[10],
            )
        else:
            updated[at] = adamw_step(
                weights[at], grads[at], moments[at], moments[9 + at], decay, rate
            )
    return (
        block_out,
        d_input,
        *grads,
        *[entry[0] for entry in updated],
        *[entry[1] for entry in updated],
        *[entry[2] for entry in updated],
    )


def weight_specs():
    return (
        P("fsdp"),
        P("fsdp", None, "tp"),
        P("fsdp", "tp"),
        P("fsdp", "tp"),
        P(None, ("tp", "fsdp")),
        P(None, ("tp", "fsdp")),
        P(None, "tp"),
        P(("tp", "fsdp")),
        P("tp", "fsdp"),
    )


def solution(mesh):
    rows = P(("fsdp", "tp"), None)
    return jax.shard_map(
        body,
        mesh=mesh,
        in_specs=(rows, rows, P("fsdp", None), P("fsdp")) + weight_specs() * 3,
        out_specs=(rows, rows) + weight_specs() * 4,
        check_vma=False,
    )
```

```python
import functools
import jax
import jax.numpy as jnp
from jax import lax
from jax.experimental import pallas as pl
from jax.experimental.layout import Layout, with_layout_constraint
from jax.experimental.pallas import tpu as pltpu
from jax.sharding import PartitionSpec as P

N = 128
Q = 256
LANE = 128
BLK = 128
SLOTS = 32
UNROLL = 10
LOG2E = 1.4426950408889634
F32 = jnp.float32
BF16 = jnp.bfloat16
VMEM_CAP = 56 << 20


def mm(left, right):
    return lax.dot_general(left, right, (((1,), (0,)), ((), ())), preferred_element_type=F32)


def mm_nt(left, right):
    return lax.dot_general(left, right, (((1,), (1,)), ((), ())), preferred_element_type=F32)


def split_two(value):
    high = value.astype(BF16)
    low = (value - high.astype(F32)).astype(BF16)
    return high, low


def split_three(value):
    high = value.astype(BF16).astype(F32)
    rest = value - high
    mid = rest.astype(BF16).astype(F32)
    return high, mid, rest - mid


def as_columns(value):
    parts = split_three(value)
    stacked = jnp.concatenate(list(parts) + [jnp.zeros_like(value)], axis=0)
    return stacked.T.astype(BF16)


def lane_sums(value, table):
    parts = jnp.concatenate(split_three(value), axis=0).astype(BF16)
    sums = mm(parts, table)
    return sums[:SLOTS] + sums[SLOTS : 2 * SLOTS] + sums[2 * SLOTS :]


def iota2(shape, axis):
    return lax.broadcasted_iota(jnp.int32, shape, axis)


def step_terms(small_ref, meta_ref, hp_ref):
    on = hp_ref[:, 2:3]
    pre = (small_ref[...] + hp_ref[:, 0:1]) * on
    steps = (jnp.maximum(pre, 0.0) + jnp.log1p(jnp.exp(-jnp.abs(pre)))) * on
    upto = (iota2((Q, Q), 0) <= iota2((Q, Q), 1)).astype(BF16)
    cum = lane_sums(steps * hp_ref[:, 1:2], upto) * LOG2E
    into = jnp.exp2(cum) * meta_ref[0, 1:2, :] * on
    tail = jnp.exp2(cum[:, Q - 1 : Q] - cum) * meta_ref[0, 2:3, :] * on
    return pre, steps, cum, into, tail


def ssd_fwd_kernel(
    heads,
    raw_ref,
    small_ref,
    bc_ref,
    masks_ref,
    meta_ref,
    seg_ref,
    taps_ref,
    hp_ref,
    skip_ref,
    expand_ref,
    widen_ref,
    y_ref,
    st_ref,
    state,
    tail_rows,
    window,
    row_cum,
    scores,
    columns,
    spreads,
    wide_cum,
):
    chunk = pl.program_id(0)

    @pl.when(chunk == 0)
    def _():
        state[...] = jnp.zeros_like(state)
        tail_rows[...] = jnp.zeros_like(tail_rows)

    st_ref[0] = state[...]
    _, steps, cum, into, tail = step_terms(small_ref, meta_ref, hp_ref)
    row_cum[...] = cum
    for at, value in enumerate((cum, steps, into, tail)):
        columns[at] = as_columns(value)
    for at in range(3):
        spreads[at] = mm(columns[at + 1], expand_ref[...])
    cum_cols = jnp.concatenate([cum] * 4, axis=0).T
    for head in range(heads):
        wide_cum[:, head * LANE : (head + 1) * LANE] = jnp.broadcast_to(
            cum_cols[:, head : head + 1], (Q, LANE)
        )
    same = (seg_ref[:, 0:1] == meta_ref[0, 0:1, :]) & (iota2((Q, Q), 0) >= iota2((Q, Q), 1))
    b_turned = bc_ref[:N, :]
    c_rows = bc_ref[N:, :].astype(F32).T.astype(BF16)
    scores[...] = jnp.where(same, mm(c_rows, b_turned), 0.0)
    first = iota2((Q, LANE), 1) < LANE // 2

    def pair(index, _):
        lanes = pl.ds(pl.multiple_of(index * LANE, LANE), LANE)
        both = pl.ds(pl.multiple_of(index * 2 * LANE, 2 * LANE), 2 * LANE)
        window[0:8, :] = tail_rows[:, lanes]
        current = raw_ref[:, lanes]
        window[8 : 8 + Q, :] = current
        conv = taps_ref[4:5, lanes] + taps_ref[3:4, lanes] * current
        for offset in range(1, 4):
            conv = conv + taps_ref[3 - offset : 4 - offset, lanes] * (
                masks_ref[:, (offset - 1) * LANE : offset * LANE]
                * window[8 - offset : 8 - offset + Q, :]
            )
        vals = conv * jax.nn.sigmoid(conv)
        scaled = (vals * spreads[0, :, lanes]).astype(BF16)
        zero = jnp.zeros_like(scaled)
        own = (jnp.where(first, scaled, zero), jnp.where(first, zero, scaled))
        held = state[:, lanes]
        into_here = spreads[1, :, lanes]
        base = into_here * mm(c_rows, held.astype(BF16)) + skip_ref[0:1, lanes] * vals
        cum_cols = wide_cum[:, both]
        for low in range(0, Q, BLK):
            width = low + BLK
            total = base[low:width, :]
            for which in range(2):
                across = row_cum[pl.ds(index * 2 + which, 1), :][:, :width]
                down = cum_cols[low:width, which * LANE : (which + 1) * LANE]
                down = jnp.concatenate([down] * (width // LANE), axis=1)
                decays = jnp.exp2(jnp.minimum(down - across, 0.0))
                mixing = (decays * scores[low:width, :width]).astype(BF16)
                total = total + mm(mixing, own[which][:width, :])
            y_ref[low:width, lanes] = total
        weighted = (spreads[2, :, lanes] * scaled.astype(F32)).astype(BF16)
        state[:, lanes] = held * into_here[Q - 1 : Q, :] + mm(b_turned, weighted)
        return 0

    lax.fori_loop(0, heads // 2, pair, 0, unroll=UNROLL)
    tail_rows[...] = raw_ref[Q - 8 : Q, :]


def ssd_bwd_kernel(
    heads,
    raw_ref,
    halo_ref,
    small_ref,
    bc_ref,
    masks_ref,
    masks_next_ref,
    meta_ref,
    seg_ref,
    taps_ref,
    hp_ref,
    skip_ref,
    expand_ref,
    widen_ref,
    gather_ref,
    y_ref,
    dy_ref,
    st_ref,
    dx_ref,
    ddt_ref,
    dbc_ref,
    dtaps_ref,
    dhp_ref,
    dskip_ref,
    dstate,
    next_rows,
    carried,
    window,
    dwindow,
    row_cum,
    scores,
    dscores,
    columns,
    into_dy,
    tail_vals,
    balance_parts,
    direct_parts,
    wide_cum,
):
    chunk = pl.program_id(0)

    @pl.when(chunk == 0)
    def _():
        dstate[...] = jnp.zeros_like(dstate)
        next_rows[...] = jnp.zeros_like(next_rows)
        carried[...] = jnp.zeros_like(carried)
        dtaps_ref[...] = jnp.zeros_like(dtaps_ref)
        dhp_ref[...] = jnp.zeros_like(dhp_ref)
        dskip_ref[...] = jnp.zeros_like(dskip_ref)

    pre, steps, cum, into, tail = step_terms(small_ref, meta_ref, hp_ref)
    row_cum[...] = cum
    for at, value in enumerate((cum, steps, into, tail)):
        columns[at] = as_columns(value)
    cum_cols = jnp.concatenate([cum] * 4, axis=0).T
    for head in range(heads):
        wide_cum[:, head * LANE : (head + 1) * LANE] = jnp.broadcast_to(
            cum_cols[:, head : head + 1], (Q, LANE)
        )
    same = (seg_ref[:, 0:1] == meta_ref[0, 0:1, :]) & (iota2((Q, Q), 0) <= iota2((Q, Q), 1))
    b_rows = bc_ref[:N, :].astype(F32).T.astype(BF16)
    c_turned = bc_ref[N:, :]
    scores[...] = jnp.where(same, mm(b_rows, c_turned), 0.0)
    dscores[...] = jnp.zeros_like(dscores)
    carry_high, carry_low = split_two(carried[...])
    gather_all = gather_ref[...]
    from_next = mm(carry_high, gather_all) + mm(carry_low, gather_all)
    dstate_half = dstate[...].astype(BF16)
    first = iota2((Q, LANE), 1) < LANE // 2

    def pair(index, _):
        lanes = pl.ds(pl.multiple_of(index * LANE, LANE), LANE)
        both = pl.ds(pl.multiple_of(index * 2 * LANE, 2 * LANE), 2 * LANE)
        window[0:8, :] = halo_ref[:, lanes]
        current = raw_ref[:, lanes]
        window[8 : 8 + Q, :] = current
        conv = taps_ref[4:5, lanes] + taps_ref[3:4, lanes] * current
        for offset in range(1, 4):
            conv = conv + taps_ref[3 - offset : 4 - offset, lanes] * (
                masks_ref[:, (offset - 1) * LANE : offset * LANE]
                * window[8 - offset : 8 - offset + Q, :]
            )
        gate = jax.nn.sigmoid(conv)
        vals = conv * gate
        expand = expand_ref[:, lanes]
        step_here = mm(columns[1], expand)
        scaled = (vals * step_here).astype(BF16)
        skip = skip_ref[0:1, lanes]
        dy = dy_ref[:, lanes]
        dy_half = dy.astype(BF16)
        zero = jnp.zeros_like(scaled)
        own = (jnp.where(first, scaled, zero), jnp.where(first, zero, scaled))
        own_dy = (jnp.where(first, dy_half, zero), jnp.where(first, zero, dy_half))
        dheld = dstate[:, lanes]
        tail_here = mm(columns[3], expand)
        into_here = mm(columns[2], expand)
        base = tail_here * mm(b_rows, dheld.astype(BF16))
        cum_cols = wide_cum[:, both]
        pieces = []
        for low in range(0, Q, BLK):
            high = low + BLK
            total = base[low:high, :]
            for which in range(2):
                across = row_cum[pl.ds(index * 2 + which, 1), :][:, low:]
                down = cum_cols[low:high, which * LANE : (which + 1) * LANE]
                down = jnp.concatenate([down] * ((Q - low) // LANE), axis=1)
                decays = jnp.exp2(jnp.minimum(across - down, 0.0))
                mixing = (decays * scores[low:high, low:]).astype(BF16)
                total = total + mm(mixing, own_dy[which][low:, :])
                dmix = mm_nt(own[which][low:high, :], dy_half[low:, :])
                dscores[low:high, low:] += dmix * decays
            pieces.append(total)
        dscaled = jnp.concatenate(pieces, axis=0)
        held = st_ref[0, :, lanes]
        edy = (into_here * dy).astype(BF16)
        scaled_f = scaled.astype(F32)
        into_dy[:, lanes] = edy
        tail_vals[:, lanes] = (tail_here * scaled_f).astype(BF16)
        balance = dy_half.astype(F32) * (y_ref[:, lanes] - skip * vals) - scaled_f * dscaled
        part_high, part_low = split_two(balance)
        balance_parts[0, :, lanes] = part_high
        balance_parts[1, :, lanes] = part_low
        part_high, part_low = split_two(vals * dscaled)
        direct_parts[0, :, lanes] = part_high
        direct_parts[1, :, lanes] = part_low
        dskip_ref[0:1, lanes] += jnp.sum(dy * vals, axis=0, keepdims=True)
        dheld_new = into_here[Q - 1 : Q, :] * dheld + mm(c_turned, edy)
        dstate[:, lanes] = dheld_new
        carried[0:1, lanes] = jnp.sum(dheld_new * held, axis=0, keepdims=True)
        dvals = step_here * dscaled + skip * dy
        dconv = dvals * (gate * (1.0 + conv * (1.0 - gate)))
        dwindow[0:Q, :] = dconv
        dwindow[Q : Q + 8, :] = next_rows[:, lanes]
        next_rows[:, lanes] = dconv[0:8, :]
        dtaps_ref[4:5, lanes] += jnp.sum(dconv, axis=0, keepdims=True)
        dtaps_ref[3:4, lanes] += jnp.sum(dconv * current, axis=0, keepdims=True)
        draw = taps_ref[3:4, lanes] * dconv
        for offset in range(1, 4):
            mask = masks_ref[:, (offset - 1) * LANE : offset * LANE]
            mask_next = masks_next_ref[:, (offset - 1) * LANE : offset * LANE]
            mask_later = jnp.concatenate([mask, mask_next], axis=0)[offset : offset + Q, :]
            shifted = mask * window[8 - offset : 8 - offset + Q, :]
            dtaps_ref[3 - offset : 4 - offset, lanes] += jnp.sum(
                dconv * shifted, axis=0, keepdims=True
            )
            draw = draw + taps_ref[3 - offset : 4 - offset, lanes] * (
                mask_later * dwindow[offset : offset + Q, :]
            )
        dx_ref[:, lanes] = draw.astype(BF16)
        return 0

    lax.fori_loop(0, heads // 2, pair, 0, unroll=UNROLL)
    dscores_now = jnp.where(same, dscores[...], 0.0)
    d_b = mm_nt(tail_vals[...], dstate_half) + mm_nt(dscores_now.astype(BF16), c_turned)
    d_c = mm_nt(into_dy[...], st_ref[0].astype(BF16)) + mm(dscores_now.T.astype(BF16), b_rows)
    dbc_ref[:N, :] = d_b.T
    dbc_ref[N:, :] = d_c.T
    balance = mm(balance_parts[0], gather_all) + mm(balance_parts[1], gather_all)
    balance = balance + jnp.where(iota2((Q, LANE), 0) == Q - 1, from_next[0:1, :], 0.0)
    direct = mm(direct_parts[0], gather_all) + mm(direct_parts[1], gather_all)
    since = (iota2((Q, Q), 0) >= iota2((Q, Q), 1)).astype(BF16)
    dlogs = lane_sums(balance.T[:SLOTS], since)
    dsteps = dlogs * hp_ref[:, 1:2] + direct.T[:SLOTS]
    dsteps = dsteps * jax.nn.sigmoid(pre) * hp_ref[:, 2:3]
    ddt_ref[...] = dsteps
    dhp_ref[:, 0:1] += jnp.sum(dsteps, axis=1, keepdims=True)
    dhp_ref[:, 1:2] += jnp.sum(dlogs * steps, axis=1, keepdims=True)


def head_tables(heads):
    width = heads * (LANE // 2)
    owner = jnp.arange(width) // (LANE // 2)
    wide_owner = jnp.arange(heads * LANE) // LANE
    slot = jnp.arange(LANE)
    real = (slot < 3 * SLOTS)[:, None]
    expand = ((slot % SLOTS)[:, None] == owner[None, :]) & real
    widen = ((slot % SLOTS)[:, None] == wide_owner[None, :]) & real
    gather = owner[:, None] == slot[None, :]
    return expand.astype(BF16), widen.astype(BF16), gather.astype(BF16)


def segment_tables(segment):
    length = segment.shape[0]
    chunks = length // Q
    doc_masks = []
    for offset in range(1, 4):
        earlier = jnp.concatenate(
            [jnp.full((offset,), -1, jnp.int32), segment[: length - offset]], axis=0
        )
        doc_masks.append((earlier == segment).astype(F32))
    masks = jnp.concatenate(
        [jnp.broadcast_to(mask[:, None], (length, LANE)) for mask in doc_masks], axis=1
    )
    by_chunk = segment.reshape(chunks, Q)
    last = by_chunk[:, Q - 1]
    before = jnp.concatenate([jnp.full((1,), -1, jnp.int32), last[: chunks - 1]], axis=0)
    rows = [
        by_chunk.astype(F32),
        (by_chunk == before[:, None]).astype(F32),
        (by_chunk == last[:, None]).astype(F32),
    ]
    meta = jnp.pad(jnp.stack(rows, axis=1), ((0, 0), (0, 5), (0, 0)))
    seg_cols = jnp.broadcast_to(segment.astype(F32)[:, None], (length, LANE))
    return doc_masks, masks, meta, seg_cols


def head_columns(head_params):
    heads = head_params.shape[1]
    rates = -jnp.exp(head_params[1])
    table = jnp.stack([head_params[0], rates, jnp.ones_like(rates)], axis=1)
    return jnp.pad(table, ((0, SLOTS - heads), (0, LANE - 3)))


def time_like(seconds):
    return pl.CostEstimate(
        flops=int(seconds * 1.1e15), bytes_accessed=int(seconds * 3.4e12), transcendentals=0
    )


def full_spec(shape):
    return pl.BlockSpec(shape, lambda c: (0,) * len(shape))


def ssd_forward(raw, small, bc, tables, taps, hp, skip, spread, heads):
    length = raw.shape[0]
    width = heads * (LANE // 2)
    chunks = length // Q
    _, masks, meta, seg_cols = tables
    expand, widen, _ = spread
    return pl.pallas_call(
        functools.partial(ssd_fwd_kernel, heads),
        grid=(chunks,),
        out_shape=(
            jax.ShapeDtypeStruct((length, width), F32),
            jax.ShapeDtypeStruct((chunks, N, width), F32),
        ),
        in_specs=[
            pl.BlockSpec((Q, width), lambda c: (c, 0)),
            pl.BlockSpec((SLOTS, Q), lambda c: (0, c)),
            pl.BlockSpec((2 * N, Q), lambda c: (0, c)),
            pl.BlockSpec((Q, 3 * LANE), lambda c: (c, 0)),
            pl.BlockSpec((1, 8, Q), lambda c: (c, 0, 0)),
            pl.BlockSpec((Q, LANE), lambda c: (c, 0)),
            full_spec((8, width)),
            full_spec((SLOTS, LANE)),
            full_spec((8, width)),
            full_spec((LANE, width)),
            full_spec((LANE, heads * LANE)),
        ],
        out_specs=(
            pl.BlockSpec((Q, width), lambda c: (c, 0)),
            pl.BlockSpec((1, N, width), lambda c: (c, 0, 0)),
        ),
        scratch_shapes=[
            pltpu.VMEM((N, width), F32),
            pltpu.VMEM((8, width), F32),
            pltpu.VMEM((Q + 8, LANE), F32),
            pltpu.VMEM((SLOTS, Q), F32),
            pltpu.VMEM((Q, Q), F32),
            pltpu.VMEM((4, Q, LANE), BF16),
            pltpu.VMEM((3, Q, width), F32),
            pltpu.VMEM((Q, heads * LANE), F32),
        ],
        compiler_params=pltpu.CompilerParams(vmem_limit_bytes=VMEM_CAP),
        cost_estimate=time_like(37e-6 * length * heads / 30720),
        name="ssd_fwd",
    )(raw, small, bc, masks, meta, seg_cols, taps, hp, skip, expand, widen)


def ssd_backward(raw, small, bc, tables, taps, hp, skip, spread, y, dy, states, heads):
    length = raw.shape[0]
    width = heads * (LANE // 2)
    chunks = length // Q
    per = Q // 8
    _, masks, meta, seg_cols = tables

    def at(c):
        return chunks - 1 - c

    return pl.pallas_call(
        functools.partial(ssd_bwd_kernel, heads),
        grid=(chunks,),
        out_shape=(
            jax.ShapeDtypeStruct((length, width), BF16),
            jax.ShapeDtypeStruct((SLOTS, length), F32),
            jax.ShapeDtypeStruct((2 * N, length), F32),
            jax.ShapeDtypeStruct((8, width), F32),
            jax.ShapeDtypeStruct((SLOTS, LANE), F32),
            jax.ShapeDtypeStruct((8, width), F32),
        ),
        in_specs=[
            pl.BlockSpec((Q, width), lambda c: (at(c), 0)),
            pl.BlockSpec((8, width), lambda c: (jnp.maximum(at(c) * per - 1, 0), 0)),
            pl.BlockSpec((SLOTS, Q), lambda c: (0, at(c))),
            pl.BlockSpec((2 * N, Q), lambda c: (0, at(c))),
            pl.BlockSpec((Q, 3 * LANE), lambda c: (at(c), 0)),
            pl.BlockSpec(
                (8, 3 * LANE), lambda c: (jnp.minimum((at(c) + 1) * per, chunks * per - 1), 0)
            ),
            pl.BlockSpec((1, 8, Q), lambda c: (at(c), 0, 0)),
            pl.BlockSpec((Q, LANE), lambda c: (at(c), 0)),
            full_spec((8, width)),
            full_spec((SLOTS, LANE)),
            full_spec((8, width)),
            full_spec((LANE, width)),
            full_spec((LANE, heads * LANE)),
            full_spec((width, LANE)),
            pl.BlockSpec((Q, width), lambda c: (at(c), 0)),
            pl.BlockSpec((Q, width), lambda c: (at(c), 0)),
            pl.BlockSpec((1, N, width), lambda c: (at(c), 0, 0)),
        ],
        out_specs=(
            pl.BlockSpec((Q, width), lambda c: (at(c), 0)),
            pl.BlockSpec((SLOTS, Q), lambda c: (0, at(c))),
            pl.BlockSpec((2 * N, Q), lambda c: (0, at(c))),
            full_spec((8, width)),
            full_spec((SLOTS, LANE)),
            full_spec((8, width)),
        ),
        scratch_shapes=[
            pltpu.VMEM((N, width), F32),
            pltpu.VMEM((8, width), F32),
            pltpu.VMEM((8, width), F32),
            pltpu.VMEM((Q + 8, LANE), F32),
            pltpu.VMEM((Q + 8, LANE), F32),
            pltpu.VMEM((SLOTS, Q), F32),
            pltpu.VMEM((Q, Q), F32),
            pltpu.VMEM((Q, Q), F32),
            pltpu.VMEM((4, Q, LANE), BF16),
            pltpu.VMEM((Q, width), BF16),
            pltpu.VMEM((Q, width), BF16),
            pltpu.VMEM((2, Q, width), BF16),
            pltpu.VMEM((2, Q, width), BF16),
            pltpu.VMEM((Q, heads * LANE), F32),
        ],
        compiler_params=pltpu.CompilerParams(vmem_limit_bytes=VMEM_CAP),
        cost_estimate=time_like(69e-6 * length * heads / 30720),
        name="ssd_bwd",
    )(
        raw,
        raw,
        small,
        bc,
        masks,
        masks,
        meta,
        seg_cols,
        taps,
        hp,
        skip,
        *spread,
        y,
        dy,
        states,
    )


def dn_kernel(count, rows, at_ref, *refs):
    dz, dx, side, normed = (refs[k * count : (k + 1) * count] for k in range(4))
    gate_ref, inner_ref, out_ref, sums_ref = refs[4 * count : 4 * count + 4]
    turned = refs[4 * count + 4]
    width = dz[0].shape[1]

    @pl.when(pl.program_id(0) == 0)
    def _():
        for k in range(count):
            turned[k * rows : (k + 1) * rows, :] = side[k][...].T.astype(BF16)

    gate = gate_ref[...]
    inner = inner_ref[:, :width]
    last = inner_ref[:, width:]
    sums = None
    for k in range(count):
        at = slice(k * rows, (k + 1) * rows)
        total = mm_nt(dz[k][...], gate) + mm_nt(dx[k][...], inner) + mm_nt(turned[at, :], last)
        out_ref[at, :] = total.astype(BF16)
        part = jnp.sum(total * normed[k][...].astype(F32), axis=0, keepdims=True)
        sums = part if sums is None else sums + part
    sums_ref[0:1, :] = sums


def d_normed_blocks(d_z, d_x, d_side, gate_all, x_all, normed, blocks, which, rows, tile=256):
    length, width = d_z.shape
    count = blocks.shape[0]
    half = gate_all.shape[0] // 2
    first = which * half // tile

    def rows_of(k):
        return pl.BlockSpec((rows, width), lambda n, at, k=k: (at[k], 0))

    def cols_of(k):
        return pl.BlockSpec((LANE, rows), lambda n, at, k=k: (0, at[k]))

    def tile_of(k):
        return pl.BlockSpec((rows, tile), lambda n, at, k=k: (at[k], n + first))

    each = range(count)
    return pl.pallas_call(
        functools.partial(dn_kernel, count, rows),
        grid_spec=pltpu.PrefetchScalarGridSpec(
            num_scalar_prefetch=1,
            grid=(half // tile,),
            in_specs=[rows_of(k) for k in each]
            + [rows_of(k) for k in each]
            + [cols_of(k) for k in each]
            + [tile_of(k) for k in each]
            + [
                pl.BlockSpec((tile, width), lambda n, at: (n + first, 0)),
                pl.BlockSpec((tile, width + LANE), lambda n, at: (n + first, 0)),
            ],
            out_specs=(
                pl.BlockSpec((count * rows, tile), lambda n, at: (0, n)),
                pl.BlockSpec((8, tile), lambda n, at: (0, n)),
            ),
            scratch_shapes=[pltpu.VMEM((count * rows, LANE), BF16)],
        ),
        out_shape=(
            jax.ShapeDtypeStruct((count * rows, half), BF16),
            jax.ShapeDtypeStruct((8, half), F32),
        ),
        compiler_params=pltpu.CompilerParams(vmem_limit_bytes=VMEM_CAP),
        cost_estimate=time_like(1e-7),
        name="d_normed",
    )(
        blocks,
        *([d_z] * count),
        *([d_x] * count),
        *([d_side] * count),
        *([normed] * count),
        gate_all,
        x_all,
    )


def adam_kernel(step, gate_ref, inner_ref, weight_ref, first_ref, second_ref, *outs):
    grad_out, weight_out, first_out, second_out = outs
    for part, grad_ref in ((0, gate_ref), (1, inner_ref)):
        grad = grad_ref[...].astype(F32)
        new_weight, new_first, new_second = step(
            weight_ref[:, part, :], grad, first_ref[:, part, :], second_ref[:, part, :]
        )
        grad_out[:, part, :] = grad
        weight_out[:, part, :] = new_weight
        first_out[:, part, :] = new_first
        second_out[:, part, :] = new_second


def adam_pair(step, grad_gate, grad_inner, weight, first, second, rows=40):
    shard, _, width = weight.shape
    deep = pl.BlockSpec((rows, 2, width), lambda n: (n, 0, 0))
    flat = pl.BlockSpec((rows, width), lambda n: (n, 0))
    like = jax.ShapeDtypeStruct(weight.shape, F32)
    return pl.pallas_call(
        functools.partial(adam_kernel, step),
        grid=(shard // rows,),
        out_shape=(like, jax.ShapeDtypeStruct(weight.shape, weight.dtype), like, like),
        in_specs=[flat, flat, deep, deep, deep],
        out_specs=(deep,) * 4,
        compiler_params=pltpu.CompilerParams(vmem_limit_bytes=VMEM_CAP),
        cost_estimate=pl.CostEstimate(flops=1000, bytes_accessed=1000, transcendentals=0),
        name="adam_pair",
    )(grad_gate, grad_inner, weight, first, second)

DI = 5120
STEP = 3
NORM_EPS = 1e-05
BETA_ONE = 0.9
BETA_TWO = 0.95
LEARN_RATE = 0.004
LEARN_SMALL = 0.15
WEIGHT_DECAY = 0.1
ADAM_EPS = 1e-08


def by_rows(value):
    return with_layout_constraint(value, Layout(major_to_minor=(0, 1)))


def silu_act(values):
    return values * jax.nn.sigmoid(values)


def later(row, offset):
    return jnp.pad(row, ((0, 0), (offset, 0)))[:, : row.shape[1]]


def state_act(raw_cols, conv_taps, doc_masks):
    conv = conv_taps[4][:, None] + conv_taps[3][:, None] * raw_cols
    for offset in range(1, 4):
        conv = conv + conv_taps[3 - offset][:, None] * (
            doc_masks[offset - 1][None, :] * later(raw_cols, offset)
        )
    return silu_act(conv)


def contract_rows(left_mat, right_mat):
    return lax.dot_general(
        left_mat, right_mat, (((0,), (0,)), ((), ())), preferred_element_type=F32
    )


def adamw_step(weight, gradient, first_moment, second_moment, decay_factor, learn_rate):
    new_first = BETA_ONE * first_moment + (1.0 - BETA_ONE) * gradient
    new_second = BETA_TWO * second_moment + (1.0 - BETA_TWO) * gradient * gradient
    first_hat = new_first / (1.0 - BETA_ONE**STEP)
    second_hat = new_second / (1.0 - BETA_TWO**STEP)
    weight_f = weight.astype(F32)
    updated = weight_f - learn_rate * (
        first_hat / (jnp.sqrt(second_hat) + ADAM_EPS) + decay_factor * weight_f
    )
    return (updated.astype(weight.dtype), new_first, new_second)


def swap(value, distance, size):
    return lax.ppermute(value, "tp", [(at, at ^ distance) for at in range(size)])


def tied(*values):
    return lax.optimization_barrier(values)


def gather_parts(value, size, near_done):
    if size != 4:
        one, *others = near_done(swap(value, 1, size))
        return [value, one] + [swap(value, k, size) for k in range(2, size)], *others
    half = value.shape[0] // 2
    one, two = swap(value, 1, size), swap(value, 2, size)
    one, *others = near_done(one)
    far = jnp.concatenate([swap(two[:half], 1, size), swap(one[half:], 2, size)], axis=0)
    return [value, one, two, far], *others


def scatter_start(left, right, rows, index, size):
    def block(value, distance):
        return lax.dynamic_slice_in_dim(value, (index ^ distance) * rows, rows, 0)

    sent, kept = [], []
    for half, near in ((left, 1), (right, 2)):
        if size == 4:
            pair = jnp.concatenate([block(half, 3), block(half, near)], axis=0)
            sent.append(swap(pair, near, size))
            kept.append((block(half, 3 - near), block(half, 0)))
        else:
            sent.append([swap(block(half, k), k, size) for k in range(1, size)])
            kept.append(block(half, 0))
    return sent, kept


def scatter_middle(sent, kept, rows, size):
    if size != 4:
        return sent, [(one,) for one in kept]
    passed = [
        (kept[at][0].astype(F32) + sent[at][:rows].astype(F32)).astype(BF16) for at in range(2)
    ]
    return passed, [(kept[at][1], sent[at][rows:]) for at in range(2)]


def scatter_last(passed, size):
    if size != 4:
        return passed[0] + passed[1]
    return [swap(passed[0], 2, size), swap(passed[1], 1, size)]


def scatter_end(own, last):
    each = len(last) // 2
    totals = []
    for at in range(2):
        total = own[at][0].astype(F32)
        for piece in own[at][1:]:
            total = total + piece.astype(F32)
        for piece in last[at * each : (at + 1) * each]:
            total = total + piece.astype(F32)
        totals.append(total)
    return jnp.concatenate(totals, axis=1)


def row_sum(value, size):
    total = value
    for distance in range(1, size):
        total = total + swap(value, distance, size)
    return total


def all_sum(value, size):
    distance = 1
    while distance < size:
        value = value + swap(value, distance, size)
        distance *= 2
    return value


def fsdp_swap(value, distance, size):
    return lax.ppermute(value, "fsdp", [(at, at ^ distance) for at in range(size)])


def gather_by_swaps(value, index, size):
    whole = jnp.zeros((size,) + value.shape, value.dtype)
    for distance in range(size):
        piece = value if distance == 0 else fsdp_swap(value, distance, size)
        whole = lax.dynamic_update_slice(whole, piece[None], (index ^ distance, jnp.int32(0)))
    return whole


def pair_sum(value, index, size):
    blocks = value.reshape(size // 2, 2, value.shape[0] // size, value.shape[1])
    core = index % 2
    away = lax.dynamic_slice_in_dim(blocks, 1 - core, 1, 1)[:, 0]
    own = lax.dynamic_slice_in_dim(blocks, core, 1, 1)[:, 0]
    return (own.astype(F32) + fsdp_swap(away, 1, size).astype(F32)).astype(value.dtype)


def chip_scatter(value, size):
    groups = [list(range(core, size, 2)) for core in range(2)]
    flat = value.reshape(value.shape[0] * value.shape[1], value.shape[2])
    return lax.psum_scatter(
        flat, "fsdp", scatter_dimension=0, axis_index_groups=groups, tiled=True
    )


def chip_sum(value, index, size):
    chip = index // 2

    def block(distance):
        return lax.dynamic_slice_in_dim(value, chip ^ distance, 1, 0)[0]

    total = block(0).astype(F32)
    for distance in range(1, size // 2):
        total = total + fsdp_swap(block(distance), 2 * distance, size).astype(F32)
    return total


def pad_cols(value, width):
    return jnp.pad(value, ((0, 0), (0, width - value.shape[1])))


def body(
    block_in,
    cotangent,
    segment_ids,
    group_fill,
    input_gain,
    proj_inner,
    proj_step,
    proj_state,
    conv_inner,
    conv_state,
    head_params,
    mixer_gain,
    proj_output,
    *moments,
):
    tp_size = lax.axis_size("tp")
    fsdp_size = lax.axis_size("fsdp")
    tp_index = lax.axis_index("tp")
    fsdp_index = lax.axis_index("fsdp")
    own_rows, model = block_in.shape
    group_rows = own_rows * tp_size
    shard, _, width = proj_inner.shape
    heads = proj_step.shape[1]
    state_cols = proj_state.shape[1]
    segment = segment_ids[0]
    filled = group_fill[0]

    small_values = jnp.concatenate(
        [conv_inner.reshape(-1), conv_state.reshape(-1), mixer_gain], axis=0
    )
    small_count = small_values.shape[0]
    inner_n, state_n = conv_inner.size, conv_state.size
    small_cols = -(-(small_count + 3 * heads) // shard)
    small_block = jnp.pad(small_values, (0, small_cols * shard - small_count)).reshape(
        shard, small_cols
    )
    used = heads + state_cols
    side = pad_cols(
        jnp.concatenate([proj_step, proj_state, input_gain[:, None], small_block], axis=1), LANE
    )
    (inner_halves,) = tied(proj_inner.transpose(1, 0, 2))
    x_local = jnp.concatenate([inner_halves[1], side], axis=1)
    x_all = lax.all_gather(x_local, "fsdp", axis=0, tiled=True)
    gate_all = lax.all_gather(inner_halves[0], "fsdp", axis=0, tiled=True)
    gain_all = lax.dynamic_update_slice(
        jnp.zeros((fsdp_size, shard), BF16), input_gain[None], (fsdp_index, jnp.int32(0))
    )
    distance = 1
    while distance < fsdp_size:
        gain_all = gain_all + fsdp_swap(gain_all, distance, fsdp_size)
        distance *= 2
    gain_f = gain_all.reshape(model).astype(F32)
    positions = tp_index * own_rows + jnp.arange(own_rows, dtype=jnp.int32)
    live_rows = (positions < filled)[:, None]
    block_f = block_in.astype(F32)
    cot_f = cotangent.astype(F32)
    own_grad = jnp.where(live_rows, cot_f, 0.0).astype(BF16)
    blank = jnp.zeros((group_rows, model), BF16)

    def unit_of(rows):
        rows_f = rows.astype(F32)
        scale = lax.rsqrt(jnp.mean(rows_f * rows_f, axis=1, keepdims=True) + NORM_EPS)
        return rows_f * scale, scale

    def normed_of(rows):
        return (unit_of(rows)[0] * gain_f[None, :]).astype(BF16)

    def put(whole, part, distance):
        return lax.dynamic_update_slice(
            whole, part, ((tp_index ^ distance) * own_rows, jnp.int32(0))
        )

    started = put(blank, normed_of(block_in), 0)

    def near_done(one):
        return tied(one, started, own_grad)

    row_parts, started, own_grad = gather_parts(block_in, tp_size, near_done)
    row_parts = [by_rows(part) for part in row_parts]
    own_grad, *row_parts = tied(own_grad, *row_parts)
    near = min(3, tp_size)
    grad_parts = [by_rows(own_grad)] + [swap(own_grad, k, tp_size) for k in range(1, near)]

    side_all = x_all[:, width:]
    extras = side_all[:, used + 1 : used + 1 + small_cols].reshape(fsdp_size, shard * small_cols)

    def from_owners(flat, rows):
        return flat.reshape(fsdp_size, rows, -1).transpose(1, 0, 2).reshape(rows, -1).astype(F32)

    taps_inner = from_owners(extras[:, :inner_n], 5)
    taps_state = from_owners(extras[:, inner_n : inner_n + state_n], 5)
    mixer_f = from_owners(extras[:, inner_n + state_n : small_count], 1)[0]

    normed = started
    for distance in range(1, tp_size - 1):
        normed = put(normed, normed_of(row_parts[distance]), distance)
    far_rows, normed = tied(row_parts[-1], normed)
    normed = by_rows(put(normed, normed_of(far_rows), tp_size - 1))
    small = lax.dot_general(
        side_all, normed, (((0,), (1,)), ((), ())), preferred_element_type=F32
    )
    raw = mm(normed, x_all)
    tables = segment_tables(segment)
    doc_masks = tables[0]
    state_vals, state_back = jax.vjp(
        lambda raw_cols, conv_taps: state_act(raw_cols, conv_taps, doc_masks),
        small[heads:used],
        taps_state,
    )
    state_local = state_vals.astype(BF16)
    bc = jnp.zeros((tp_size * state_cols, group_rows), BF16)
    for k in range(tp_size):
        piece = state_local if k == 0 else swap(state_local, k, tp_size)
        bc = lax.dynamic_update_slice(bc, piece, ((tp_index ^ k) * state_cols, jnp.int32(0)))
    own_grad, bc, out_local = tied(own_grad, bc, proj_output.T)
    out_all = lax.all_gather(out_local, "fsdp", axis=0, tiled=True)
    grad_parts += [swap(own_grad, k, tp_size) for k in range(near, tp_size)]
    spread = head_tables(heads)
    taps8 = jnp.pad(taps_inner, ((0, 3), (0, 0)))
    hp8 = head_columns(head_params)
    skip8 = jnp.broadcast_to(jnp.repeat(head_params[2], LANE // 2)[None, :], (8, width))
    mixed, states = ssd_forward(raw, small, bc, tables, taps8, hp8, skip8, spread, heads)

    z_raw = mm(normed, gate_all)
    sig = jax.nn.sigmoid(z_raw)
    gate_act = z_raw * sig
    gated = mixed * gate_act
    square_sum, *grad_parts = tied(jnp.sum(gated * gated, axis=1), *grad_parts)
    square_sum = row_sum(square_sum, tp_size)
    group_grad = jnp.zeros((group_rows, model), BF16)
    for distance in range(tp_size):
        group_grad = put(group_grad, grad_parts[distance], distance)
    group_grad = by_rows(group_grad)
    inv_gate = lax.rsqrt(square_sum / DI + NORM_EPS)[:, None]
    unit_gated = gated * inv_gate
    normed_gated = (unit_gated * mixer_f[None, :]).astype(BF16)
    sum_out = pair_sum(
        contract_rows(group_grad, normed_gated).astype(BF16), fsdp_index, fsdp_size
    )
    half = model // 2
    mixed_halves = [mm_nt(normed_gated, out_all[:half])]
    normed_gated, sum_out = tied(normed_gated, sum_out)
    grad_out = chip_scatter(sum_out, fsdp_size)
    mixed_halves.append(mm_nt(normed_gated, out_all[half:]))
    inner_sum = jnp.sum(mixed_halves[0] * group_grad[:, :half].astype(F32), axis=1) + jnp.sum(
        mixed_halves[1] * group_grad[:, half:].astype(F32), axis=1
    )
    inner_sum = row_sum(inner_sum, tp_size)
    mixed_left, mixed_right = (part.astype(BF16) for part in mixed_halves)
    mixed_sent, mixed_kept = scatter_start(mixed_left, mixed_right, own_rows, tp_index, tp_size)

    inner_mean = inner_sum[:, None] / DI
    d_ng = mm(group_grad, out_all)
    grad_mixer = jnp.sum(d_ng * unit_gated, axis=0)
    d_gated = inv_gate * (d_ng * mixer_f[None, :] - unit_gated * inner_mean)
    d_mixed = d_gated * gate_act
    d_z = (d_gated * mixed * sig * (1.0 + z_raw * (1.0 - sig))).astype(BF16)
    part_gate, mixed_sent = tied(contract_rows(normed, d_z).astype(BF16), mixed_sent)
    sum_gate = pair_sum(part_gate, fsdp_index, fsdp_size)
    mixed_passed, mixed_kept = scatter_middle(mixed_sent, mixed_kept, own_rows, tp_size)
    sum_gate, grad_out = tied(sum_gate, grad_out)

    d_mixed, sum_gate, mixed_passed = tied(d_mixed, sum_gate, mixed_passed)
    mixed_last = scatter_last(mixed_passed, tp_size)
    grad_gate = chip_scatter(sum_gate, fsdp_size)
    d_x, d_dt, d_bc, d_taps, d_heads, d_skip = ssd_backward(
        raw, small, bc, tables, taps8, hp8, skip8, spread, mixed, d_mixed, states, heads
    )
    def state_block(distance):
        return lax.dynamic_slice_in_dim(d_bc, (tp_index ^ distance) * state_cols, state_cols, 0)

    state_parts = [state_block(0)]
    state_parts += [swap(state_block(k), k, tp_size) for k in range(1, tp_size)]
    part_x, mixed_last, grad_gate, *state_parts = tied(
        contract_rows(normed, d_x).astype(BF16), mixed_last, grad_gate, *state_parts
    )
    sum_x = pair_sum(part_x, fsdp_index, fsdp_size)

    d_state_raw, grad_conv_state = state_back(sum(state_parts[1:], state_parts[0]).astype(F32))
    d_side = jnp.concatenate([d_dt[:heads], d_state_raw], axis=0)
    d_side = jnp.pad(d_side, ((0, LANE - used), (0, 0)))

    four = tp_size == 4
    side_part = lax.dot_general(
        normed, d_side.astype(BF16), (((0,), (1,)), ((), ())), preferred_element_type=F32
    )

    def side_gradient(side_part, d_taps, d_skip, d_heads, grad_conv_state, gain_sums):
        grad_head = jnp.stack(
            [
                d_heads[:heads, 0],
                hp8[:heads, 1] * d_heads[:heads, 1],
                jnp.sum(d_skip[0].reshape(heads, LANE // 2), axis=1),
            ],
            axis=0,
        )

        def by_owner(value):
            rows = value.shape[0]
            return value.reshape(rows, fsdp_size, -1).transpose(1, 0, 2).reshape(fsdp_size, -1)

        grad_extras = jnp.concatenate(
            [
                by_owner(d_taps[:5]),
                by_owner(grad_conv_state),
                by_owner(grad_mixer[None, :]),
                jnp.broadcast_to(grad_head.reshape(1, -1), (fsdp_size, 3 * heads)),
            ],
            axis=1,
        )
        grad_extras = pad_cols(grad_extras, small_cols * shard).reshape(fsdp_size * shard, small_cols)
        grad_extras = jnp.concatenate([gain_sums[:, None], grad_extras], axis=1)
        side_part = side_part + jnp.pad(
            grad_extras, ((0, 0), (used, LANE - used - 1 - small_cols))
        )
        side_part = pair_sum(side_part, fsdp_index, fsdp_size)
        return chip_sum(side_part, fsdp_index, fsdp_size)

    def d_normed_of(distances, which):
        return d_normed_blocks(
            d_z, d_x, d_side, gate_all, x_all, normed, tp_index ^ jnp.array(distances), which, own_rows
        )

    if four:
        left_away, gains_one = d_normed_of([3, 1], 0)
        gains_one, sum_x = tied(gains_one, sum_x)
        right_away, gains_two = d_normed_of([3, 2], 1)
        gains_two, mixed_last, d_taps, d_skip, d_heads, grad_conv_state = tied(
            gains_two, mixed_last, d_taps, d_skip, d_heads, grad_conv_state
        )
        sent = [swap(left_away, 1, 4), swap(right_away, 2, 4)]
        left_kept, gains_three = d_normed_of([2, 0], 0)
        sent[0], d_side_late, side_part, grad_out = tied(sent[0], d_side, side_part, grad_out)
        right_kept, gains_four = d_normed_blocks(
            d_z, d_x, d_side_late, gate_all, x_all, normed, tp_index ^ jnp.array([1, 0]), 1, own_rows
        )
        kept = [
            (left_kept[:own_rows], left_kept[own_rows:]),
            (right_kept[:own_rows], right_kept[own_rows:]),
        ]
        gain_sums = jnp.concatenate([gains_one + gains_three, gains_two + gains_four], axis=1)[0]
    else:
        left, gains_one = d_normed_of(list(range(tp_size)), 0)
        right, gains_two = d_normed_of(list(range(tp_size)), 1)
        sent = [
            [
                swap(part[k * own_rows : (k + 1) * own_rows], k, tp_size)
                for k in range(1, tp_size)
            ]
            for part in (left, right)
        ]
        kept = [left[:own_rows], right[:own_rows]]
        gain_sums = jnp.concatenate([gains_one, gains_two], axis=1)[0]
    grad_x = chip_scatter(sum_x, fsdp_size)
    passed, kept = scatter_middle(sent, kept, own_rows, tp_size)
    passed, mixed_last = tied(passed, mixed_last)
    mixed_rows = scatter_end(mixed_kept, mixed_last)
    block_out = (block_f + jnp.where(live_rows, mixed_rows, 0.0)).astype(BF16)
    grad_x, passed = tied(grad_x, passed)
    last = scatter_last(passed, tp_size)
    grad_side = side_gradient(side_part, d_taps, d_skip, d_heads, grad_conv_state, gain_sums)
    grad_side, last[0] = tied(grad_side, last[0])
    grad_input_gain = all_sum(grad_side[:, used], tp_size) / input_gain.astype(F32)
    d_normed = scatter_end(kept, last)

    unit_rows, inv_rms = unit_of(block_in)
    scaled = d_normed * gain_f[None, :]
    d_block = inv_rms * (scaled - unit_rows * jnp.mean(scaled * unit_rows, axis=1, keepdims=True))
    d_input = (cot_f + d_block).astype(BF16)

    own_extras = grad_side[:, used + 1 : used + 1 + small_cols].reshape(-1)
    grads = (
        grad_input_gain,
        None,
        grad_side[:, :heads],
        grad_side[:, heads:used],
        own_extras[:inner_n].reshape(conv_inner.shape),
        own_extras[inner_n : inner_n + state_n].reshape(conv_state.shape),
        own_extras[small_count : small_count + 3 * heads].reshape(3, heads),
        own_extras[inner_n + state_n : small_count],
        grad_out.astype(F32).T,
    )
    weights = (
        input_gain,
        proj_inner,
        proj_step,
        proj_state,
        conv_inner,
        conv_state,
        head_params,
        mixer_gain,
        proj_output,
    )
    large = (1, 2, 3, 8)
    grads = list(grads)
    updated = [None] * 9
    for at in range(9):
        decay = WEIGHT_DECAY if at in large else 0.0
        rate = LEARN_RATE if at in large else LEARN_SMALL
        if at == 1:
            grads[1], *updated[1] = adam_pair(
                lambda w, g, m, v: adamw_step(w, g, m, v, WEIGHT_DECAY, LEARN_RATE),
                grad_gate,
                grad_x,
                proj_inner,
                moments[1],
                moments[10],
            )
        else:
            updated[at] = adamw_step(
                weights[at], grads[at], moments[at], moments[9 + at], decay, rate
            )
    return (
        block_out,
        d_input,
        *grads,
        *[entry[0] for entry in updated],
        *[entry[1] for entry in updated],
        *[entry[2] for entry in updated],
    )


def weight_specs():
    return (
        P("fsdp"),
        P("fsdp", None, "tp"),
        P("fsdp", "tp"),
        P("fsdp", "tp"),
        P(None, ("tp", "fsdp")),
        P(None, ("tp", "fsdp")),
        P(None, "tp"),
        P(("tp", "fsdp")),
        P("tp", "fsdp"),
    )


def solution(mesh):
    rows = P(("fsdp", "tp"), None)
    return jax.shard_map(
        body,
        mesh=mesh,
        in_specs=(rows, rows, P("fsdp", None), P("fsdp")) + weight_specs() * 3,
        out_specs=(rows, rows) + weight_specs() * 4,
        check_vma=False,
    )
```

```python
import functools
import jax
import jax.numpy as jnp
from jax import lax
from jax.experimental import pallas as pl
from jax.experimental.layout import Layout, with_layout_constraint
from jax.experimental.pallas import tpu as pltpu
from jax.sharding import PartitionSpec as P

N = 128
Q = 256
LANE = 128
BLK = 128
SLOTS = 32
UNROLL = 10
LOG2E = 1.4426950408889634
F32 = jnp.float32
BF16 = jnp.bfloat16
VMEM_CAP = 56 << 20


def mm(left, right):
    return lax.dot_general(left, right, (((1,), (0,)), ((), ())), preferred_element_type=F32)


def mm_nt(left, right):
    return lax.dot_general(left, right, (((1,), (1,)), ((), ())), preferred_element_type=F32)


def split_two(value):
    high = value.astype(BF16)
    low = (value - high.astype(F32)).astype(BF16)
    return high, low


def split_three(value):
    high = value.astype(BF16).astype(F32)
    rest = value - high
    mid = rest.astype(BF16).astype(F32)
    return high, mid, rest - mid


def as_columns(value):
    parts = split_three(value)
    stacked = jnp.concatenate(list(parts) + [jnp.zeros_like(value)], axis=0)
    return stacked.T.astype(BF16)


def lane_sums(value, table):
    parts = jnp.concatenate(split_three(value), axis=0).astype(BF16)
    sums = mm(parts, table)
    return sums[:SLOTS] + sums[SLOTS : 2 * SLOTS] + sums[2 * SLOTS :]


def iota2(shape, axis):
    return lax.broadcasted_iota(jnp.int32, shape, axis)


def step_terms(small_ref, meta_ref, hp_ref):
    on = hp_ref[:, 2:3]
    pre = (small_ref[...] + hp_ref[:, 0:1]) * on
    steps = (jnp.maximum(pre, 0.0) + jnp.log1p(jnp.exp(-jnp.abs(pre)))) * on
    upto = (iota2((Q, Q), 0) <= iota2((Q, Q), 1)).astype(BF16)
    cum = lane_sums(steps * hp_ref[:, 1:2], upto) * LOG2E
    into = jnp.exp2(cum) * meta_ref[0, 1:2, :] * on
    tail = jnp.exp2(cum[:, Q - 1 : Q] - cum) * meta_ref[0, 2:3, :] * on
    return pre, steps, cum, into, tail


def ssd_fwd_kernel(
    heads,
    raw_ref,
    small_ref,
    bc_ref,
    masks_ref,
    meta_ref,
    seg_ref,
    taps_ref,
    hp_ref,
    skip_ref,
    expand_ref,
    widen_ref,
    y_ref,
    st_ref,
    state,
    tail_rows,
    window,
    row_cum,
    scores,
    columns,
    spreads,
    wide_cum,
):
    chunk = pl.program_id(0)

    @pl.when(chunk == 0)
    def _():
        state[...] = jnp.zeros_like(state)
        tail_rows[...] = jnp.zeros_like(tail_rows)

    st_ref[0] = state[...]
    _, steps, cum, into, tail = step_terms(small_ref, meta_ref, hp_ref)
    row_cum[...] = cum
    for at, value in enumerate((cum, steps, into, tail)):
        columns[at] = as_columns(value)
    for at in range(3):
        spreads[at] = mm(columns[at + 1], expand_ref[...])
    cum_cols = jnp.concatenate([cum] * 4, axis=0).T
    for head in range(heads):
        wide_cum[:, head * LANE : (head + 1) * LANE] = jnp.broadcast_to(
            cum_cols[:, head : head + 1], (Q, LANE)
        )
    same = (seg_ref[:, 0:1] == meta_ref[0, 0:1, :]) & (iota2((Q, Q), 0) >= iota2((Q, Q), 1))
    b_turned = bc_ref[:N, :]
    c_rows = bc_ref[N:, :].astype(F32).T.astype(BF16)
    scores[...] = jnp.where(same, mm(c_rows, b_turned), 0.0)
    first = iota2((Q, LANE), 1) < LANE // 2

    def pair(index, _):
        lanes = pl.ds(pl.multiple_of(index * LANE, LANE), LANE)
        both = pl.ds(pl.multiple_of(index * 2 * LANE, 2 * LANE), 2 * LANE)
        window[0:8, :] = tail_rows[:, lanes]
        current = raw_ref[:, lanes]
        window[8 : 8 + Q, :] = current
        conv = taps_ref[4:5, lanes] + taps_ref[3:4, lanes] * current
        for offset in range(1, 4):
            conv = conv + taps_ref[3 - offset : 4 - offset, lanes] * (
                masks_ref[:, (offset - 1) * LANE : offset * LANE]
                * window[8 - offset : 8 - offset + Q, :]
            )
        vals = conv * jax.nn.sigmoid(conv)
        scaled = (vals * spreads[0, :, lanes]).astype(BF16)
        zero = jnp.zeros_like(scaled)
        own = (jnp.where(first, scaled, zero), jnp.where(first, zero, scaled))
        held = state[:, lanes]
        into_here = spreads[1, :, lanes]
        base = into_here * mm(c_rows, held.astype(BF16)) + skip_ref[0:1, lanes] * vals
        cum_cols = wide_cum[:, both]
        for low in range(0, Q, BLK):
            width = low + BLK
            total = base[low:width, :]
            for which in range(2):
                across = row_cum[pl.ds(index * 2 + which, 1), :][:, :width]
                down = cum_cols[low:width, which * LANE : (which + 1) * LANE]
                down = jnp.concatenate([down] * (width // LANE), axis=1)
                decays = jnp.exp2(jnp.minimum(down - across, 0.0))
                mixing = (decays * scores[low:width, :width]).astype(BF16)
                total = total + mm(mixing, own[which][:width, :])
            y_ref[low:width, lanes] = total
        weighted = (spreads[2, :, lanes] * scaled.astype(F32)).astype(BF16)
        state[:, lanes] = held * into_here[Q - 1 : Q, :] + mm(b_turned, weighted)
        return 0

    lax.fori_loop(0, heads // 2, pair, 0, unroll=UNROLL)
    tail_rows[...] = raw_ref[Q - 8 : Q, :]


def ssd_bwd_kernel(
    heads,
    raw_ref,
    halo_ref,
    small_ref,
    bc_ref,
    masks_ref,
    masks_next_ref,
    meta_ref,
    seg_ref,
    taps_ref,
    hp_ref,
    skip_ref,
    expand_ref,
    widen_ref,
    gather_ref,
    y_ref,
    dy_ref,
    st_ref,
    dx_ref,
    ddt_ref,
    dbc_ref,
    dtaps_ref,
    dhp_ref,
    dskip_ref,
    dstate,
    next_rows,
    carried,
    window,
    dwindow,
    row_cum,
    scores,
    dscores,
    columns,
    into_dy,
    tail_vals,
    balance_parts,
    direct_parts,
    wide_cum,
):
    chunk = pl.program_id(0)

    @pl.when(chunk == 0)
    def _():
        dstate[...] = jnp.zeros_like(dstate)
        next_rows[...] = jnp.zeros_like(next_rows)
        carried[...] = jnp.zeros_like(carried)
        dtaps_ref[...] = jnp.zeros_like(dtaps_ref)
        dhp_ref[...] = jnp.zeros_like(dhp_ref)
        dskip_ref[...] = jnp.zeros_like(dskip_ref)

    pre, steps, cum, into, tail = step_terms(small_ref, meta_ref, hp_ref)
    row_cum[...] = cum
    for at, value in enumerate((cum, steps, into, tail)):
        columns[at] = as_columns(value)
    cum_cols = jnp.concatenate([cum] * 4, axis=0).T
    for head in range(heads):
        wide_cum[:, head * LANE : (head + 1) * LANE] = jnp.broadcast_to(
            cum_cols[:, head : head + 1], (Q, LANE)
        )
    same = (seg_ref[:, 0:1] == meta_ref[0, 0:1, :]) & (iota2((Q, Q), 0) <= iota2((Q, Q), 1))
    b_rows = bc_ref[:N, :].astype(F32).T.astype(BF16)
    c_turned = bc_ref[N:, :]
    scores[...] = jnp.where(same, mm(b_rows, c_turned), 0.0)
    dscores[...] = jnp.zeros_like(dscores)
    carry_high, carry_low = split_two(carried[...])
    gather_all = gather_ref[...]
    from_next = mm(carry_high, gather_all) + mm(carry_low, gather_all)
    dstate_half = dstate[...].astype(BF16)
    first = iota2((Q, LANE), 1) < LANE // 2

    def pair(index, _):
        lanes = pl.ds(pl.multiple_of(index * LANE, LANE), LANE)
        both = pl.ds(pl.multiple_of(index * 2 * LANE, 2 * LANE), 2 * LANE)
        window[0:8, :] = halo_ref[:, lanes]
        current = raw_ref[:, lanes]
        window[8 : 8 + Q, :] = current
        conv = taps_ref[4:5, lanes] + taps_ref[3:4, lanes] * current
        for offset in range(1, 4):
            conv = conv + taps_ref[3 - offset : 4 - offset, lanes] * (
                masks_ref[:, (offset - 1) * LANE : offset * LANE]
                * window[8 - offset : 8 - offset + Q, :]
            )
        gate = jax.nn.sigmoid(conv)
        vals = conv * gate
        expand = expand_ref[:, lanes]
        step_here = mm(columns[1], expand)
        scaled = (vals * step_here).astype(BF16)
        skip = skip_ref[0:1, lanes]
        dy = dy_ref[:, lanes]
        dy_half = dy.astype(BF16)
        zero = jnp.zeros_like(scaled)
        own = (jnp.where(first, scaled, zero), jnp.where(first, zero, scaled))
        own_dy = (jnp.where(first, dy_half, zero), jnp.where(first, zero, dy_half))
        dheld = dstate[:, lanes]
        tail_here = mm(columns[3], expand)
        into_here = mm(columns[2], expand)
        base = tail_here * mm(b_rows, dheld.astype(BF16))
        cum_cols = wide_cum[:, both]
        pieces = []
        for low in range(0, Q, BLK):
            high = low + BLK
            total = base[low:high, :]
            for which in range(2):
                across = row_cum[pl.ds(index * 2 + which, 1), :][:, low:]
                down = cum_cols[low:high, which * LANE : (which + 1) * LANE]
                down = jnp.concatenate([down] * ((Q - low) // LANE), axis=1)
                decays = jnp.exp2(jnp.minimum(across - down, 0.0))
                mixing = (decays * scores[low:high, low:]).astype(BF16)
                total = total + mm(mixing, own_dy[which][low:, :])
                dmix = mm_nt(own[which][low:high, :], dy_half[low:, :])
                dscores[low:high, low:] += dmix * decays
            pieces.append(total)
        dscaled = jnp.concatenate(pieces, axis=0)
        held = st_ref[0, :, lanes]
        edy = (into_here * dy).astype(BF16)
        scaled_f = scaled.astype(F32)
        into_dy[:, lanes] = edy
        tail_vals[:, lanes] = (tail_here * scaled_f).astype(BF16)
        balance = dy_half.astype(F32) * (y_ref[:, lanes] - skip * vals) - scaled_f * dscaled
        part_high, part_low = split_two(balance)
        balance_parts[0, :, lanes] = part_high
        balance_parts[1, :, lanes] = part_low
        part_high, part_low = split_two(vals * dscaled)
        direct_parts[0, :, lanes] = part_high
        direct_parts[1, :, lanes] = part_low
        dskip_ref[0:1, lanes] += jnp.sum(dy * vals, axis=0, keepdims=True)
        dheld_new = into_here[Q - 1 : Q, :] * dheld + mm(c_turned, edy)
        dstate[:, lanes] = dheld_new
        carried[0:1, lanes] = jnp.sum(dheld_new * held, axis=0, keepdims=True)
        dvals = step_here * dscaled + skip * dy
        dconv = dvals * (gate * (1.0 + conv * (1.0 - gate)))
        dwindow[0:Q, :] = dconv
        dwindow[Q : Q + 8, :] = next_rows[:, lanes]
        next_rows[:, lanes] = dconv[0:8, :]
        dtaps_ref[4:5, lanes] += jnp.sum(dconv, axis=0, keepdims=True)
        dtaps_ref[3:4, lanes] += jnp.sum(dconv * current, axis=0, keepdims=True)
        draw = taps_ref[3:4, lanes] * dconv
        for offset in range(1, 4):
            mask = masks_ref[:, (offset - 1) * LANE : offset * LANE]
            mask_next = masks_next_ref[:, (offset - 1) * LANE : offset * LANE]
            mask_later = jnp.concatenate([mask, mask_next], axis=0)[offset : offset + Q, :]
            shifted = mask * window[8 - offset : 8 - offset + Q, :]
            dtaps_ref[3 - offset : 4 - offset, lanes] += jnp.sum(
                dconv * shifted, axis=0, keepdims=True
            )
            draw = draw + taps_ref[3 - offset : 4 - offset, lanes] * (
                mask_later * dwindow[offset : offset + Q, :]
            )
        dx_ref[:, lanes] = draw.astype(BF16)
        return 0

    lax.fori_loop(0, heads // 2, pair, 0, unroll=UNROLL)
    dscores_now = jnp.where(same, dscores[...], 0.0)
    d_b = mm_nt(tail_vals[...], dstate_half) + mm_nt(dscores_now.astype(BF16), c_turned)
    d_c = mm_nt(into_dy[...], st_ref[0].astype(BF16)) + mm(dscores_now.T.astype(BF16), b_rows)
    dbc_ref[:N, :] = d_b.T
    dbc_ref[N:, :] = d_c.T
    balance = mm(balance_parts[0], gather_all) + mm(balance_parts[1], gather_all)
    balance = balance + jnp.where(iota2((Q, LANE), 0) == Q - 1, from_next[0:1, :], 0.0)
    direct = mm(direct_parts[0], gather_all) + mm(direct_parts[1], gather_all)
    since = (iota2((Q, Q), 0) >= iota2((Q, Q), 1)).astype(BF16)
    dlogs = lane_sums(balance.T[:SLOTS], since)
    dsteps = dlogs * hp_ref[:, 1:2] + direct.T[:SLOTS]
    dsteps = dsteps * jax.nn.sigmoid(pre) * hp_ref[:, 2:3]
    ddt_ref[...] = dsteps
    dhp_ref[:, 0:1] += jnp.sum(dsteps, axis=1, keepdims=True)
    dhp_ref[:, 1:2] += jnp.sum(dlogs * steps, axis=1, keepdims=True)


def head_tables(heads):
    width = heads * (LANE // 2)
    owner = jnp.arange(width) // (LANE // 2)
    wide_owner = jnp.arange(heads * LANE) // LANE
    slot = jnp.arange(LANE)
    real = (slot < 3 * SLOTS)[:, None]
    expand = ((slot % SLOTS)[:, None] == owner[None, :]) & real
    widen = ((slot % SLOTS)[:, None] == wide_owner[None, :]) & real
    gather = owner[:, None] == slot[None, :]
    return expand.astype(BF16), widen.astype(BF16), gather.astype(BF16)


def segment_tables(segment):
    length = segment.shape[0]
    chunks = length // Q
    doc_masks = []
    for offset in range(1, 4):
        earlier = jnp.concatenate(
            [jnp.full((offset,), -1, jnp.int32), segment[: length - offset]], axis=0
        )
        doc_masks.append((earlier == segment).astype(F32))
    masks = jnp.concatenate(
        [jnp.broadcast_to(mask[:, None], (length, LANE)) for mask in doc_masks], axis=1
    )
    by_chunk = segment.reshape(chunks, Q)
    last = by_chunk[:, Q - 1]
    before = jnp.concatenate([jnp.full((1,), -1, jnp.int32), last[: chunks - 1]], axis=0)
    rows = [
        by_chunk.astype(F32),
        (by_chunk == before[:, None]).astype(F32),
        (by_chunk == last[:, None]).astype(F32),
    ]
    meta = jnp.pad(jnp.stack(rows, axis=1), ((0, 0), (0, 5), (0, 0)))
    seg_cols = jnp.broadcast_to(segment.astype(F32)[:, None], (length, LANE))
    return doc_masks, masks, meta, seg_cols


def head_columns(head_params):
    heads = head_params.shape[1]
    rates = -jnp.exp(head_params[1])
    table = jnp.stack([head_params[0], rates, jnp.ones_like(rates)], axis=1)
    return jnp.pad(table, ((0, SLOTS - heads), (0, LANE - 3)))


def time_like(seconds):
    return pl.CostEstimate(
        flops=int(seconds * 1.1e15), bytes_accessed=int(seconds * 3.4e12), transcendentals=0
    )


def full_spec(shape):
    return pl.BlockSpec(shape, lambda c: (0,) * len(shape))


def ssd_forward(raw, small, bc, tables, taps, hp, skip, spread, heads):
    length = raw.shape[0]
    width = heads * (LANE // 2)
    chunks = length // Q
    _, masks, meta, seg_cols = tables
    expand, widen, _ = spread
    return pl.pallas_call(
        functools.partial(ssd_fwd_kernel, heads),
        grid=(chunks,),
        out_shape=(
            jax.ShapeDtypeStruct((length, width), F32),
            jax.ShapeDtypeStruct((chunks, N, width), F32),
        ),
        in_specs=[
            pl.BlockSpec((Q, width), lambda c: (c, 0)),
            pl.BlockSpec((SLOTS, Q), lambda c: (0, c)),
            pl.BlockSpec((2 * N, Q), lambda c: (0, c)),
            pl.BlockSpec((Q, 3 * LANE), lambda c: (c, 0)),
            pl.BlockSpec((1, 8, Q), lambda c: (c, 0, 0)),
            pl.BlockSpec((Q, LANE), lambda c: (c, 0)),
            full_spec((8, width)),
            full_spec((SLOTS, LANE)),
            full_spec((8, width)),
            full_spec((LANE, width)),
            full_spec((LANE, heads * LANE)),
        ],
        out_specs=(
            pl.BlockSpec((Q, width), lambda c: (c, 0)),
            pl.BlockSpec((1, N, width), lambda c: (c, 0, 0)),
        ),
        scratch_shapes=[
            pltpu.VMEM((N, width), F32),
            pltpu.VMEM((8, width), F32),
            pltpu.VMEM((Q + 8, LANE), F32),
            pltpu.VMEM((SLOTS, Q), F32),
            pltpu.VMEM((Q, Q), F32),
            pltpu.VMEM((4, Q, LANE), BF16),
            pltpu.VMEM((3, Q, width), F32),
            pltpu.VMEM((Q, heads * LANE), F32),
        ],
        compiler_params=pltpu.CompilerParams(vmem_limit_bytes=VMEM_CAP),
        cost_estimate=time_like(37e-6 * length * heads / 30720),
        name="ssd_fwd",
    )(raw, small, bc, masks, meta, seg_cols, taps, hp, skip, expand, widen)


def ssd_backward(raw, small, bc, tables, taps, hp, skip, spread, y, dy, states, heads):
    length = raw.shape[0]
    width = heads * (LANE // 2)
    chunks = length // Q
    per = Q // 8
    _, masks, meta, seg_cols = tables

    def at(c):
        return chunks - 1 - c

    return pl.pallas_call(
        functools.partial(ssd_bwd_kernel, heads),
        grid=(chunks,),
        out_shape=(
            jax.ShapeDtypeStruct((length, width), BF16),
            jax.ShapeDtypeStruct((SLOTS, length), F32),
            jax.ShapeDtypeStruct((2 * N, length), F32),
            jax.ShapeDtypeStruct((8, width), F32),
            jax.ShapeDtypeStruct((SLOTS, LANE), F32),
            jax.ShapeDtypeStruct((8, width), F32),
        ),
        in_specs=[
            pl.BlockSpec((Q, width), lambda c: (at(c), 0)),
            pl.BlockSpec((8, width), lambda c: (jnp.maximum(at(c) * per - 1, 0), 0)),
            pl.BlockSpec((SLOTS, Q), lambda c: (0, at(c))),
            pl.BlockSpec((2 * N, Q), lambda c: (0, at(c))),
            pl.BlockSpec((Q, 3 * LANE), lambda c: (at(c), 0)),
            pl.BlockSpec(
                (8, 3 * LANE), lambda c: (jnp.minimum((at(c) + 1) * per, chunks * per - 1), 0)
            ),
            pl.BlockSpec((1, 8, Q), lambda c: (at(c), 0, 0)),
            pl.BlockSpec((Q, LANE), lambda c: (at(c), 0)),
            full_spec((8, width)),
            full_spec((SLOTS, LANE)),
            full_spec((8, width)),
            full_spec((LANE, width)),
            full_spec((LANE, heads * LANE)),
            full_spec((width, LANE)),
            pl.BlockSpec((Q, width), lambda c: (at(c), 0)),
            pl.BlockSpec((Q, width), lambda c: (at(c), 0)),
            pl.BlockSpec((1, N, width), lambda c: (at(c), 0, 0)),
        ],
        out_specs=(
            pl.BlockSpec((Q, width), lambda c: (at(c), 0)),
            pl.BlockSpec((SLOTS, Q), lambda c: (0, at(c))),
            pl.BlockSpec((2 * N, Q), lambda c: (0, at(c))),
            full_spec((8, width)),
            full_spec((SLOTS, LANE)),
            full_spec((8, width)),
        ),
        scratch_shapes=[
            pltpu.VMEM((N, width), F32),
            pltpu.VMEM((8, width), F32),
            pltpu.VMEM((8, width), F32),
            pltpu.VMEM((Q + 8, LANE), F32),
            pltpu.VMEM((Q + 8, LANE), F32),
            pltpu.VMEM((SLOTS, Q), F32),
            pltpu.VMEM((Q, Q), F32),
            pltpu.VMEM((Q, Q), F32),
            pltpu.VMEM((4, Q, LANE), BF16),
            pltpu.VMEM((Q, width), BF16),
            pltpu.VMEM((Q, width), BF16),
            pltpu.VMEM((2, Q, width), BF16),
            pltpu.VMEM((2, Q, width), BF16),
            pltpu.VMEM((Q, heads * LANE), F32),
        ],
        compiler_params=pltpu.CompilerParams(vmem_limit_bytes=VMEM_CAP),
        cost_estimate=time_like(69e-6 * length * heads / 30720),
        name="ssd_bwd",
    )(
        raw,
        raw,
        small,
        bc,
        masks,
        masks,
        meta,
        seg_cols,
        taps,
        hp,
        skip,
        *spread,
        y,
        dy,
        states,
    )


def dn_kernel(count, rows, at_ref, *refs):
    dz, dx, side, normed = (refs[k * count : (k + 1) * count] for k in range(4))
    gate_ref, inner_ref, out_ref, sums_ref = refs[4 * count : 4 * count + 4]
    turned = refs[4 * count + 4]
    width = dz[0].shape[1]

    @pl.when(pl.program_id(0) == 0)
    def _():
        for k in range(count):
            turned[k * rows : (k + 1) * rows, :] = side[k][...].T.astype(BF16)

    gate = gate_ref[...]
    inner = inner_ref[:, :width]
    last = inner_ref[:, width:]
    sums = None
    for k in range(count):
        at = slice(k * rows, (k + 1) * rows)
        total = mm_nt(dz[k][...], gate) + mm_nt(dx[k][...], inner) + mm_nt(turned[at, :], last)
        out_ref[at, :] = total.astype(BF16)
        part = jnp.sum(total * normed[k][...].astype(F32), axis=0, keepdims=True)
        sums = part if sums is None else sums + part
    sums_ref[0:1, :] = sums


def d_normed_blocks(d_z, d_x, d_side, gate_all, x_all, normed, blocks, which, rows, tile=256):
    length, width = d_z.shape
    count = blocks.shape[0]
    half = gate_all.shape[0] // 2
    first = which * half // tile

    def rows_of(k):
        return pl.BlockSpec((rows, width), lambda n, at, k=k: (at[k], 0))

    def cols_of(k):
        return pl.BlockSpec((LANE, rows), lambda n, at, k=k: (0, at[k]))

    def tile_of(k):
        return pl.BlockSpec((rows, tile), lambda n, at, k=k: (at[k], n + first))

    each = range(count)
    return pl.pallas_call(
        functools.partial(dn_kernel, count, rows),
        grid_spec=pltpu.PrefetchScalarGridSpec(
            num_scalar_prefetch=1,
            grid=(half // tile,),
            in_specs=[rows_of(k) for k in each]
            + [rows_of(k) for k in each]
            + [cols_of(k) for k in each]
            + [tile_of(k) for k in each]
            + [
                pl.BlockSpec((tile, width), lambda n, at: (n + first, 0)),
                pl.BlockSpec((tile, width + LANE), lambda n, at: (n + first, 0)),
            ],
            out_specs=(
                pl.BlockSpec((count * rows, tile), lambda n, at: (0, n)),
                pl.BlockSpec((8, tile), lambda n, at: (0, n)),
            ),
            scratch_shapes=[pltpu.VMEM((count * rows, LANE), BF16)],
        ),
        out_shape=(
            jax.ShapeDtypeStruct((count * rows, half), BF16),
            jax.ShapeDtypeStruct((8, half), F32),
        ),
        compiler_params=pltpu.CompilerParams(vmem_limit_bytes=VMEM_CAP),
        cost_estimate=time_like(1e-7),
        name="d_normed",
    )(
        blocks,
        *([d_z] * count),
        *([d_x] * count),
        *([d_side] * count),
        *([normed] * count),
        gate_all,
        x_all,
    )


def adam_kernel(step, gate_ref, inner_ref, weight_ref, first_ref, second_ref, *outs):
    grad_out, weight_out, first_out, second_out = outs
    for part, grad_ref in ((0, gate_ref), (1, inner_ref)):
        grad = grad_ref[...].astype(F32)
        new_weight, new_first, new_second = step(
            weight_ref[:, part, :], grad, first_ref[:, part, :], second_ref[:, part, :]
        )
        grad_out[:, part, :] = grad
        weight_out[:, part, :] = new_weight
        first_out[:, part, :] = new_first
        second_out[:, part, :] = new_second


def adam_pair(step, grad_gate, grad_inner, weight, first, second, rows=40):
    shard, _, width = weight.shape
    deep = pl.BlockSpec((rows, 2, width), lambda n: (n, 0, 0))
    flat = pl.BlockSpec((rows, width), lambda n: (n, 0))
    like = jax.ShapeDtypeStruct(weight.shape, F32)
    return pl.pallas_call(
        functools.partial(adam_kernel, step),
        grid=(shard // rows,),
        out_shape=(like, jax.ShapeDtypeStruct(weight.shape, weight.dtype), like, like),
        in_specs=[flat, flat, deep, deep, deep],
        out_specs=(deep,) * 4,
        compiler_params=pltpu.CompilerParams(vmem_limit_bytes=VMEM_CAP),
        cost_estimate=pl.CostEstimate(flops=1000, bytes_accessed=1000, transcendentals=0),
        name="adam_pair",
    )(grad_gate, grad_inner, weight, first, second)


def product_kernel(left_ref, right_ref, out_ref):
    out_ref[...] = mm(left_ref[...], right_ref[...])


def gate_kernel(left_ref, right_ref, mixed_ref, z_ref, gated_ref, sums_ref):
    z_raw = mm(left_ref[...], right_ref[...])
    gated = mixed_ref[...] * (z_raw * jax.nn.sigmoid(z_raw))
    z_ref[...] = z_raw
    gated_ref[...] = gated
    sums = jnp.sum(gated * gated, axis=1, keepdims=True)
    sums_ref[...] = jnp.broadcast_to(sums, (sums.shape[0], LANE)).T[:8]


def output_kernel(left_ref, right_ref, grad_ref, first_ref, second_ref, sums_ref):
    half = first_ref.shape[1]
    total = None
    for at, out_ref in ((0, first_ref), (half, second_ref)):
        part = mm_nt(left_ref[...], right_ref[at : at + half, :])
        out_ref[...] = part.astype(BF16)
        sums = jnp.sum(part * grad_ref[:, at : at + half].astype(F32), axis=1, keepdims=True)
        total = sums if total is None else total + sums
    sums_ref[...] = jnp.broadcast_to(total, (total.shape[0], LANE)).T[:8]


def gate_grad_kernel(
    left_ref, right_ref, z_ref, mixed_ref, gain_ref, inv_ref, mean_ref, dy_ref, dz_ref, dgain_ref
):
    @pl.when(pl.program_id(0) == 0)
    def _():
        dgain_ref[...] = jnp.zeros_like(dgain_ref)

    d_ng = mm(left_ref[...], right_ref[...])
    z_raw = z_ref[...]
    mixed = mixed_ref[...]
    inv = inv_ref[...]
    sig = jax.nn.sigmoid(z_raw)
    gate_act = z_raw * sig
    unit = mixed * gate_act * inv
    dgain_ref[0:1, :] += jnp.sum(d_ng * unit, axis=0, keepdims=True)
    d_gated = inv * (d_ng * gain_ref[0:1, :] - unit * mean_ref[...])
    dy_ref[...] = d_gated * gate_act
    dz_ref[...] = (d_gated * mixed * sig * (1.0 + z_raw * (1.0 - sig))).astype(BF16)


def row_call(kernel, name, seconds, length, rows, ins, outs):
    def spec(shape, split):
        if split == "rows":
            return pl.BlockSpec((rows,) + shape, lambda m: (m, 0))
        if split == "lanes":
            return pl.BlockSpec(shape + (rows,), lambda m: (0, m))
        return pl.BlockSpec(shape, lambda m: (0, 0))

    return pl.pallas_call(
        kernel,
        grid=(length // rows,),
        out_shape=tuple(jax.ShapeDtypeStruct(full, kind) for full, kind, _, _ in outs),
        in_specs=[spec(shape, split) for _, shape, split in ins],
        out_specs=tuple(spec(shape, split) for _, _, shape, split in outs),
        compiler_params=pltpu.CompilerParams(vmem_limit_bytes=VMEM_CAP),
        cost_estimate=time_like(seconds),
        name=name,
    )(*[array for array, _, _ in ins])


def inner_product(normed, x_all, width, rows=256):
    length, model = normed.shape
    return row_call(
        product_kernel,
        "inner_product",
        14e-6,
        length,
        rows,
        [(normed, (model,), "rows"), (x_all, (model, width), None)],
        [((length, width), F32, (width,), "rows")],
    )[0]


def gate_product(normed, gate_all, mixed, rows=256):
    length, model = normed.shape
    width = gate_all.shape[1]
    wide = ((length, width), F32, (width,), "rows")
    z_raw, gated, sums = row_call(
        gate_kernel,
        "gate_product",
        16e-6,
        length,
        rows,
        [(normed, (model,), "rows"), (gate_all, (model, width), None), (mixed, (width,), "rows")],
        [wide, wide, ((8, length), F32, (8,), "lanes")],
    )
    return z_raw, gated, sums[0]


def output_product(normed_gated, out_all, group_grad, rows=256):
    length, width = normed_gated.shape
    model = out_all.shape[0]
    part = ((length, model // 2), BF16, (model // 2,), "rows")
    left, right, sums = row_call(
        output_kernel,
        "output_product",
        16e-6,
        length,
        rows,
        [
            (normed_gated, (width,), "rows"),
            (out_all, (model, width), None),
            (group_grad, (model,), "rows"),
        ],
        [part, part, ((8, length), F32, (8,), "lanes")],
    )
    return left, right, sums[0]


def gate_gradient(group_grad, out_all, z_raw, mixed, gain, inv, mean, rows=256):
    length, model = group_grad.shape
    width = out_all.shape[1]
    return row_call(
        gate_grad_kernel,
        "gate_gradient",
        18e-6,
        length,
        rows,
        [
            (group_grad, (model,), "rows"),
            (out_all, (model, width), None),
            (z_raw, (width,), "rows"),
            (mixed, (width,), "rows"),
            (gain, (8, width), None),
            (inv, (1,), "rows"),
            (mean, (1,), "rows"),
        ],
        [
            ((length, width), F32, (width,), "rows"),
            ((length, width), BF16, (width,), "rows"),
            ((8, width), F32, (8, width), None),
        ],
    )

DI = 5120
STEP = 3
NORM_EPS = 1e-05
BETA_ONE = 0.9
BETA_TWO = 0.95
LEARN_RATE = 0.004
LEARN_SMALL = 0.15
WEIGHT_DECAY = 0.1
ADAM_EPS = 1e-08


def by_rows(value):
    return with_layout_constraint(value, Layout(major_to_minor=(0, 1)))


def silu_act(values):
    return values * jax.nn.sigmoid(values)


def later(row, offset):
    return jnp.pad(row, ((0, 0), (offset, 0)))[:, : row.shape[1]]


def state_act(raw_cols, conv_taps, doc_masks):
    conv = conv_taps[4][:, None] + conv_taps[3][:, None] * raw_cols
    for offset in range(1, 4):
        conv = conv + conv_taps[3 - offset][:, None] * (
            doc_masks[offset - 1][None, :] * later(raw_cols, offset)
        )
    return silu_act(conv)


def contract_rows(left_mat, right_mat):
    return lax.dot_general(
        left_mat, right_mat, (((0,), (0,)), ((), ())), preferred_element_type=F32
    )


def adamw_step(weight, gradient, first_moment, second_moment, decay_factor, learn_rate):
    new_first = BETA_ONE * first_moment + (1.0 - BETA_ONE) * gradient
    new_second = BETA_TWO * second_moment + (1.0 - BETA_TWO) * gradient * gradient
    first_hat = new_first / (1.0 - BETA_ONE**STEP)
    second_hat = new_second / (1.0 - BETA_TWO**STEP)
    weight_f = weight.astype(F32)
    updated = weight_f - learn_rate * (
        first_hat / (jnp.sqrt(second_hat) + ADAM_EPS) + decay_factor * weight_f
    )
    return (updated.astype(weight.dtype), new_first, new_second)


def swap(value, distance, size):
    return lax.ppermute(value, "tp", [(at, at ^ distance) for at in range(size)])


def tied(*values):
    return lax.optimization_barrier(values)


def gather_parts(value, size, near_done):
    if size != 4:
        one, *others = near_done(swap(value, 1, size))
        return [value, one] + [swap(value, k, size) for k in range(2, size)], *others
    half = value.shape[0] // 2
    one, two = swap(value, 1, size), swap(value, 2, size)
    one, *others = near_done(one)
    far = jnp.concatenate([swap(two[:half], 1, size), swap(one[half:], 2, size)], axis=0)
    return [value, one, two, far], *others


def scatter_start(left, right, rows, index, size):
    def block(value, distance):
        return lax.dynamic_slice_in_dim(value, (index ^ distance) * rows, rows, 0)

    sent, kept = [], []
    for half, near in ((left, 1), (right, 2)):
        if size == 4:
            pair = jnp.concatenate([block(half, 3), block(half, near)], axis=0)
            sent.append(swap(pair, near, size))
            kept.append((block(half, 3 - near), block(half, 0)))
        else:
            sent.append([swap(block(half, k), k, size) for k in range(1, size)])
            kept.append(block(half, 0))
    return sent, kept


def scatter_middle(sent, kept, rows, size):
    if size != 4:
        return sent, [(one,) for one in kept]
    passed = [
        (kept[at][0].astype(F32) + sent[at][:rows].astype(F32)).astype(BF16) for at in range(2)
    ]
    return passed, [(kept[at][1], sent[at][rows:]) for at in range(2)]


def scatter_last(passed, size):
    if size != 4:
        return passed[0] + passed[1]
    return [swap(passed[0], 2, size), swap(passed[1], 1, size)]


def scatter_end(own, last):
    each = len(last) // 2
    totals = []
    for at in range(2):
        total = own[at][0].astype(F32)
        for piece in own[at][1:]:
            total = total + piece.astype(F32)
        for piece in last[at * each : (at + 1) * each]:
            total = total + piece.astype(F32)
        totals.append(total)
    return jnp.concatenate(totals, axis=1)


def row_sum(value, size):
    total = value
    for distance in range(1, size):
        total = total + swap(value, distance, size)
    return total


def all_sum(value, index, size):
    terms = jnp.zeros((size,) + value.shape, value.dtype)
    for distance in range(size):
        piece = value if distance == 0 else swap(value, distance, size)
        terms = lax.dynamic_update_slice(terms, piece[None], (index ^ distance, jnp.int32(0)))
    return jnp.sum(terms, axis=0)


def fsdp_swap(value, distance, size):
    return lax.ppermute(value, "fsdp", [(at, at ^ distance) for at in range(size)])


def gather_by_swaps(value, index, size):
    whole = jnp.zeros((size,) + value.shape, value.dtype)
    for distance in range(size):
        piece = value if distance == 0 else fsdp_swap(value, distance, size)
        whole = lax.dynamic_update_slice(whole, piece[None], (index ^ distance, jnp.int32(0)))
    return whole


def pair_sum(value, index, size):
    blocks = value.reshape(size // 2, 2, value.shape[0] // size, value.shape[1])
    core = index % 2
    away = lax.dynamic_slice_in_dim(blocks, 1 - core, 1, 1)[:, 0]
    own = lax.dynamic_slice_in_dim(blocks, core, 1, 1)[:, 0]
    return (own.astype(F32) + fsdp_swap(away, 1, size).astype(F32)).astype(value.dtype)


def chip_scatter(value, size):
    groups = [list(range(core, size, 2)) for core in range(2)]
    flat = value.reshape(value.shape[0] * value.shape[1], value.shape[2])
    return lax.psum_scatter(
        flat, "fsdp", scatter_dimension=0, axis_index_groups=groups, tiled=True
    )


def chip_sum(value, index, size):
    chip = index // 2

    def block(distance):
        return lax.dynamic_slice_in_dim(value, chip ^ distance, 1, 0)[0]

    total = block(0).astype(F32)
    for distance in range(1, size // 2):
        total = total + fsdp_swap(block(distance), 2 * distance, size).astype(F32)
    return total


def pad_cols(value, width):
    return jnp.pad(value, ((0, 0), (0, width - value.shape[1])))


def body(
    block_in,
    cotangent,
    segment_ids,
    group_fill,
    input_gain,
    proj_inner,
    proj_step,
    proj_state,
    conv_inner,
    conv_state,
    head_params,
    mixer_gain,
    proj_output,
    *moments,
):
    tp_size = lax.axis_size("tp")
    fsdp_size = lax.axis_size("fsdp")
    tp_index = lax.axis_index("tp")
    fsdp_index = lax.axis_index("fsdp")
    own_rows, model = block_in.shape
    group_rows = own_rows * tp_size
    shard, _, width = proj_inner.shape
    heads = proj_step.shape[1]
    state_cols = proj_state.shape[1]
    segment = segment_ids[0]
    filled = group_fill[0]

    small_values = jnp.concatenate(
        [conv_inner.reshape(-1), conv_state.reshape(-1), mixer_gain], axis=0
    )
    small_count = small_values.shape[0]
    inner_n, state_n = conv_inner.size, conv_state.size
    small_cols = -(-(small_count + 3 * heads) // shard)
    small_block = jnp.pad(small_values, (0, small_cols * shard - small_count)).reshape(
        shard, small_cols
    )
    used = heads + state_cols
    side = pad_cols(
        jnp.concatenate([proj_step, proj_state, input_gain[:, None], small_block], axis=1), LANE
    )
    (inner_halves,) = tied(proj_inner.transpose(1, 0, 2))
    x_local = jnp.concatenate([inner_halves[1], side], axis=1)
    x_all = lax.all_gather(x_local, "fsdp", axis=0, tiled=True)
    gate_all = lax.all_gather(inner_halves[0], "fsdp", axis=0, tiled=True)
    gain_all = lax.dynamic_update_slice(
        jnp.zeros((fsdp_size, shard), BF16), input_gain[None], (fsdp_index, jnp.int32(0))
    )
    distance = 1
    while distance < fsdp_size:
        gain_all = gain_all + fsdp_swap(gain_all, distance, fsdp_size)
        distance *= 2
    gain_f = gain_all.reshape(model).astype(F32)
    positions = tp_index * own_rows + jnp.arange(own_rows, dtype=jnp.int32)
    live_rows = (positions < filled)[:, None]
    block_f = block_in.astype(F32)
    cot_f = cotangent.astype(F32)
    own_grad = jnp.where(live_rows, cot_f, 0.0).astype(BF16)
    blank = jnp.zeros((group_rows, model), BF16)

    def unit_of(rows):
        rows_f = rows.astype(F32)
        scale = lax.rsqrt(jnp.mean(rows_f * rows_f, axis=1, keepdims=True) + NORM_EPS)
        return rows_f * scale, scale

    def normed_of(rows):
        return (unit_of(rows)[0] * gain_f[None, :]).astype(BF16)

    def put(whole, part, distance):
        return lax.dynamic_update_slice(
            whole, part, ((tp_index ^ distance) * own_rows, jnp.int32(0))
        )

    started = put(blank, normed_of(block_in), 0)

    def near_done(one):
        return tied(one, started, own_grad)

    row_parts, started, own_grad = gather_parts(block_in, tp_size, near_done)
    row_parts = [by_rows(part) for part in row_parts]
    own_grad, *row_parts = tied(own_grad, *row_parts)
    near = min(3, tp_size)
    grad_parts = [by_rows(own_grad)] + [swap(own_grad, k, tp_size) for k in range(1, near)]

    side_all = x_all[:, width:]
    extras = side_all[:, used + 1 : used + 1 + small_cols].reshape(fsdp_size, shard * small_cols)

    def from_owners(flat, rows):
        return flat.reshape(fsdp_size, rows, -1).transpose(1, 0, 2).reshape(rows, -1).astype(F32)

    taps_inner = from_owners(extras[:, :inner_n], 5)
    taps_state = from_owners(extras[:, inner_n : inner_n + state_n], 5)
    mixer_f = from_owners(extras[:, inner_n + state_n : small_count], 1)[0]

    normed = started
    for distance in range(1, tp_size - 1):
        normed = put(normed, normed_of(row_parts[distance]), distance)
    far_rows, normed = tied(row_parts[-1], normed)
    normed = by_rows(put(normed, normed_of(far_rows), tp_size - 1))
    small = lax.dot_general(
        side_all, normed, (((0,), (1,)), ((), ())), preferred_element_type=F32
    )
    raw = inner_product(normed, x_all, width)
    tables = segment_tables(segment)
    doc_masks = tables[0]
    state_vals, state_back = jax.vjp(
        lambda raw_cols, conv_taps: state_act(raw_cols, conv_taps, doc_masks),
        small[heads:used],
        taps_state,
    )
    state_local = state_vals.astype(BF16)
    bc = jnp.zeros((tp_size * state_cols, group_rows), BF16)
    for k in range(tp_size):
        piece = state_local if k == 0 else swap(state_local, k, tp_size)
        bc = lax.dynamic_update_slice(bc, piece, ((tp_index ^ k) * state_cols, jnp.int32(0)))
    own_grad, bc, out_local = tied(own_grad, bc, proj_output.T)
    out_all = lax.all_gather(out_local, "fsdp", axis=0, tiled=True)
    grad_parts += [swap(own_grad, k, tp_size) for k in range(near, tp_size)]
    spread = head_tables(heads)
    taps8 = jnp.pad(taps_inner, ((0, 3), (0, 0)))
    hp8 = head_columns(head_params)
    skip8 = jnp.broadcast_to(jnp.repeat(head_params[2], LANE // 2)[None, :], (8, width))
    mixed, states = ssd_forward(raw, small, bc, tables, taps8, hp8, skip8, spread, heads)

    z_raw, gated, square_sum = gate_product(normed, gate_all, mixed)
    square_sum, *grad_parts = tied(square_sum, *grad_parts)
    square_sum = row_sum(square_sum, tp_size)
    group_grad = jnp.zeros((group_rows, model), BF16)
    for distance in range(tp_size):
        group_grad = put(group_grad, grad_parts[distance], distance)
    group_grad = by_rows(group_grad)
    inv_gate = lax.rsqrt(square_sum / DI + NORM_EPS)[:, None]
    normed_gated = (gated * inv_gate * mixer_f[None, :]).astype(BF16)
    sum_out = pair_sum(
        contract_rows(group_grad, normed_gated).astype(BF16), fsdp_index, fsdp_size
    )
    half = model // 2
    normed_gated, sum_out = tied(normed_gated, sum_out)
    grad_out = chip_scatter(sum_out, fsdp_size)
    mixed_left, mixed_right, inner_sum = output_product(normed_gated, out_all, group_grad)
    inner_sum = row_sum(inner_sum, tp_size)
    mixed_sent, mixed_kept = scatter_start(mixed_left, mixed_right, own_rows, tp_index, tp_size)

    inner_mean = inner_sum[:, None] / DI
    mixer8 = jnp.broadcast_to(mixer_f[None, :], (8, width))
    d_mixed, d_z, grad_mixer = gate_gradient(
        group_grad, out_all, z_raw, mixed, mixer8, inv_gate, inner_mean
    )
    grad_mixer = grad_mixer[0]
    part_gate, mixed_sent = tied(contract_rows(normed, d_z).astype(BF16), mixed_sent)
    sum_gate = pair_sum(part_gate, fsdp_index, fsdp_size)
    mixed_passed, mixed_kept = scatter_middle(mixed_sent, mixed_kept, own_rows, tp_size)
    sum_gate, grad_out = tied(sum_gate, grad_out)

    d_mixed, sum_gate, mixed_passed = tied(d_mixed, sum_gate, mixed_passed)
    mixed_last = scatter_last(mixed_passed, tp_size)
    grad_gate = chip_scatter(sum_gate, fsdp_size)
    d_x, d_dt, d_bc, d_taps, d_heads, d_skip = ssd_backward(
        raw, small, bc, tables, taps8, hp8, skip8, spread, mixed, d_mixed, states, heads
    )
    def state_block(distance):
        return lax.dynamic_slice_in_dim(d_bc, (tp_index ^ distance) * state_cols, state_cols, 0)

    state_parts = [state_block(0)]
    state_parts += [swap(state_block(k), k, tp_size) for k in range(1, tp_size)]
    part_x, mixed_last, grad_gate, *state_parts = tied(
        contract_rows(normed, d_x).astype(BF16), mixed_last, grad_gate, *state_parts
    )
    sum_x = pair_sum(part_x, fsdp_index, fsdp_size)

    d_state_raw, grad_conv_state = state_back(sum(state_parts[1:], state_parts[0]).astype(F32))
    d_side = jnp.concatenate([d_dt[:heads], d_state_raw], axis=0)
    d_side = jnp.pad(d_side, ((0, LANE - used), (0, 0)))

    four = tp_size == 4
    side_part = lax.dot_general(
        normed, d_side.astype(BF16), (((0,), (1,)), ((), ())), preferred_element_type=F32
    )

    def side_gradient(side_part, d_taps, d_skip, d_heads, grad_conv_state, gain_sums):
        grad_head = jnp.stack(
            [
                d_heads[:heads, 0],
                hp8[:heads, 1] * d_heads[:heads, 1],
                jnp.sum(d_skip[0].reshape(heads, LANE // 2), axis=1),
            ],
            axis=0,
        )

        def by_owner(value):
            rows = value.shape[0]
            return value.reshape(rows, fsdp_size, -1).transpose(1, 0, 2).reshape(fsdp_size, -1)

        grad_extras = jnp.concatenate(
            [
                by_owner(d_taps[:5]),
                by_owner(grad_conv_state),
                by_owner(grad_mixer[None, :]),
                jnp.broadcast_to(grad_head.reshape(1, -1), (fsdp_size, 3 * heads)),
            ],
            axis=1,
        )
        grad_extras = pad_cols(grad_extras, small_cols * shard).reshape(fsdp_size * shard, small_cols)
        grad_extras = jnp.concatenate([gain_sums[:, None], grad_extras], axis=1)
        side_part = side_part + jnp.pad(
            grad_extras, ((0, 0), (used, LANE - used - 1 - small_cols))
        )
        side_part = pair_sum(side_part, fsdp_index, fsdp_size)
        return chip_sum(side_part, fsdp_index, fsdp_size)

    def d_normed_of(distances, which):
        return d_normed_blocks(
            d_z, d_x, d_side, gate_all, x_all, normed, tp_index ^ jnp.array(distances), which, own_rows
        )

    if four:
        left_away, gains_one = d_normed_of([3, 1], 0)
        gains_one, sum_x = tied(gains_one, sum_x)
        right_away, gains_two = d_normed_of([3, 2], 1)
        gains_two, mixed_last, d_taps, d_skip, d_heads, grad_conv_state = tied(
            gains_two, mixed_last, d_taps, d_skip, d_heads, grad_conv_state
        )
        sent = [swap(left_away, 1, 4), swap(right_away, 2, 4)]
        left_kept, gains_three = d_normed_of([2, 0], 0)
        sent[0], d_side_late, side_part, grad_out = tied(sent[0], d_side, side_part, grad_out)
        right_kept, gains_four = d_normed_blocks(
            d_z, d_x, d_side_late, gate_all, x_all, normed, tp_index ^ jnp.array([1, 0]), 1, own_rows
        )
        kept = [
            (left_kept[:own_rows], left_kept[own_rows:]),
            (right_kept[:own_rows], right_kept[own_rows:]),
        ]
        gain_sums = jnp.concatenate([gains_one + gains_three, gains_two + gains_four], axis=1)[0]
    else:
        left, gains_one = d_normed_of(list(range(tp_size)), 0)
        right, gains_two = d_normed_of(list(range(tp_size)), 1)
        sent = [
            [
                swap(part[k * own_rows : (k + 1) * own_rows], k, tp_size)
                for k in range(1, tp_size)
            ]
            for part in (left, right)
        ]
        kept = [left[:own_rows], right[:own_rows]]
        gain_sums = jnp.concatenate([gains_one, gains_two], axis=1)[0]
    grad_x = chip_scatter(sum_x, fsdp_size)
    passed, kept = scatter_middle(sent, kept, own_rows, tp_size)
    passed, mixed_last = tied(passed, mixed_last)
    mixed_rows = scatter_end(mixed_kept, mixed_last)
    block_out = (block_f + jnp.where(live_rows, mixed_rows, 0.0)).astype(BF16)
    grad_x, passed = tied(grad_x, passed)
    last = scatter_last(passed, tp_size)
    grad_side = side_gradient(side_part, d_taps, d_skip, d_heads, grad_conv_state, gain_sums)
    grad_side, last[0] = tied(grad_side, last[0])
    grad_input_gain = all_sum(grad_side[:, used], tp_index, tp_size) / input_gain.astype(F32)
    d_normed = scatter_end(kept, last)

    unit_rows, inv_rms = unit_of(block_in)
    scaled = d_normed * gain_f[None, :]
    d_block = inv_rms * (scaled - unit_rows * jnp.mean(scaled * unit_rows, axis=1, keepdims=True))
    d_input = (cot_f + d_block).astype(BF16)

    own_extras = grad_side[:, used + 1 : used + 1 + small_cols].reshape(-1)
    grads = (
        grad_input_gain,
        None,
        grad_side[:, :heads],
        grad_side[:, heads:used],
        own_extras[:inner_n].reshape(conv_inner.shape),
        own_extras[inner_n : inner_n + state_n].reshape(conv_state.shape),
        own_extras[small_count : small_count + 3 * heads].reshape(3, heads),
        own_extras[inner_n + state_n : small_count],
        grad_out.astype(F32).T,
    )
    weights = (
        input_gain,
        proj_inner,
        proj_step,
        proj_state,
        conv_inner,
        conv_state,
        head_params,
        mixer_gain,
        proj_output,
    )
    large = (1, 2, 3, 8)
    grads = list(grads)
    updated = [None] * 9
    for at in range(9):
        decay = WEIGHT_DECAY if at in large else 0.0
        rate = LEARN_RATE if at in large else LEARN_SMALL
        if at == 1:
            grads[1], *updated[1] = adam_pair(
                lambda w, g, m, v: adamw_step(w, g, m, v, WEIGHT_DECAY, LEARN_RATE),
                grad_gate,
                grad_x,
                proj_inner,
                moments[1],
                moments[10],
            )
        else:
            updated[at] = adamw_step(
                weights[at], grads[at], moments[at], moments[9 + at], decay, rate
            )
    return (
        block_out,
        d_input,
        *grads,
        *[entry[0] for entry in updated],
        *[entry[1] for entry in updated],
        *[entry[2] for entry in updated],
    )


def weight_specs():
    return (
        P("fsdp"),
        P("fsdp", None, "tp"),
        P("fsdp", "tp"),
        P("fsdp", "tp"),
        P(None, ("tp", "fsdp")),
        P(None, ("tp", "fsdp")),
        P(None, "tp"),
        P(("tp", "fsdp")),
        P("tp", "fsdp"),
    )


def solution(mesh):
    rows = P(("fsdp", "tp"), None)
    return jax.shard_map(
        body,
        mesh=mesh,
        in_specs=(rows, rows, P("fsdp", None), P("fsdp")) + weight_specs() * 3,
        out_specs=(rows, rows) + weight_specs() * 4,
        check_vma=False,
    )
```

```python
import functools
import jax
import jax.numpy as jnp
from jax import lax
from jax.experimental import pallas as pl
from jax.experimental.layout import Layout, with_layout_constraint
from jax.experimental.pallas import tpu as pltpu
from jax.sharding import PartitionSpec as P

N = 128
Q = 256
LANE = 128
BLK = 128
SLOTS = 32
UNROLL = 10
LOG2E = 1.4426950408889634
F32 = jnp.float32
BF16 = jnp.bfloat16
VMEM_CAP = 56 << 20


def mm(left, right):
    return lax.dot_general(left, right, (((1,), (0,)), ((), ())), preferred_element_type=F32)


def mm_nt(left, right):
    return lax.dot_general(left, right, (((1,), (1,)), ((), ())), preferred_element_type=F32)


def split_two(value):
    high = value.astype(BF16)
    low = (value - high.astype(F32)).astype(BF16)
    return high, low


def split_three(value):
    high = value.astype(BF16).astype(F32)
    rest = value - high
    mid = rest.astype(BF16).astype(F32)
    return high, mid, rest - mid


def as_columns(value):
    parts = split_three(value)
    stacked = jnp.concatenate(list(parts) + [jnp.zeros_like(value)], axis=0)
    return stacked.T.astype(BF16)


def lane_sums(value, table):
    parts = jnp.concatenate(split_three(value), axis=0).astype(BF16)
    sums = mm(parts, table)
    return sums[:SLOTS] + sums[SLOTS : 2 * SLOTS] + sums[2 * SLOTS :]


def iota2(shape, axis):
    return lax.broadcasted_iota(jnp.int32, shape, axis)


def step_terms(small_ref, meta_ref, hp_ref):
    on = hp_ref[:, 2:3]
    pre = (small_ref[...] + hp_ref[:, 0:1]) * on
    steps = (jnp.maximum(pre, 0.0) + jnp.log1p(jnp.exp(-jnp.abs(pre)))) * on
    upto = (iota2((Q, Q), 0) <= iota2((Q, Q), 1)).astype(BF16)
    cum = lane_sums(steps * hp_ref[:, 1:2], upto) * LOG2E
    into = jnp.exp2(cum) * meta_ref[0, 1:2, :] * on
    tail = jnp.exp2(cum[:, Q - 1 : Q] - cum) * meta_ref[0, 2:3, :] * on
    return pre, steps, cum, into, tail


def ssd_fwd_kernel(
    heads,
    raw_ref,
    small_ref,
    bc_ref,
    masks_ref,
    meta_ref,
    seg_ref,
    taps_ref,
    hp_ref,
    skip_ref,
    expand_ref,
    widen_ref,
    y_ref,
    st_ref,
    state,
    tail_rows,
    window,
    row_cum,
    scores,
    columns,
    spreads,
    wide_cum,
):
    chunk = pl.program_id(0)

    @pl.when(chunk == 0)
    def _():
        state[...] = jnp.zeros_like(state)
        tail_rows[...] = jnp.zeros_like(tail_rows)

    st_ref[0] = state[...]
    _, steps, cum, into, tail = step_terms(small_ref, meta_ref, hp_ref)
    row_cum[...] = cum
    for at, value in enumerate((cum, steps, into, tail)):
        columns[at] = as_columns(value)
    for at in range(3):
        spreads[at] = mm(columns[at + 1], expand_ref[...])
    cum_cols = jnp.concatenate([cum] * 4, axis=0).T
    for head in range(heads):
        wide_cum[:, head * LANE : (head + 1) * LANE] = jnp.broadcast_to(
            cum_cols[:, head : head + 1], (Q, LANE)
        )
    same = (seg_ref[:, 0:1] == meta_ref[0, 0:1, :]) & (iota2((Q, Q), 0) >= iota2((Q, Q), 1))
    b_turned = bc_ref[:N, :]
    c_rows = bc_ref[N:, :].astype(F32).T.astype(BF16)
    scores[...] = jnp.where(same, mm(c_rows, b_turned), 0.0)
    first = iota2((Q, LANE), 1) < LANE // 2

    def pair(index, _):
        lanes = pl.ds(pl.multiple_of(index * LANE, LANE), LANE)
        both = pl.ds(pl.multiple_of(index * 2 * LANE, 2 * LANE), 2 * LANE)
        window[0:8, :] = tail_rows[:, lanes]
        current = raw_ref[:, lanes]
        window[8 : 8 + Q, :] = current
        conv = taps_ref[4:5, lanes] + taps_ref[3:4, lanes] * current
        for offset in range(1, 4):
            conv = conv + taps_ref[3 - offset : 4 - offset, lanes] * (
                masks_ref[:, (offset - 1) * LANE : offset * LANE]
                * window[8 - offset : 8 - offset + Q, :]
            )
        vals = conv * jax.nn.sigmoid(conv)
        scaled = (vals * spreads[0, :, lanes]).astype(BF16)
        zero = jnp.zeros_like(scaled)
        own = (jnp.where(first, scaled, zero), jnp.where(first, zero, scaled))
        held = state[:, lanes]
        into_here = spreads[1, :, lanes]
        base = into_here * mm(c_rows, held.astype(BF16)) + skip_ref[0:1, lanes] * vals
        cum_cols = wide_cum[:, both]
        for low in range(0, Q, BLK):
            width = low + BLK
            total = base[low:width, :]
            for which in range(2):
                across = row_cum[pl.ds(index * 2 + which, 1), :][:, :width]
                down = cum_cols[low:width, which * LANE : (which + 1) * LANE]
                down = jnp.concatenate([down] * (width // LANE), axis=1)
                decays = jnp.exp2(jnp.minimum(down - across, 0.0))
                mixing = (decays * scores[low:width, :width]).astype(BF16)
                total = total + mm(mixing, own[which][:width, :])
            y_ref[low:width, lanes] = total
        weighted = (spreads[2, :, lanes] * scaled.astype(F32)).astype(BF16)
        state[:, lanes] = held * into_here[Q - 1 : Q, :] + mm(b_turned, weighted)
        return 0

    lax.fori_loop(0, heads // 2, pair, 0, unroll=UNROLL)
    tail_rows[...] = raw_ref[Q - 8 : Q, :]


def ssd_bwd_kernel(
    heads,
    raw_ref,
    halo_ref,
    small_ref,
    bc_ref,
    masks_ref,
    masks_next_ref,
    meta_ref,
    seg_ref,
    taps_ref,
    hp_ref,
    skip_ref,
    expand_ref,
    widen_ref,
    gather_ref,
    y_ref,
    dy_ref,
    st_ref,
    dx_ref,
    ddt_ref,
    dbc_ref,
    dtaps_ref,
    dhp_ref,
    dskip_ref,
    dstate,
    next_rows,
    carried,
    window,
    dwindow,
    row_cum,
    scores,
    dscores,
    columns,
    into_dy,
    tail_vals,
    balance_parts,
    direct_parts,
    wide_cum,
):
    chunk = pl.program_id(0)

    @pl.when(chunk == 0)
    def _():
        dstate[...] = jnp.zeros_like(dstate)
        next_rows[...] = jnp.zeros_like(next_rows)
        carried[...] = jnp.zeros_like(carried)
        dtaps_ref[...] = jnp.zeros_like(dtaps_ref)
        dhp_ref[...] = jnp.zeros_like(dhp_ref)
        dskip_ref[...] = jnp.zeros_like(dskip_ref)

    pre, steps, cum, into, tail = step_terms(small_ref, meta_ref, hp_ref)
    row_cum[...] = cum
    for at, value in enumerate((cum, steps, into, tail)):
        columns[at] = as_columns(value)
    cum_cols = jnp.concatenate([cum] * 4, axis=0).T
    for head in range(heads):
        wide_cum[:, head * LANE : (head + 1) * LANE] = jnp.broadcast_to(
            cum_cols[:, head : head + 1], (Q, LANE)
        )
    same = (seg_ref[:, 0:1] == meta_ref[0, 0:1, :]) & (iota2((Q, Q), 0) <= iota2((Q, Q), 1))
    b_rows = bc_ref[:N, :].astype(F32).T.astype(BF16)
    c_turned = bc_ref[N:, :]
    scores[...] = jnp.where(same, mm(b_rows, c_turned), 0.0)
    dscores[...] = jnp.zeros_like(dscores)
    carry_high, carry_low = split_two(carried[...])
    gather_all = gather_ref[...]
    from_next = mm(carry_high, gather_all) + mm(carry_low, gather_all)
    dstate_half = dstate[...].astype(BF16)
    first = iota2((Q, LANE), 1) < LANE // 2

    def pair(index, _):
        lanes = pl.ds(pl.multiple_of(index * LANE, LANE), LANE)
        both = pl.ds(pl.multiple_of(index * 2 * LANE, 2 * LANE), 2 * LANE)
        window[0:8, :] = halo_ref[:, lanes]
        current = raw_ref[:, lanes]
        window[8 : 8 + Q, :] = current
        conv = taps_ref[4:5, lanes] + taps_ref[3:4, lanes] * current
        for offset in range(1, 4):
            conv = conv + taps_ref[3 - offset : 4 - offset, lanes] * (
                masks_ref[:, (offset - 1) * LANE : offset * LANE]
                * window[8 - offset : 8 - offset + Q, :]
            )
        gate = jax.nn.sigmoid(conv)
        vals = conv * gate
        expand = expand_ref[:, lanes]
        step_here = mm(columns[1], expand)
        scaled = (vals * step_here).astype(BF16)
        skip = skip_ref[0:1, lanes]
        dy = dy_ref[:, lanes]
        dy_half = dy.astype(BF16)
        zero = jnp.zeros_like(scaled)
        own = (jnp.where(first, scaled, zero), jnp.where(first, zero, scaled))
        own_dy = (jnp.where(first, dy_half, zero), jnp.where(first, zero, dy_half))
        dheld = dstate[:, lanes]
        tail_here = mm(columns[3], expand)
        into_here = mm(columns[2], expand)
        base = tail_here * mm(b_rows, dheld.astype(BF16))
        cum_cols = wide_cum[:, both]
        pieces = []
        for low in range(0, Q, BLK):
            high = low + BLK
            total = base[low:high, :]
            for which in range(2):
                across = row_cum[pl.ds(index * 2 + which, 1), :][:, low:]
                down = cum_cols[low:high, which * LANE : (which + 1) * LANE]
                down = jnp.concatenate([down] * ((Q - low) // LANE), axis=1)
                decays = jnp.exp2(jnp.minimum(across - down, 0.0))
                mixing = (decays * scores[low:high, low:]).astype(BF16)
                total = total + mm(mixing, own_dy[which][low:, :])
                dmix = mm_nt(own[which][low:high, :], dy_half[low:, :])
                dscores[low:high, low:] += dmix * decays
            pieces.append(total)
        dscaled = jnp.concatenate(pieces, axis=0)
        held = st_ref[0, :, lanes]
        edy = (into_here * dy).astype(BF16)
        scaled_f = scaled.astype(F32)
        into_dy[:, lanes] = edy
        tail_vals[:, lanes] = (tail_here * scaled_f).astype(BF16)
        balance = dy_half.astype(F32) * (y_ref[:, lanes] - skip * vals) - scaled_f * dscaled
        part_high, part_low = split_two(balance)
        balance_parts[0, :, lanes] = part_high
        balance_parts[1, :, lanes] = part_low
        part_high, part_low = split_two(vals * dscaled)
        direct_parts[0, :, lanes] = part_high
        direct_parts[1, :, lanes] = part_low
        dskip_ref[0:1, lanes] += jnp.sum(dy * vals, axis=0, keepdims=True)
        dheld_new = into_here[Q - 1 : Q, :] * dheld + mm(c_turned, edy)
        dstate[:, lanes] = dheld_new
        carried[0:1, lanes] = jnp.sum(dheld_new * held, axis=0, keepdims=True)
        dvals = step_here * dscaled + skip * dy
        dconv = dvals * (gate * (1.0 + conv * (1.0 - gate)))
        dwindow[0:Q, :] = dconv
        dwindow[Q : Q + 8, :] = next_rows[:, lanes]
        next_rows[:, lanes] = dconv[0:8, :]
        dtaps_ref[4:5, lanes] += jnp.sum(dconv, axis=0, keepdims=True)
        dtaps_ref[3:4, lanes] += jnp.sum(dconv * current, axis=0, keepdims=True)
        draw = taps_ref[3:4, lanes] * dconv
        for offset in range(1, 4):
            mask = masks_ref[:, (offset - 1) * LANE : offset * LANE]
            mask_next = masks_next_ref[:, (offset - 1) * LANE : offset * LANE]
            mask_later = jnp.concatenate([mask, mask_next], axis=0)[offset : offset + Q, :]
            shifted = mask * window[8 - offset : 8 - offset + Q, :]
            dtaps_ref[3 - offset : 4 - offset, lanes] += jnp.sum(
                dconv * shifted, axis=0, keepdims=True
            )
            draw = draw + taps_ref[3 - offset : 4 - offset, lanes] * (
                mask_later * dwindow[offset : offset + Q, :]
            )
        dx_ref[:, lanes] = draw.astype(BF16)
        return 0

    lax.fori_loop(0, heads // 2, pair, 0, unroll=UNROLL)
    dscores_now = jnp.where(same, dscores[...], 0.0)
    d_b = mm_nt(tail_vals[...], dstate_half) + mm_nt(dscores_now.astype(BF16), c_turned)
    d_c = mm_nt(into_dy[...], st_ref[0].astype(BF16)) + mm(dscores_now.T.astype(BF16), b_rows)
    dbc_ref[:N, :] = d_b.T
    dbc_ref[N:, :] = d_c.T
    balance = mm(balance_parts[0], gather_all) + mm(balance_parts[1], gather_all)
    balance = balance + jnp.where(iota2((Q, LANE), 0) == Q - 1, from_next[0:1, :], 0.0)
    direct = mm(direct_parts[0], gather_all) + mm(direct_parts[1], gather_all)
    since = (iota2((Q, Q), 0) >= iota2((Q, Q), 1)).astype(BF16)
    dlogs = lane_sums(balance.T[:SLOTS], since)
    dsteps = dlogs * hp_ref[:, 1:2] + direct.T[:SLOTS]
    dsteps = dsteps * jax.nn.sigmoid(pre) * hp_ref[:, 2:3]
    ddt_ref[...] = dsteps
    dhp_ref[:, 0:1] += jnp.sum(dsteps, axis=1, keepdims=True)
    dhp_ref[:, 1:2] += jnp.sum(dlogs * steps, axis=1, keepdims=True)


def head_tables(heads):
    width = heads * (LANE // 2)
    owner = jnp.arange(width) // (LANE // 2)
    wide_owner = jnp.arange(heads * LANE) // LANE
    slot = jnp.arange(LANE)
    real = (slot < 3 * SLOTS)[:, None]
    expand = ((slot % SLOTS)[:, None] == owner[None, :]) & real
    widen = ((slot % SLOTS)[:, None] == wide_owner[None, :]) & real
    gather = owner[:, None] == slot[None, :]
    return expand.astype(BF16), widen.astype(BF16), gather.astype(BF16)


def segment_tables(segment):
    length = segment.shape[0]
    chunks = length // Q
    doc_masks = []
    for offset in range(1, 4):
        earlier = jnp.concatenate(
            [jnp.full((offset,), -1, jnp.int32), segment[: length - offset]], axis=0
        )
        doc_masks.append((earlier == segment).astype(F32))
    masks = jnp.concatenate(
        [jnp.broadcast_to(mask[:, None], (length, LANE)) for mask in doc_masks], axis=1
    )
    by_chunk = segment.reshape(chunks, Q)
    last = by_chunk[:, Q - 1]
    before = jnp.concatenate([jnp.full((1,), -1, jnp.int32), last[: chunks - 1]], axis=0)
    rows = [
        by_chunk.astype(F32),
        (by_chunk == before[:, None]).astype(F32),
        (by_chunk == last[:, None]).astype(F32),
    ]
    meta = jnp.pad(jnp.stack(rows, axis=1), ((0, 0), (0, 5), (0, 0)))
    seg_cols = jnp.broadcast_to(segment.astype(F32)[:, None], (length, LANE))
    return doc_masks, masks, meta, seg_cols


def head_columns(head_params):
    heads = head_params.shape[1]
    rates = -jnp.exp(head_params[1])
    table = jnp.stack([head_params[0], rates, jnp.ones_like(rates)], axis=1)
    return jnp.pad(table, ((0, SLOTS - heads), (0, LANE - 3)))


def time_like(seconds):
    return pl.CostEstimate(
        flops=int(seconds * 1.1e15), bytes_accessed=int(seconds * 3.4e12), transcendentals=0
    )


def full_spec(shape):
    return pl.BlockSpec(shape, lambda c: (0,) * len(shape))


def ssd_forward(raw, small, bc, tables, taps, hp, skip, spread, heads):
    length = raw.shape[0]
    width = heads * (LANE // 2)
    chunks = length // Q
    _, masks, meta, seg_cols = tables
    expand, widen, _ = spread
    return pl.pallas_call(
        functools.partial(ssd_fwd_kernel, heads),
        grid=(chunks,),
        out_shape=(
            jax.ShapeDtypeStruct((length, width), F32),
            jax.ShapeDtypeStruct((chunks, N, width), F32),
        ),
        in_specs=[
            pl.BlockSpec((Q, width), lambda c: (c, 0)),
            pl.BlockSpec((SLOTS, Q), lambda c: (0, c)),
            pl.BlockSpec((2 * N, Q), lambda c: (0, c)),
            pl.BlockSpec((Q, 3 * LANE), lambda c: (c, 0)),
            pl.BlockSpec((1, 8, Q), lambda c: (c, 0, 0)),
            pl.BlockSpec((Q, LANE), lambda c: (c, 0)),
            full_spec((8, width)),
            full_spec((SLOTS, LANE)),
            full_spec((8, width)),
            full_spec((LANE, width)),
            full_spec((LANE, heads * LANE)),
        ],
        out_specs=(
            pl.BlockSpec((Q, width), lambda c: (c, 0)),
            pl.BlockSpec((1, N, width), lambda c: (c, 0, 0)),
        ),
        scratch_shapes=[
            pltpu.VMEM((N, width), F32),
            pltpu.VMEM((8, width), F32),
            pltpu.VMEM((Q + 8, LANE), F32),
            pltpu.VMEM((SLOTS, Q), F32),
            pltpu.VMEM((Q, Q), F32),
            pltpu.VMEM((4, Q, LANE), BF16),
            pltpu.VMEM((3, Q, width), F32),
            pltpu.VMEM((Q, heads * LANE), F32),
        ],
        compiler_params=pltpu.CompilerParams(vmem_limit_bytes=VMEM_CAP),
        cost_estimate=time_like(37e-6 * length * heads / 30720),
        name="ssd_fwd",
    )(raw, small, bc, masks, meta, seg_cols, taps, hp, skip, expand, widen)


def ssd_backward(raw, small, bc, tables, taps, hp, skip, spread, y, dy, states, heads):
    length = raw.shape[0]
    width = heads * (LANE // 2)
    chunks = length // Q
    per = Q // 8
    _, masks, meta, seg_cols = tables

    def at(c):
        return chunks - 1 - c

    return pl.pallas_call(
        functools.partial(ssd_bwd_kernel, heads),
        grid=(chunks,),
        out_shape=(
            jax.ShapeDtypeStruct((length, width), BF16),
            jax.ShapeDtypeStruct((SLOTS, length), F32),
            jax.ShapeDtypeStruct((2 * N, length), F32),
            jax.ShapeDtypeStruct((8, width), F32),
            jax.ShapeDtypeStruct((SLOTS, LANE), F32),
            jax.ShapeDtypeStruct((8, width), F32),
        ),
        in_specs=[
            pl.BlockSpec((Q, width), lambda c: (at(c), 0)),
            pl.BlockSpec((8, width), lambda c: (jnp.maximum(at(c) * per - 1, 0), 0)),
            pl.BlockSpec((SLOTS, Q), lambda c: (0, at(c))),
            pl.BlockSpec((2 * N, Q), lambda c: (0, at(c))),
            pl.BlockSpec((Q, 3 * LANE), lambda c: (at(c), 0)),
            pl.BlockSpec(
                (8, 3 * LANE), lambda c: (jnp.minimum((at(c) + 1) * per, chunks * per - 1), 0)
            ),
            pl.BlockSpec((1, 8, Q), lambda c: (at(c), 0, 0)),
            pl.BlockSpec((Q, LANE), lambda c: (at(c), 0)),
            full_spec((8, width)),
            full_spec((SLOTS, LANE)),
            full_spec((8, width)),
            full_spec((LANE, width)),
            full_spec((LANE, heads * LANE)),
            full_spec((width, LANE)),
            pl.BlockSpec((Q, width), lambda c: (at(c), 0)),
            pl.BlockSpec((Q, width), lambda c: (at(c), 0)),
            pl.BlockSpec((1, N, width), lambda c: (at(c), 0, 0)),
        ],
        out_specs=(
            pl.BlockSpec((Q, width), lambda c: (at(c), 0)),
            pl.BlockSpec((SLOTS, Q), lambda c: (0, at(c))),
            pl.BlockSpec((2 * N, Q), lambda c: (0, at(c))),
            full_spec((8, width)),
            full_spec((SLOTS, LANE)),
            full_spec((8, width)),
        ),
        scratch_shapes=[
            pltpu.VMEM((N, width), F32),
            pltpu.VMEM((8, width), F32),
            pltpu.VMEM((8, width), F32),
            pltpu.VMEM((Q + 8, LANE), F32),
            pltpu.VMEM((Q + 8, LANE), F32),
            pltpu.VMEM((SLOTS, Q), F32),
            pltpu.VMEM((Q, Q), F32),
            pltpu.VMEM((Q, Q), F32),
            pltpu.VMEM((4, Q, LANE), BF16),
            pltpu.VMEM((Q, width), BF16),
            pltpu.VMEM((Q, width), BF16),
            pltpu.VMEM((2, Q, width), BF16),
            pltpu.VMEM((2, Q, width), BF16),
            pltpu.VMEM((Q, heads * LANE), F32),
        ],
        compiler_params=pltpu.CompilerParams(vmem_limit_bytes=VMEM_CAP),
        cost_estimate=time_like(69e-6 * length * heads / 30720),
        name="ssd_bwd",
    )(
        raw,
        raw,
        small,
        bc,
        masks,
        masks,
        meta,
        seg_cols,
        taps,
        hp,
        skip,
        *spread,
        y,
        dy,
        states,
    )


def dn_kernel(count, rows, at_ref, *refs):
    dz, dx, side, normed = (refs[k * count : (k + 1) * count] for k in range(4))
    gate_ref, inner_ref, out_ref, sums_ref = refs[4 * count : 4 * count + 4]
    turned = refs[4 * count + 4]
    width = dz[0].shape[1]

    @pl.when(pl.program_id(0) == 0)
    def _():
        for k in range(count):
            turned[k * rows : (k + 1) * rows, :] = side[k][...].T.astype(BF16)

    gate = gate_ref[...]
    inner = inner_ref[:, :width]
    last = inner_ref[:, width:]
    sums = None
    for k in range(count):
        at = slice(k * rows, (k + 1) * rows)
        total = mm_nt(dz[k][...], gate) + mm_nt(dx[k][...], inner) + mm_nt(turned[at, :], last)
        out_ref[at, :] = total.astype(BF16)
        part = jnp.sum(total * normed[k][...].astype(F32), axis=0, keepdims=True)
        sums = part if sums is None else sums + part
    sums_ref[0:1, :] = sums


def d_normed_blocks(d_z, d_x, d_side, gate_all, x_all, normed, blocks, which, rows, tile=256):
    length, width = d_z.shape
    count = blocks.shape[0]
    half = gate_all.shape[0] // 2
    first = which * half // tile

    def rows_of(k):
        return pl.BlockSpec((rows, width), lambda n, at, k=k: (at[k], 0))

    def cols_of(k):
        return pl.BlockSpec((LANE, rows), lambda n, at, k=k: (0, at[k]))

    def tile_of(k):
        return pl.BlockSpec((rows, tile), lambda n, at, k=k: (at[k], n + first))

    each = range(count)
    return pl.pallas_call(
        functools.partial(dn_kernel, count, rows),
        grid_spec=pltpu.PrefetchScalarGridSpec(
            num_scalar_prefetch=1,
            grid=(half // tile,),
            in_specs=[rows_of(k) for k in each]
            + [rows_of(k) for k in each]
            + [cols_of(k) for k in each]
            + [tile_of(k) for k in each]
            + [
                pl.BlockSpec((tile, width), lambda n, at: (n + first, 0)),
                pl.BlockSpec((tile, width + LANE), lambda n, at: (n + first, 0)),
            ],
            out_specs=(
                pl.BlockSpec((count * rows, tile), lambda n, at: (0, n)),
                pl.BlockSpec((8, tile), lambda n, at: (0, n)),
            ),
            scratch_shapes=[pltpu.VMEM((count * rows, LANE), BF16)],
        ),
        out_shape=(
            jax.ShapeDtypeStruct((count * rows, half), BF16),
            jax.ShapeDtypeStruct((8, half), F32),
        ),
        compiler_params=pltpu.CompilerParams(vmem_limit_bytes=VMEM_CAP),
        cost_estimate=time_like(1e-7),
        name="d_normed",
    )(
        blocks,
        *([d_z] * count),
        *([d_x] * count),
        *([d_side] * count),
        *([normed] * count),
        gate_all,
        x_all,
    )


def adam_kernel(step, gate_ref, inner_ref, weight_ref, first_ref, second_ref, *outs):
    grad_out, weight_out, first_out, second_out = outs
    for part, grad_ref in ((0, gate_ref), (1, inner_ref)):
        grad = grad_ref[...].astype(F32)
        new_weight, new_first, new_second = step(
            weight_ref[:, part, :], grad, first_ref[:, part, :], second_ref[:, part, :]
        )
        grad_out[:, part, :] = grad
        weight_out[:, part, :] = new_weight
        first_out[:, part, :] = new_first
        second_out[:, part, :] = new_second


def adam_pair(step, grad_gate, grad_inner, weight, first, second, rows=40):
    shard, _, width = weight.shape
    deep = pl.BlockSpec((rows, 2, width), lambda n: (n, 0, 0))
    flat = pl.BlockSpec((rows, width), lambda n: (n, 0))
    like = jax.ShapeDtypeStruct(weight.shape, F32)
    return pl.pallas_call(
        functools.partial(adam_kernel, step),
        grid=(shard // rows,),
        out_shape=(like, jax.ShapeDtypeStruct(weight.shape, weight.dtype), like, like),
        in_specs=[flat, flat, deep, deep, deep],
        out_specs=(deep,) * 4,
        compiler_params=pltpu.CompilerParams(vmem_limit_bytes=VMEM_CAP),
        cost_estimate=pl.CostEstimate(flops=1000, bytes_accessed=1000, transcendentals=0),
        name="adam_pair",
    )(grad_gate, grad_inner, weight, first, second)


def product_kernel(left_ref, right_ref, out_ref):
    out_ref[...] = mm(left_ref[...], right_ref[...])


def gate_kernel(left_ref, right_ref, mixed_ref, z_ref, gated_ref, sums_ref):
    z_raw = mm(left_ref[...], right_ref[...])
    gated = mixed_ref[...] * (z_raw * jax.nn.sigmoid(z_raw))
    z_ref[...] = z_raw
    gated_ref[...] = gated
    sums = jnp.sum(gated * gated, axis=1, keepdims=True)
    sums_ref[...] = jnp.broadcast_to(sums, (sums.shape[0], LANE)).T[:8]


def output_kernel(left_ref, right_ref, grad_ref, first_ref, second_ref, sums_ref):
    half = first_ref.shape[1]
    total = None
    for at, out_ref in ((0, first_ref), (half, second_ref)):
        part = mm_nt(left_ref[...], right_ref[at : at + half, :])
        out_ref[...] = part.astype(BF16)
        sums = jnp.sum(part * grad_ref[:, at : at + half].astype(F32), axis=1, keepdims=True)
        total = sums if total is None else total + sums
    sums_ref[...] = jnp.broadcast_to(total, (total.shape[0], LANE)).T[:8]


def gate_grad_kernel(
    left_ref, right_ref, z_ref, mixed_ref, gain_ref, inv_ref, mean_ref, dy_ref, dz_ref, dgain_ref
):
    @pl.when(pl.program_id(0) == 0)
    def _():
        dgain_ref[...] = jnp.zeros_like(dgain_ref)

    d_ng = mm(left_ref[...], right_ref[...])
    z_raw = z_ref[...]
    mixed = mixed_ref[...]
    inv = inv_ref[...]
    sig = jax.nn.sigmoid(z_raw)
    gate_act = z_raw * sig
    unit = mixed * gate_act * inv
    dgain_ref[0:1, :] += jnp.sum(d_ng * unit, axis=0, keepdims=True)
    d_gated = inv * (d_ng * gain_ref[0:1, :] - unit * mean_ref[...])
    dy_ref[...] = d_gated * gate_act
    dz_ref[...] = (d_gated * mixed * sig * (1.0 + z_raw * (1.0 - sig))).astype(BF16)


def row_call(kernel, name, seconds, length, rows, ins, outs):
    def spec(shape, split):
        if split == "rows":
            return pl.BlockSpec((rows,) + shape, lambda m: (m, 0))
        if split == "lanes":
            return pl.BlockSpec(shape + (rows,), lambda m: (0, m))
        return pl.BlockSpec(shape, lambda m: (0, 0))

    return pl.pallas_call(
        kernel,
        grid=(length // rows,),
        out_shape=tuple(jax.ShapeDtypeStruct(full, kind) for full, kind, _, _ in outs),
        in_specs=[spec(shape, split) for _, shape, split in ins],
        out_specs=tuple(spec(shape, split) for _, _, shape, split in outs),
        compiler_params=pltpu.CompilerParams(vmem_limit_bytes=VMEM_CAP),
        cost_estimate=time_like(seconds),
        name=name,
    )(*[array for array, _, _ in ins])


def inner_product(normed, x_all, width, rows=256):
    length, model = normed.shape
    return row_call(
        product_kernel,
        "inner_product",
        14e-6,
        length,
        rows,
        [(normed, (model,), "rows"), (x_all, (model, width), None)],
        [((length, width), F32, (width,), "rows")],
    )[0]


def gate_product(normed, gate_all, mixed, rows=256):
    length, model = normed.shape
    width = gate_all.shape[1]
    wide = ((length, width), F32, (width,), "rows")
    z_raw, gated, sums = row_call(
        gate_kernel,
        "gate_product",
        16e-6,
        length,
        rows,
        [(normed, (model,), "rows"), (gate_all, (model, width), None), (mixed, (width,), "rows")],
        [wide, wide, ((8, length), F32, (8,), "lanes")],
    )
    return z_raw, gated, sums[0]


def output_product(normed_gated, out_all, group_grad, rows=256):
    length, width = normed_gated.shape
    model = out_all.shape[0]
    part = ((length, model // 2), BF16, (model // 2,), "rows")
    left, right, sums = row_call(
        output_kernel,
        "output_product",
        16e-6,
        length,
        rows,
        [
            (normed_gated, (width,), "rows"),
            (out_all, (model, width), None),
            (group_grad, (model,), "rows"),
        ],
        [part, part, ((8, length), F32, (8,), "lanes")],
    )
    return left, right, sums[0]


def gate_gradient(group_grad, out_all, z_raw, mixed, gain, inv, mean, rows=256):
    length, model = group_grad.shape
    width = out_all.shape[1]
    return row_call(
        gate_grad_kernel,
        "gate_gradient",
        18e-6,
        length,
        rows,
        [
            (group_grad, (model,), "rows"),
            (out_all, (model, width), None),
            (z_raw, (width,), "rows"),
            (mixed, (width,), "rows"),
            (gain, (8, width), None),
            (inv, (1,), "rows"),
            (mean, (1,), "rows"),
        ],
        [
            ((length, width), F32, (width,), "rows"),
            ((length, width), BF16, (width,), "rows"),
            ((8, width), F32, (8, width), None),
        ],
    )

DI = 5120
STEP = 3
NORM_EPS = 1e-05
BETA_ONE = 0.9
BETA_TWO = 0.95
LEARN_RATE = 0.004
LEARN_SMALL = 0.15
WEIGHT_DECAY = 0.1
ADAM_EPS = 1e-08


def by_rows(value):
    return with_layout_constraint(value, Layout(major_to_minor=(0, 1)))


def silu_act(values):
    return values * jax.nn.sigmoid(values)


def later(row, offset):
    return jnp.pad(row, ((0, 0), (offset, 0)))[:, : row.shape[1]]


def state_act(raw_cols, conv_taps, doc_masks):
    conv = conv_taps[4][:, None] + conv_taps[3][:, None] * raw_cols
    for offset in range(1, 4):
        conv = conv + conv_taps[3 - offset][:, None] * (
            doc_masks[offset - 1][None, :] * later(raw_cols, offset)
        )
    return silu_act(conv)


def contract_rows(left_mat, right_mat):
    return lax.dot_general(
        left_mat, right_mat, (((0,), (0,)), ((), ())), preferred_element_type=F32
    )


def adamw_step(weight, gradient, first_moment, second_moment, decay_factor, learn_rate):
    new_first = BETA_ONE * first_moment + (1.0 - BETA_ONE) * gradient
    new_second = BETA_TWO * second_moment + (1.0 - BETA_TWO) * gradient * gradient
    first_hat = new_first / (1.0 - BETA_ONE**STEP)
    second_hat = new_second / (1.0 - BETA_TWO**STEP)
    weight_f = weight.astype(F32)
    updated = weight_f - learn_rate * (
        first_hat / (jnp.sqrt(second_hat) + ADAM_EPS) + decay_factor * weight_f
    )
    return (updated.astype(weight.dtype), new_first, new_second)


def swap(value, distance, size):
    return lax.ppermute(value, "tp", [(at, at ^ distance) for at in range(size)])


def tied(*values):
    return lax.optimization_barrier(values)


def gather_parts(value, size, near_done):
    if size != 4:
        one, *others = near_done(swap(value, 1, size))
        return [value, one] + [swap(value, k, size) for k in range(2, size)], *others
    half = value.shape[0] // 2
    one, two = swap(value, 1, size), swap(value, 2, size)
    one, *others = near_done(one)
    far = jnp.concatenate([swap(two[:half], 1, size), swap(one[half:], 2, size)], axis=0)
    return [value, one, two, far], *others


def scatter_start(left, right, rows, index, size):
    def block(value, distance):
        return lax.dynamic_slice_in_dim(value, (index ^ distance) * rows, rows, 0)

    sent, kept = [], []
    for half, near in ((left, 1), (right, 2)):
        if size == 4:
            pair = jnp.concatenate([block(half, 3), block(half, near)], axis=0)
            sent.append(swap(pair, near, size))
            kept.append((block(half, 3 - near), block(half, 0)))
        else:
            sent.append([swap(block(half, k), k, size) for k in range(1, size)])
            kept.append(block(half, 0))
    return sent, kept


def scatter_middle(sent, kept, rows, size):
    if size != 4:
        return sent, [(one,) for one in kept]
    passed = [
        (kept[at][0].astype(F32) + sent[at][:rows].astype(F32)).astype(BF16) for at in range(2)
    ]
    return passed, [(kept[at][1], sent[at][rows:]) for at in range(2)]


def scatter_last(passed, size):
    if size != 4:
        return passed[0] + passed[1]
    return [swap(passed[0], 2, size), swap(passed[1], 1, size)]


def scatter_end(own, last):
    each = len(last) // 2
    totals = []
    for at in range(2):
        total = own[at][0].astype(F32)
        for piece in own[at][1:]:
            total = total + piece.astype(F32)
        for piece in last[at * each : (at + 1) * each]:
            total = total + piece.astype(F32)
        totals.append(total)
    return jnp.concatenate(totals, axis=1)


def row_sum(value, size):
    total = value
    for distance in range(1, size):
        total = total + swap(value, distance, size)
    return total


def all_sum(value, index, size):
    terms = jnp.zeros((size,) + value.shape, value.dtype)
    for distance in range(size):
        piece = value if distance == 0 else swap(value, distance, size)
        terms = lax.dynamic_update_slice(terms, piece[None], (index ^ distance, jnp.int32(0)))
    return jnp.sum(terms, axis=0)


def fsdp_swap(value, distance, size):
    return lax.ppermute(value, "fsdp", [(at, at ^ distance) for at in range(size)])


def gather_by_swaps(value, index, size):
    whole = jnp.zeros((size,) + value.shape, value.dtype)
    for distance in range(size):
        piece = value if distance == 0 else fsdp_swap(value, distance, size)
        whole = lax.dynamic_update_slice(whole, piece[None], (index ^ distance, jnp.int32(0)))
    return whole


def pair_sum(value, index, size):
    blocks = value.reshape(size // 2, 2, value.shape[0] // size, value.shape[1])
    core = index % 2
    away = lax.dynamic_slice_in_dim(blocks, 1 - core, 1, 1)[:, 0]
    own = lax.dynamic_slice_in_dim(blocks, core, 1, 1)[:, 0]
    return (own.astype(F32) + fsdp_swap(away, 1, size).astype(F32)).astype(value.dtype)


def chip_scatter(value, size):
    groups = [list(range(core, size, 2)) for core in range(2)]
    flat = value.reshape(value.shape[0] * value.shape[1], value.shape[2])
    return lax.psum_scatter(
        flat, "fsdp", scatter_dimension=0, axis_index_groups=groups, tiled=True
    )


def chip_sum(value, index, size, after):
    chip = index // 2

    def block(distance):
        return lax.dynamic_slice_in_dim(value, chip ^ distance, 1, 0)[0]

    pieces = [fsdp_swap(block(k), 2 * k, size) for k in range(1, size // 2)]
    pieces, after = tied(pieces, after)
    return sum(pieces, block(0)), after


def pad_cols(value, width):
    return jnp.pad(value, ((0, 0), (0, width - value.shape[1])))


def body(
    block_in,
    cotangent,
    segment_ids,
    group_fill,
    input_gain,
    proj_inner,
    proj_step,
    proj_state,
    conv_inner,
    conv_state,
    head_params,
    mixer_gain,
    proj_output,
    *moments,
):
    tp_size = lax.axis_size("tp")
    fsdp_size = lax.axis_size("fsdp")
    tp_index = lax.axis_index("tp")
    fsdp_index = lax.axis_index("fsdp")
    own_rows, model = block_in.shape
    group_rows = own_rows * tp_size
    shard, _, width = proj_inner.shape
    heads = proj_step.shape[1]
    state_cols = proj_state.shape[1]
    segment = segment_ids[0]
    filled = group_fill[0]

    small_values = jnp.concatenate(
        [input_gain, conv_inner.reshape(-1), conv_state.reshape(-1), mixer_gain], axis=0
    )
    inner_n, state_n = conv_inner.size, conv_state.size
    small_count = inner_n + state_n + mixer_gain.size
    small_cols = -(-(small_count + 3 * heads) // shard)
    used = heads + state_cols
    side = pad_cols(jnp.concatenate([proj_step, proj_state], axis=1), LANE)
    (inner_halves,) = tied(proj_inner.transpose(1, 0, 2))
    x_local = jnp.concatenate([inner_halves[1], side], axis=1)
    x_all = lax.all_gather(x_local, "fsdp", axis=0, tiled=True)
    gate_all = lax.all_gather(inner_halves[0], "fsdp", axis=0, tiled=True)
    small_all = lax.dynamic_update_slice(
        jnp.zeros((fsdp_size, small_values.size), BF16),
        small_values[None],
        (fsdp_index, jnp.int32(0)),
    )
    distance = 1
    while distance < fsdp_size:
        small_all = small_all + fsdp_swap(small_all, distance, fsdp_size)
        distance *= 2
    gain_f = small_all[:, :shard].reshape(model).astype(F32)
    extras = small_all[:, shard:]

    def from_owners(flat, rows):
        return flat.reshape(fsdp_size, rows, -1).transpose(1, 0, 2).reshape(rows, -1).astype(F32)

    taps_inner = from_owners(extras[:, :inner_n], 5)
    taps_state = from_owners(extras[:, inner_n : inner_n + state_n], 5)
    mixer_f = from_owners(extras[:, inner_n + state_n : small_count], 1)[0]
    taps8 = jnp.pad(taps_inner, ((0, 3), (0, 0)))
    mixer8 = jnp.broadcast_to(mixer_f[None, :], (8, width))
    spread = head_tables(heads)
    tables = segment_tables(segment)
    doc_masks = tables[0]
    hp8 = head_columns(head_params)
    skip8 = jnp.broadcast_to(jnp.repeat(head_params[2], LANE // 2)[None, :], (8, width))
    positions = tp_index * own_rows + jnp.arange(own_rows, dtype=jnp.int32)
    live_rows = (positions < filled)[:, None]
    block_f = block_in.astype(F32)
    cot_f = cotangent.astype(F32)
    own_grad = jnp.where(live_rows, cot_f, 0.0).astype(BF16)
    blank = jnp.zeros((group_rows, model), BF16)

    def unit_of(rows):
        rows_f = rows.astype(F32)
        scale = lax.rsqrt(jnp.mean(rows_f * rows_f, axis=1, keepdims=True) + NORM_EPS)
        return rows_f * scale, scale

    def normed_of(rows):
        return (unit_of(rows)[0] * gain_f[None, :]).astype(BF16)

    def put(whole, part, distance):
        return lax.dynamic_update_slice(
            whole, part, ((tp_index ^ distance) * own_rows, jnp.int32(0))
        )

    started = put(blank, normed_of(block_in), 0)

    def near_done(one):
        return tied(one, started, own_grad, taps8, taps_state, mixer8, hp8, skip8, *tables[1:])

    row_parts, started, own_grad, taps8, taps_state, mixer8, hp8, skip8, *late = gather_parts(
        block_in, tp_size, near_done
    )
    tables = (doc_masks, *late)
    row_parts = [by_rows(part) for part in row_parts]
    own_grad, *row_parts = tied(own_grad, *row_parts)
    near = min(3, tp_size)
    grad_parts = [by_rows(own_grad)] + [swap(own_grad, k, tp_size) for k in range(1, near)]

    side_all = x_all[:, width:]
    normed = started
    for distance in range(1, tp_size - 1):
        normed = put(normed, normed_of(row_parts[distance]), distance)
    far_rows, normed = tied(row_parts[-1], normed)
    normed = by_rows(put(normed, normed_of(far_rows), tp_size - 1))
    small = lax.dot_general(
        side_all, normed, (((0,), (1,)), ((), ())), preferred_element_type=F32
    )
    raw = inner_product(normed, x_all, width)
    state_vals, state_back = jax.vjp(
        lambda raw_cols, conv_taps: state_act(raw_cols, conv_taps, doc_masks),
        small[heads:used],
        taps_state,
    )
    state_local = state_vals.astype(BF16)
    bc = jnp.zeros((tp_size * state_cols, group_rows), BF16)
    for k in range(tp_size):
        piece = state_local if k == 0 else swap(state_local, k, tp_size)
        bc = lax.dynamic_update_slice(bc, piece, ((tp_index ^ k) * state_cols, jnp.int32(0)))
    own_grad, bc, out_local = tied(own_grad, bc, proj_output.T)
    out_all = lax.all_gather(out_local, "fsdp", axis=0, tiled=True)
    grad_parts += [swap(own_grad, k, tp_size) for k in range(near, tp_size)]
    mixed, states = ssd_forward(raw, small, bc, tables, taps8, hp8, skip8, spread, heads)

    z_raw, gated, square_sum = gate_product(normed, gate_all, mixed)
    square_sum, *grad_parts = tied(square_sum, *grad_parts)
    square_sum = row_sum(square_sum, tp_size)
    group_grad = jnp.zeros((group_rows, model), BF16)
    for distance in range(tp_size):
        group_grad = put(group_grad, grad_parts[distance], distance)
    group_grad = by_rows(group_grad)
    inv_gate = lax.rsqrt(square_sum / DI + NORM_EPS)[:, None]
    normed_gated = (gated * inv_gate * mixer8[0:1]).astype(BF16)
    sum_out = pair_sum(
        contract_rows(group_grad, normed_gated).astype(BF16), fsdp_index, fsdp_size
    )
    half = model // 2
    normed_gated, sum_out = tied(normed_gated, sum_out)
    grad_out = chip_scatter(sum_out, fsdp_size)
    mixed_left, mixed_right, inner_sum = output_product(normed_gated, out_all, group_grad)
    inner_sum = row_sum(inner_sum, tp_size)
    mixed_sent, mixed_kept = scatter_start(mixed_left, mixed_right, own_rows, tp_index, tp_size)

    inner_mean = inner_sum[:, None] / DI
    d_mixed, d_z, grad_mixer = gate_gradient(
        group_grad, out_all, z_raw, mixed, mixer8, inv_gate, inner_mean
    )
    grad_mixer = grad_mixer[0]
    part_gate, mixed_sent = tied(contract_rows(normed, d_z).astype(BF16), mixed_sent)
    sum_gate = pair_sum(part_gate, fsdp_index, fsdp_size)
    mixed_passed, mixed_kept = scatter_middle(mixed_sent, mixed_kept, own_rows, tp_size)
    sum_gate, grad_out = tied(sum_gate, grad_out)

    d_mixed, sum_gate, mixed_passed = tied(d_mixed, sum_gate, mixed_passed)
    mixed_last = scatter_last(mixed_passed, tp_size)
    grad_gate = chip_scatter(sum_gate, fsdp_size)
    d_x, d_dt, d_bc, d_taps, d_heads, d_skip = ssd_backward(
        raw, small, bc, tables, taps8, hp8, skip8, spread, mixed, d_mixed, states, heads
    )
    def state_block(distance):
        return lax.dynamic_slice_in_dim(d_bc, (tp_index ^ distance) * state_cols, state_cols, 0)

    state_parts = [state_block(0)]
    state_parts += [swap(state_block(k), k, tp_size) for k in range(1, tp_size)]
    part_x, mixed_last, grad_gate, *state_parts = tied(
        contract_rows(normed, d_x).astype(BF16), mixed_last, grad_gate, *state_parts
    )
    sum_x = pair_sum(part_x, fsdp_index, fsdp_size)

    d_state_raw, grad_conv_state = state_back(sum(state_parts[1:], state_parts[0]).astype(F32))
    d_side = jnp.concatenate([d_dt[:heads], d_state_raw], axis=0)
    d_side = jnp.pad(d_side, ((0, LANE - used), (0, 0)))

    four = tp_size == 4
    side_part = lax.dot_general(
        normed, d_side.astype(BF16), (((0,), (1,)), ((), ())), preferred_element_type=F32
    )

    def side_gradient(side_part, d_taps, d_skip, d_heads, grad_conv_state, gain_sums, after):
        grad_head = jnp.stack(
            [
                d_heads[:heads, 0],
                hp8[:heads, 1] * d_heads[:heads, 1],
                jnp.sum(d_skip[0].reshape(heads, LANE // 2), axis=1),
            ],
            axis=0,
        )

        def by_owner(value):
            rows = value.shape[0]
            return value.reshape(rows, fsdp_size, -1).transpose(1, 0, 2).reshape(fsdp_size, -1)

        grad_extras = jnp.concatenate(
            [
                by_owner(d_taps[:5]),
                by_owner(grad_conv_state),
                by_owner(grad_mixer[None, :]),
                jnp.broadcast_to(grad_head.reshape(1, -1), (fsdp_size, 3 * heads)),
            ],
            axis=1,
        )
        grad_extras = pad_cols(grad_extras, small_cols * shard).reshape(fsdp_size * shard, small_cols)
        grad_extras = jnp.concatenate([gain_sums[:, None], grad_extras], axis=1)
        side_part = side_part + jnp.pad(
            grad_extras, ((0, 0), (used, LANE - used - 1 - small_cols))
        )
        side_part = pair_sum(side_part, fsdp_index, fsdp_size)
        return chip_sum(side_part, fsdp_index, fsdp_size, after)

    def d_normed_of(distances, which):
        return d_normed_blocks(
            d_z, d_x, d_side, gate_all, x_all, normed, tp_index ^ jnp.array(distances), which, own_rows
        )

    if four:
        left_away, gains_one = d_normed_of([3, 1], 0)
        gains_one, sum_x = tied(gains_one, sum_x)
        right_away, gains_two = d_normed_of([3, 2], 1)
        gains_two, mixed_last, d_taps, d_skip, d_heads, grad_conv_state = tied(
            gains_two, mixed_last, d_taps, d_skip, d_heads, grad_conv_state
        )
        sent = [swap(left_away, 1, 4), swap(right_away, 2, 4)]
        left_kept, gains_three = d_normed_of([2, 0], 0)
        mixed_rows = scatter_end(mixed_kept, mixed_last)
        block_out = (block_f + jnp.where(live_rows, mixed_rows, 0.0)).astype(BF16)
        sent[0], d_side_late, side_part, grad_out = tied(sent[0], d_side, side_part, grad_out)
        right_kept, gains_four = d_normed_blocks(
            d_z, d_x, d_side_late, gate_all, x_all, normed, tp_index ^ jnp.array([1, 0]), 1, own_rows
        )
        kept = [
            (left_kept[:own_rows], left_kept[own_rows:]),
            (right_kept[:own_rows], right_kept[own_rows:]),
        ]
        gain_sums = jnp.concatenate([gains_one + gains_three, gains_two + gains_four], axis=1)[0]
    else:
        mixed_rows = scatter_end(mixed_kept, mixed_last)
        block_out = (block_f + jnp.where(live_rows, mixed_rows, 0.0)).astype(BF16)
        left, gains_one = d_normed_of(list(range(tp_size)), 0)
        right, gains_two = d_normed_of(list(range(tp_size)), 1)
        sent = [
            [
                swap(part[k * own_rows : (k + 1) * own_rows], k, tp_size)
                for k in range(1, tp_size)
            ]
            for part in (left, right)
        ]
        kept = [left[:own_rows], right[:own_rows]]
        gain_sums = jnp.concatenate([gains_one, gains_two], axis=1)[0]
    grad_x = chip_scatter(sum_x, fsdp_size)
    passed, kept = scatter_middle(sent, kept, own_rows, tp_size)
    grad_x, passed = tied(grad_x, passed)
    last = scatter_last(passed, tp_size)
    pair = adam_pair(
        lambda w, g, m, v: adamw_step(w, g, m, v, WEIGHT_DECAY, LEARN_RATE),
        grad_gate,
        grad_x,
        proj_inner,
        moments[1],
        moments[10],
    )
    kept, last = tied(kept, last)
    grad_side, pair = side_gradient(
        side_part, d_taps, d_skip, d_heads, grad_conv_state, gain_sums, pair
    )
    grad_side, last[0] = tied(grad_side, last[0])
    grad_input_gain = all_sum(grad_side[:, used], tp_index, tp_size) / input_gain.astype(F32)
    d_normed = scatter_end(kept, last)

    unit_rows, inv_rms = unit_of(block_in)
    scaled = d_normed * gain_f[None, :]
    d_block = inv_rms * (scaled - unit_rows * jnp.mean(scaled * unit_rows, axis=1, keepdims=True))
    d_input = (cot_f + d_block).astype(BF16)

    own_extras = grad_side[:, used + 1 : used + 1 + small_cols].reshape(-1)
    grads = (
        grad_input_gain,
        None,
        grad_side[:, :heads],
        grad_side[:, heads:used],
        own_extras[:inner_n].reshape(conv_inner.shape),
        own_extras[inner_n : inner_n + state_n].reshape(conv_state.shape),
        own_extras[small_count : small_count + 3 * heads].reshape(3, heads),
        own_extras[inner_n + state_n : small_count],
        grad_out.astype(F32).T,
    )
    weights = (
        input_gain,
        proj_inner,
        proj_step,
        proj_state,
        conv_inner,
        conv_state,
        head_params,
        mixer_gain,
        proj_output,
    )
    large = (1, 2, 3, 8)
    grads = list(grads)
    updated = [None] * 9
    for at in range(9):
        decay = WEIGHT_DECAY if at in large else 0.0
        rate = LEARN_RATE if at in large else LEARN_SMALL
        if at == 1:
            grads[1], *updated[1] = pair
        else:
            updated[at] = adamw_step(
                weights[at], grads[at], moments[at], moments[9 + at], decay, rate
            )
    return (
        block_out,
        d_input,
        *grads,
        *[entry[0] for entry in updated],
        *[entry[1] for entry in updated],
        *[entry[2] for entry in updated],
    )


def weight_specs():
    return (
        P("fsdp"),
        P("fsdp", None, "tp"),
        P("fsdp", "tp"),
        P("fsdp", "tp"),
        P(None, ("tp", "fsdp")),
        P(None, ("tp", "fsdp")),
        P(None, "tp"),
        P(("tp", "fsdp")),
        P("tp", "fsdp"),
    )


def solution(mesh):
    rows = P(("fsdp", "tp"), None)
    return jax.shard_map(
        body,
        mesh=mesh,
        in_specs=(rows, rows, P("fsdp", None), P("fsdp")) + weight_specs() * 3,
        out_specs=(rows, rows) + weight_specs() * 4,
        check_vma=False,
    )
```

```python
import functools
import jax
import jax.numpy as jnp
from jax import lax
from jax.experimental import pallas as pl
from jax.experimental.layout import Layout, with_layout_constraint
from jax.experimental.pallas import tpu as pltpu
from jax.sharding import PartitionSpec as P

N = 128
Q = 256
LANE = 128
BLK = 128
SLOTS = 32
UNROLL = 10
LOG2E = 1.4426950408889634
F32 = jnp.float32
BF16 = jnp.bfloat16
VMEM_CAP = 56 << 20


def mm(left, right):
    return lax.dot_general(left, right, (((1,), (0,)), ((), ())), preferred_element_type=F32)


def mm_nt(left, right):
    return lax.dot_general(left, right, (((1,), (1,)), ((), ())), preferred_element_type=F32)


def split_two(value):
    high = value.astype(BF16)
    low = (value - high.astype(F32)).astype(BF16)
    return high, low


def split_three(value):
    high = value.astype(BF16).astype(F32)
    rest = value - high
    mid = rest.astype(BF16).astype(F32)
    return high, mid, rest - mid


def as_columns(value):
    parts = split_three(value)
    stacked = jnp.concatenate(list(parts) + [jnp.zeros_like(value)], axis=0)
    return stacked.T.astype(BF16)


def lane_sums(value, table):
    parts = jnp.concatenate(split_three(value), axis=0).astype(BF16)
    sums = mm(parts, table)
    return sums[:SLOTS] + sums[SLOTS : 2 * SLOTS] + sums[2 * SLOTS :]


def iota2(shape, axis):
    return lax.broadcasted_iota(jnp.int32, shape, axis)


def step_terms(small_ref, meta_ref, hp_ref):
    on = hp_ref[:, 2:3]
    pre = (small_ref[...] + hp_ref[:, 0:1]) * on
    steps = (jnp.maximum(pre, 0.0) + jnp.log1p(jnp.exp(-jnp.abs(pre)))) * on
    upto = (iota2((Q, Q), 0) <= iota2((Q, Q), 1)).astype(BF16)
    cum = lane_sums(steps * hp_ref[:, 1:2], upto) * LOG2E
    into = jnp.exp2(cum) * meta_ref[0, 1:2, :] * on
    tail = jnp.exp2(cum[:, Q - 1 : Q] - cum) * meta_ref[0, 2:3, :] * on
    return pre, steps, cum, into, tail


def ssd_fwd_kernel(
    heads,
    raw_ref,
    small_ref,
    bc_ref,
    masks_ref,
    meta_ref,
    seg_ref,
    taps_ref,
    hp_ref,
    skip_ref,
    expand_ref,
    widen_ref,
    y_ref,
    st_ref,
    state,
    tail_rows,
    window,
    row_cum,
    scores,
    columns,
    spreads,
    wide_cum,
):
    chunk = pl.program_id(0)

    @pl.when(chunk == 0)
    def _():
        state[...] = jnp.zeros_like(state)
        tail_rows[...] = jnp.zeros_like(tail_rows)

    st_ref[0] = state[...]
    _, steps, cum, into, tail = step_terms(small_ref, meta_ref, hp_ref)
    row_cum[...] = cum
    for at, value in enumerate((cum, steps, into, tail)):
        columns[at] = as_columns(value)
    for at in range(3):
        spreads[at] = mm(columns[at + 1], expand_ref[...])
    cum_cols = jnp.concatenate([cum] * 4, axis=0).T
    for head in range(heads):
        wide_cum[:, head * LANE : (head + 1) * LANE] = jnp.broadcast_to(
            cum_cols[:, head : head + 1], (Q, LANE)
        )
    same = (seg_ref[:, 0:1] == meta_ref[0, 0:1, :]) & (iota2((Q, Q), 0) >= iota2((Q, Q), 1))
    b_turned = bc_ref[:N, :]
    c_rows = bc_ref[N:, :].astype(F32).T.astype(BF16)
    scores[...] = jnp.where(same, mm(c_rows, b_turned), 0.0)
    first = iota2((Q, LANE), 1) < LANE // 2

    def pair(index, _):
        lanes = pl.ds(pl.multiple_of(index * LANE, LANE), LANE)
        both = pl.ds(pl.multiple_of(index * 2 * LANE, 2 * LANE), 2 * LANE)
        window[0:8, :] = tail_rows[:, lanes]
        current = raw_ref[:, lanes]
        window[8 : 8 + Q, :] = current
        conv = taps_ref[4:5, lanes] + taps_ref[3:4, lanes] * current
        for offset in range(1, 4):
            conv = conv + taps_ref[3 - offset : 4 - offset, lanes] * (
                masks_ref[:, (offset - 1) * LANE : offset * LANE]
                * window[8 - offset : 8 - offset + Q, :]
            )
        vals = conv * jax.nn.sigmoid(conv)
        scaled = (vals * spreads[0, :, lanes]).astype(BF16)
        zero = jnp.zeros_like(scaled)
        own = (jnp.where(first, scaled, zero), jnp.where(first, zero, scaled))
        held = state[:, lanes]
        into_here = spreads[1, :, lanes]
        base = into_here * mm(c_rows, held.astype(BF16)) + skip_ref[0:1, lanes] * vals
        cum_cols = wide_cum[:, both]
        for low in range(0, Q, BLK):
            width = low + BLK
            total = base[low:width, :]
            for which in range(2):
                across = row_cum[pl.ds(index * 2 + which, 1), :][:, :width]
                down = cum_cols[low:width, which * LANE : (which + 1) * LANE]
                down = jnp.concatenate([down] * (width // LANE), axis=1)
                decays = jnp.exp2(jnp.minimum(down - across, 0.0))
                mixing = (decays * scores[low:width, :width]).astype(BF16)
                total = total + mm(mixing, own[which][:width, :])
            y_ref[low:width, lanes] = total
        weighted = (spreads[2, :, lanes] * scaled.astype(F32)).astype(BF16)
        state[:, lanes] = held * into_here[Q - 1 : Q, :] + mm(b_turned, weighted)
        return 0

    lax.fori_loop(0, heads // 2, pair, 0, unroll=UNROLL)
    tail_rows[...] = raw_ref[Q - 8 : Q, :]


def ssd_bwd_kernel(
    heads,
    raw_ref,
    halo_ref,
    small_ref,
    bc_ref,
    masks_ref,
    masks_next_ref,
    meta_ref,
    seg_ref,
    taps_ref,
    hp_ref,
    skip_ref,
    expand_ref,
    widen_ref,
    gather_ref,
    y_ref,
    dy_ref,
    st_ref,
    dx_ref,
    ddt_ref,
    dbc_ref,
    dtaps_ref,
    dhp_ref,
    dskip_ref,
    dstate,
    next_rows,
    carried,
    window,
    dwindow,
    row_cum,
    scores,
    dscores,
    columns,
    into_dy,
    tail_vals,
    balance_parts,
    direct_parts,
    wide_cum,
):
    chunk = pl.program_id(0)

    @pl.when(chunk == 0)
    def _():
        dstate[...] = jnp.zeros_like(dstate)
        next_rows[...] = jnp.zeros_like(next_rows)
        carried[...] = jnp.zeros_like(carried)
        dtaps_ref[...] = jnp.zeros_like(dtaps_ref)
        dhp_ref[...] = jnp.zeros_like(dhp_ref)
        dskip_ref[...] = jnp.zeros_like(dskip_ref)

    pre, steps, cum, into, tail = step_terms(small_ref, meta_ref, hp_ref)
    row_cum[...] = cum
    for at, value in enumerate((cum, steps, into, tail)):
        columns[at] = as_columns(value)
    cum_cols = jnp.concatenate([cum] * 4, axis=0).T
    for head in range(heads):
        wide_cum[:, head * LANE : (head + 1) * LANE] = jnp.broadcast_to(
            cum_cols[:, head : head + 1], (Q, LANE)
        )
    same = (seg_ref[:, 0:1] == meta_ref[0, 0:1, :]) & (iota2((Q, Q), 0) <= iota2((Q, Q), 1))
    b_rows = bc_ref[:N, :].astype(F32).T.astype(BF16)
    c_turned = bc_ref[N:, :]
    scores[...] = jnp.where(same, mm(b_rows, c_turned), 0.0)
    dscores[...] = jnp.zeros_like(dscores)
    carry_high, carry_low = split_two(carried[...])
    gather_all = gather_ref[...]
    from_next = mm(carry_high, gather_all) + mm(carry_low, gather_all)
    dstate_half = dstate[...].astype(BF16)
    first = iota2((Q, LANE), 1) < LANE // 2

    def pair(index, _):
        lanes = pl.ds(pl.multiple_of(index * LANE, LANE), LANE)
        both = pl.ds(pl.multiple_of(index * 2 * LANE, 2 * LANE), 2 * LANE)
        window[0:8, :] = halo_ref[:, lanes]
        current = raw_ref[:, lanes]
        window[8 : 8 + Q, :] = current
        conv = taps_ref[4:5, lanes] + taps_ref[3:4, lanes] * current
        for offset in range(1, 4):
            conv = conv + taps_ref[3 - offset : 4 - offset, lanes] * (
                masks_ref[:, (offset - 1) * LANE : offset * LANE]
                * window[8 - offset : 8 - offset + Q, :]
            )
        gate = jax.nn.sigmoid(conv)
        vals = conv * gate
        expand = expand_ref[:, lanes]
        step_here = mm(columns[1], expand)
        scaled = (vals * step_here).astype(BF16)
        skip = skip_ref[0:1, lanes]
        dy = dy_ref[:, lanes]
        dy_half = dy.astype(BF16)
        zero = jnp.zeros_like(scaled)
        own = (jnp.where(first, scaled, zero), jnp.where(first, zero, scaled))
        own_dy = (jnp.where(first, dy_half, zero), jnp.where(first, zero, dy_half))
        dheld = dstate[:, lanes]
        tail_here = mm(columns[3], expand)
        into_here = mm(columns[2], expand)
        base = tail_here * mm(b_rows, dheld.astype(BF16))
        cum_cols = wide_cum[:, both]
        pieces = []
        for low in range(0, Q, BLK):
            high = low + BLK
            total = base[low:high, :]
            for which in range(2):
                across = row_cum[pl.ds(index * 2 + which, 1), :][:, low:]
                down = cum_cols[low:high, which * LANE : (which + 1) * LANE]
                down = jnp.concatenate([down] * ((Q - low) // LANE), axis=1)
                decays = jnp.exp2(jnp.minimum(across - down, 0.0))
                mixing = (decays * scores[low:high, low:]).astype(BF16)
                total = total + mm(mixing, own_dy[which][low:, :])
                dmix = mm_nt(own[which][low:high, :], dy_half[low:, :])
                dscores[low:high, low:] += dmix * decays
            pieces.append(total)
        dscaled = jnp.concatenate(pieces, axis=0)
        held = st_ref[0, :, lanes]
        edy = (into_here * dy).astype(BF16)
        scaled_f = scaled.astype(F32)
        into_dy[:, lanes] = edy
        tail_vals[:, lanes] = (tail_here * scaled_f).astype(BF16)
        balance = dy_half.astype(F32) * (y_ref[:, lanes] - skip * vals) - scaled_f * dscaled
        part_high, part_low = split_two(balance)
        balance_parts[0, :, lanes] = part_high
        balance_parts[1, :, lanes] = part_low
        part_high, part_low = split_two(vals * dscaled)
        direct_parts[0, :, lanes] = part_high
        direct_parts[1, :, lanes] = part_low
        dskip_ref[0:1, lanes] += jnp.sum(dy * vals, axis=0, keepdims=True)
        dheld_new = into_here[Q - 1 : Q, :] * dheld + mm(c_turned, edy)
        dstate[:, lanes] = dheld_new
        carried[0:1, lanes] = jnp.sum(dheld_new * held, axis=0, keepdims=True)
        dvals = step_here * dscaled + skip * dy
        dconv = dvals * (gate * (1.0 + conv * (1.0 - gate)))
        dwindow[0:Q, :] = dconv
        dwindow[Q : Q + 8, :] = next_rows[:, lanes]
        next_rows[:, lanes] = dconv[0:8, :]
        dtaps_ref[4:5, lanes] += jnp.sum(dconv, axis=0, keepdims=True)
        dtaps_ref[3:4, lanes] += jnp.sum(dconv * current, axis=0, keepdims=True)
        draw = taps_ref[3:4, lanes] * dconv
        for offset in range(1, 4):
            mask = masks_ref[:, (offset - 1) * LANE : offset * LANE]
            mask_next = masks_next_ref[:, (offset - 1) * LANE : offset * LANE]
            mask_later = jnp.concatenate([mask, mask_next], axis=0)[offset : offset + Q, :]
            shifted = mask * window[8 - offset : 8 - offset + Q, :]
            dtaps_ref[3 - offset : 4 - offset, lanes] += jnp.sum(
                dconv * shifted, axis=0, keepdims=True
            )
            draw = draw + taps_ref[3 - offset : 4 - offset, lanes] * (
                mask_later * dwindow[offset : offset + Q, :]
            )
        dx_ref[:, lanes] = draw.astype(BF16)
        return 0

    lax.fori_loop(0, heads // 2, pair, 0, unroll=UNROLL)
    dscores_now = jnp.where(same, dscores[...], 0.0)
    d_b = mm_nt(tail_vals[...], dstate_half) + mm_nt(dscores_now.astype(BF16), c_turned)
    d_c = mm_nt(into_dy[...], st_ref[0].astype(BF16)) + mm(dscores_now.T.astype(BF16), b_rows)
    dbc_ref[:N, :] = d_b.T
    dbc_ref[N:, :] = d_c.T
    balance = mm(balance_parts[0], gather_all) + mm(balance_parts[1], gather_all)
    balance = balance + jnp.where(iota2((Q, LANE), 0) == Q - 1, from_next[0:1, :], 0.0)
    direct = mm(direct_parts[0], gather_all) + mm(direct_parts[1], gather_all)
    since = (iota2((Q, Q), 0) >= iota2((Q, Q), 1)).astype(BF16)
    dlogs = lane_sums(balance.T[:SLOTS], since)
    dsteps = dlogs * hp_ref[:, 1:2] + direct.T[:SLOTS]
    dsteps = dsteps * jax.nn.sigmoid(pre) * hp_ref[:, 2:3]
    ddt_ref[...] = dsteps
    dhp_ref[:, 0:1] += jnp.sum(dsteps, axis=1, keepdims=True)
    dhp_ref[:, 1:2] += jnp.sum(dlogs * steps, axis=1, keepdims=True)


def head_tables(heads):
    width = heads * (LANE // 2)
    owner = jnp.arange(width) // (LANE // 2)
    wide_owner = jnp.arange(heads * LANE) // LANE
    slot = jnp.arange(LANE)
    real = (slot < 3 * SLOTS)[:, None]
    expand = ((slot % SLOTS)[:, None] == owner[None, :]) & real
    widen = ((slot % SLOTS)[:, None] == wide_owner[None, :]) & real
    gather = owner[:, None] == slot[None, :]
    return expand.astype(BF16), widen.astype(BF16), gather.astype(BF16)


def segment_tables(segment):
    length = segment.shape[0]
    chunks = length // Q
    doc_masks = []
    for offset in range(1, 4):
        earlier = jnp.concatenate(
            [jnp.full((offset,), -1, jnp.int32), segment[: length - offset]], axis=0
        )
        doc_masks.append((earlier == segment).astype(F32))
    masks = jnp.concatenate(
        [jnp.broadcast_to(mask[:, None], (length, LANE)) for mask in doc_masks], axis=1
    )
    by_chunk = segment.reshape(chunks, Q)
    last = by_chunk[:, Q - 1]
    before = jnp.concatenate([jnp.full((1,), -1, jnp.int32), last[: chunks - 1]], axis=0)
    rows = [
        by_chunk.astype(F32),
        (by_chunk == before[:, None]).astype(F32),
        (by_chunk == last[:, None]).astype(F32),
    ]
    meta = jnp.pad(jnp.stack(rows, axis=1), ((0, 0), (0, 5), (0, 0)))
    seg_cols = jnp.broadcast_to(segment.astype(F32)[:, None], (length, LANE))
    return doc_masks, masks, meta, seg_cols


def head_columns(head_params):
    heads = head_params.shape[1]
    rates = -jnp.exp(head_params[1])
    table = jnp.stack([head_params[0], rates, jnp.ones_like(rates)], axis=1)
    return jnp.pad(table, ((0, SLOTS - heads), (0, LANE - 3)))


def time_like(seconds):
    return pl.CostEstimate(
        flops=int(seconds * 1.1e15), bytes_accessed=int(seconds * 3.4e12), transcendentals=0
    )


def full_spec(shape):
    return pl.BlockSpec(shape, lambda c: (0,) * len(shape))


def ssd_forward(raw, small, bc, tables, taps, hp, skip, spread, heads):
    length = raw.shape[0]
    width = heads * (LANE // 2)
    chunks = length // Q
    _, masks, meta, seg_cols = tables
    expand, widen, _ = spread
    return pl.pallas_call(
        functools.partial(ssd_fwd_kernel, heads),
        grid=(chunks,),
        out_shape=(
            jax.ShapeDtypeStruct((length, width), F32),
            jax.ShapeDtypeStruct((chunks, N, width), F32),
        ),
        in_specs=[
            pl.BlockSpec((Q, width), lambda c: (c, 0)),
            pl.BlockSpec((SLOTS, Q), lambda c: (0, c)),
            pl.BlockSpec((2 * N, Q), lambda c: (0, c)),
            pl.BlockSpec((Q, 3 * LANE), lambda c: (c, 0)),
            pl.BlockSpec((1, 8, Q), lambda c: (c, 0, 0)),
            pl.BlockSpec((Q, LANE), lambda c: (c, 0)),
            full_spec((8, width)),
            full_spec((SLOTS, LANE)),
            full_spec((8, width)),
            full_spec((LANE, width)),
            full_spec((LANE, heads * LANE)),
        ],
        out_specs=(
            pl.BlockSpec((Q, width), lambda c: (c, 0)),
            pl.BlockSpec((1, N, width), lambda c: (c, 0, 0)),
        ),
        scratch_shapes=[
            pltpu.VMEM((N, width), F32),
            pltpu.VMEM((8, width), F32),
            pltpu.VMEM((Q + 8, LANE), F32),
            pltpu.VMEM((SLOTS, Q), F32),
            pltpu.VMEM((Q, Q), F32),
            pltpu.VMEM((4, Q, LANE), BF16),
            pltpu.VMEM((3, Q, width), F32),
            pltpu.VMEM((Q, heads * LANE), F32),
        ],
        compiler_params=pltpu.CompilerParams(vmem_limit_bytes=VMEM_CAP),
        cost_estimate=time_like(37e-6 * length * heads / 30720),
        name="ssd_fwd",
    )(raw, small, bc, masks, meta, seg_cols, taps, hp, skip, expand, widen)


def ssd_backward(raw, small, bc, tables, taps, hp, skip, spread, y, dy, states, heads):
    length = raw.shape[0]
    width = heads * (LANE // 2)
    chunks = length // Q
    per = Q // 8
    _, masks, meta, seg_cols = tables

    def at(c):
        return chunks - 1 - c

    return pl.pallas_call(
        functools.partial(ssd_bwd_kernel, heads),
        grid=(chunks,),
        out_shape=(
            jax.ShapeDtypeStruct((length, width), BF16),
            jax.ShapeDtypeStruct((SLOTS, length), F32),
            jax.ShapeDtypeStruct((2 * N, length), F32),
            jax.ShapeDtypeStruct((8, width), F32),
            jax.ShapeDtypeStruct((SLOTS, LANE), F32),
            jax.ShapeDtypeStruct((8, width), F32),
        ),
        in_specs=[
            pl.BlockSpec((Q, width), lambda c: (at(c), 0)),
            pl.BlockSpec((8, width), lambda c: (jnp.maximum(at(c) * per - 1, 0), 0)),
            pl.BlockSpec((SLOTS, Q), lambda c: (0, at(c))),
            pl.BlockSpec((2 * N, Q), lambda c: (0, at(c))),
            pl.BlockSpec((Q, 3 * LANE), lambda c: (at(c), 0)),
            pl.BlockSpec(
                (8, 3 * LANE), lambda c: (jnp.minimum((at(c) + 1) * per, chunks * per - 1), 0)
            ),
            pl.BlockSpec((1, 8, Q), lambda c: (at(c), 0, 0)),
            pl.BlockSpec((Q, LANE), lambda c: (at(c), 0)),
            full_spec((8, width)),
            full_spec((SLOTS, LANE)),
            full_spec((8, width)),
            full_spec((LANE, width)),
            full_spec((LANE, heads * LANE)),
            full_spec((width, LANE)),
            pl.BlockSpec((Q, width), lambda c: (at(c), 0)),
            pl.BlockSpec((Q, width), lambda c: (at(c), 0)),
            pl.BlockSpec((1, N, width), lambda c: (at(c), 0, 0)),
        ],
        out_specs=(
            pl.BlockSpec((Q, width), lambda c: (at(c), 0)),
            pl.BlockSpec((SLOTS, Q), lambda c: (0, at(c))),
            pl.BlockSpec((2 * N, Q), lambda c: (0, at(c))),
            full_spec((8, width)),
            full_spec((SLOTS, LANE)),
            full_spec((8, width)),
        ),
        scratch_shapes=[
            pltpu.VMEM((N, width), F32),
            pltpu.VMEM((8, width), F32),
            pltpu.VMEM((8, width), F32),
            pltpu.VMEM((Q + 8, LANE), F32),
            pltpu.VMEM((Q + 8, LANE), F32),
            pltpu.VMEM((SLOTS, Q), F32),
            pltpu.VMEM((Q, Q), F32),
            pltpu.VMEM((Q, Q), F32),
            pltpu.VMEM((4, Q, LANE), BF16),
            pltpu.VMEM((Q, width), BF16),
            pltpu.VMEM((Q, width), BF16),
            pltpu.VMEM((2, Q, width), BF16),
            pltpu.VMEM((2, Q, width), BF16),
            pltpu.VMEM((Q, heads * LANE), F32),
        ],
        compiler_params=pltpu.CompilerParams(vmem_limit_bytes=VMEM_CAP),
        cost_estimate=time_like(69e-6 * length * heads / 30720),
        name="ssd_bwd",
    )(
        raw,
        raw,
        small,
        bc,
        masks,
        masks,
        meta,
        seg_cols,
        taps,
        hp,
        skip,
        *spread,
        y,
        dy,
        states,
    )


def dn_kernel(count, rows, at_ref, *refs):
    dz, dx, side, normed = (refs[k * count : (k + 1) * count] for k in range(4))
    gate_ref, inner_ref, out_ref, sums_ref = refs[4 * count : 4 * count + 4]
    turned = refs[4 * count + 4]
    width = dz[0].shape[1]

    @pl.when(pl.program_id(0) == 0)
    def _():
        for k in range(count):
            turned[k * rows : (k + 1) * rows, :] = side[k][...].T.astype(BF16)

    gate = gate_ref[...]
    inner = inner_ref[:, :width]
    last = inner_ref[:, width:]
    sums = None
    for k in range(count):
        at = slice(k * rows, (k + 1) * rows)
        total = mm_nt(dz[k][...], gate) + mm_nt(dx[k][...], inner) + mm_nt(turned[at, :], last)
        out_ref[at, :] = total.astype(BF16)
        part = jnp.sum(total * normed[k][...].astype(F32), axis=0, keepdims=True)
        sums = part if sums is None else sums + part
    sums_ref[0:1, :] = sums


def d_normed_blocks(d_z, d_x, d_side, gate_all, x_all, normed, blocks, which, rows, tile=256):
    length, width = d_z.shape
    count = blocks.shape[0]
    half = gate_all.shape[0] // 2
    first = which * half // tile

    def rows_of(k):
        return pl.BlockSpec((rows, width), lambda n, at, k=k: (at[k], 0))

    def cols_of(k):
        return pl.BlockSpec((LANE, rows), lambda n, at, k=k: (0, at[k]))

    def tile_of(k):
        return pl.BlockSpec((rows, tile), lambda n, at, k=k: (at[k], n + first))

    each = range(count)
    return pl.pallas_call(
        functools.partial(dn_kernel, count, rows),
        grid_spec=pltpu.PrefetchScalarGridSpec(
            num_scalar_prefetch=1,
            grid=(half // tile,),
            in_specs=[rows_of(k) for k in each]
            + [rows_of(k) for k in each]
            + [cols_of(k) for k in each]
            + [tile_of(k) for k in each]
            + [
                pl.BlockSpec((tile, width), lambda n, at: (n + first, 0)),
                pl.BlockSpec((tile, width + LANE), lambda n, at: (n + first, 0)),
            ],
            out_specs=(
                pl.BlockSpec((count * rows, tile), lambda n, at: (0, n)),
                pl.BlockSpec((8, tile), lambda n, at: (0, n)),
            ),
            scratch_shapes=[pltpu.VMEM((count * rows, LANE), BF16)],
        ),
        out_shape=(
            jax.ShapeDtypeStruct((count * rows, half), BF16),
            jax.ShapeDtypeStruct((8, half), F32),
        ),
        compiler_params=pltpu.CompilerParams(vmem_limit_bytes=VMEM_CAP),
        cost_estimate=time_like(1e-7),
        name="d_normed",
    )(
        blocks,
        *([d_z] * count),
        *([d_x] * count),
        *([d_side] * count),
        *([normed] * count),
        gate_all,
        x_all,
    )


def adam_kernel(step, gate_ref, inner_ref, weight_ref, first_ref, second_ref, *outs):
    grad_out, weight_out, first_out, second_out = outs
    for part, grad_ref in ((0, gate_ref), (1, inner_ref)):
        grad = grad_ref[...].astype(F32)
        new_weight, new_first, new_second = step(
            weight_ref[:, part, :], grad, first_ref[:, part, :], second_ref[:, part, :]
        )
        grad_out[:, part, :] = grad
        weight_out[:, part, :] = new_weight
        first_out[:, part, :] = new_first
        second_out[:, part, :] = new_second


def adam_pair(step, grad_gate, grad_inner, weight, first, second, rows=40):
    shard, _, width = weight.shape
    deep = pl.BlockSpec((rows, 2, width), lambda n: (n, 0, 0))
    flat = pl.BlockSpec((rows, width), lambda n: (n, 0))
    like = jax.ShapeDtypeStruct(weight.shape, F32)
    return pl.pallas_call(
        functools.partial(adam_kernel, step),
        grid=(shard // rows,),
        out_shape=(like, jax.ShapeDtypeStruct(weight.shape, weight.dtype), like, like),
        in_specs=[flat, flat, deep, deep, deep],
        out_specs=(deep,) * 4,
        compiler_params=pltpu.CompilerParams(vmem_limit_bytes=VMEM_CAP),
        cost_estimate=pl.CostEstimate(flops=1000, bytes_accessed=1000, transcendentals=0),
        name="adam_pair",
    )(grad_gate, grad_inner, weight, first, second)


def product_kernel(left_ref, right_ref, out_ref):
    out_ref[...] = mm(left_ref[...], right_ref[...])


def gate_kernel(left_ref, right_ref, mixed_ref, z_ref, gated_ref, sums_ref):
    z_raw = mm(left_ref[...], right_ref[...])
    gated = mixed_ref[...] * (z_raw * jax.nn.sigmoid(z_raw))
    z_ref[...] = z_raw
    gated_ref[...] = gated
    sums = jnp.sum(gated * gated, axis=1, keepdims=True)
    sums_ref[...] = jnp.broadcast_to(sums, (sums.shape[0], LANE)).T[:8]


def output_kernel(left_ref, right_ref, grad_ref, first_ref, second_ref, sums_ref):
    half = first_ref.shape[1]
    total = None
    for at, out_ref in ((0, first_ref), (half, second_ref)):
        part = mm_nt(left_ref[...], right_ref[at : at + half, :])
        out_ref[...] = part.astype(BF16)
        sums = jnp.sum(part * grad_ref[:, at : at + half].astype(F32), axis=1, keepdims=True)
        total = sums if total is None else total + sums
    sums_ref[...] = jnp.broadcast_to(total, (total.shape[0], LANE)).T[:8]


def gate_grad_kernel(
    left_ref, right_ref, z_ref, mixed_ref, gain_ref, inv_ref, mean_ref, dy_ref, dz_ref, dgain_ref
):
    @pl.when(pl.program_id(0) == 0)
    def _():
        dgain_ref[...] = jnp.zeros_like(dgain_ref)

    d_ng = mm(left_ref[...], right_ref[...])
    z_raw = z_ref[...]
    mixed = mixed_ref[...]
    inv = inv_ref[...]
    sig = jax.nn.sigmoid(z_raw)
    gate_act = z_raw * sig
    unit = mixed * gate_act * inv
    dgain_ref[0:1, :] += jnp.sum(d_ng * unit, axis=0, keepdims=True)
    d_gated = inv * (d_ng * gain_ref[0:1, :] - unit * mean_ref[...])
    dy_ref[...] = d_gated * gate_act
    dz_ref[...] = (d_gated * mixed * sig * (1.0 + z_raw * (1.0 - sig))).astype(BF16)


def row_call(kernel, name, seconds, length, rows, ins, outs):
    def spec(shape, split):
        if split == "rows":
            return pl.BlockSpec((rows,) + shape, lambda m: (m, 0))
        if split == "lanes":
            return pl.BlockSpec(shape + (rows,), lambda m: (0, m))
        return pl.BlockSpec(shape, lambda m: (0, 0))

    return pl.pallas_call(
        kernel,
        grid=(length // rows,),
        out_shape=tuple(jax.ShapeDtypeStruct(full, kind) for full, kind, _, _ in outs),
        in_specs=[spec(shape, split) for _, shape, split in ins],
        out_specs=tuple(spec(shape, split) for _, _, shape, split in outs),
        compiler_params=pltpu.CompilerParams(vmem_limit_bytes=VMEM_CAP),
        cost_estimate=time_like(seconds),
        name=name,
    )(*[array for array, _, _ in ins])


def inner_product(normed, x_all, width, rows=256):
    length, model = normed.shape
    return row_call(
        product_kernel,
        "inner_product",
        14e-6,
        length,
        rows,
        [(normed, (model,), "rows"), (x_all, (model, width), None)],
        [((length, width), F32, (width,), "rows")],
    )[0]


def gate_product(normed, gate_all, mixed, rows=256):
    length, model = normed.shape
    width = gate_all.shape[1]
    wide = ((length, width), F32, (width,), "rows")
    z_raw, gated, sums = row_call(
        gate_kernel,
        "gate_product",
        16e-6,
        length,
        rows,
        [(normed, (model,), "rows"), (gate_all, (model, width), None), (mixed, (width,), "rows")],
        [wide, wide, ((8, length), F32, (8,), "lanes")],
    )
    return z_raw, gated, sums[0]


def output_product(normed_gated, out_all, group_grad, rows=256):
    length, width = normed_gated.shape
    model = out_all.shape[0]
    part = ((length, model // 2), BF16, (model // 2,), "rows")
    left, right, sums = row_call(
        output_kernel,
        "output_product",
        16e-6,
        length,
        rows,
        [
            (normed_gated, (width,), "rows"),
            (out_all, (model, width), None),
            (group_grad, (model,), "rows"),
        ],
        [part, part, ((8, length), F32, (8,), "lanes")],
    )
    return left, right, sums[0]


def gate_gradient(group_grad, out_all, z_raw, mixed, gain, inv, mean, rows=256):
    length, model = group_grad.shape
    width = out_all.shape[1]
    return row_call(
        gate_grad_kernel,
        "gate_gradient",
        18e-6,
        length,
        rows,
        [
            (group_grad, (model,), "rows"),
            (out_all, (model, width), None),
            (z_raw, (width,), "rows"),
            (mixed, (width,), "rows"),
            (gain, (8, width), None),
            (inv, (1,), "rows"),
            (mean, (1,), "rows"),
        ],
        [
            ((length, width), F32, (width,), "rows"),
            ((length, width), BF16, (width,), "rows"),
            ((8, width), F32, (8, width), None),
        ],
    )


def added(refs):
    total = refs[0][...].astype(F32)
    for ref in refs[1:]:
        total = total + ref[...].astype(F32)
    return total


def block_out_kernel(count, *refs):
    left, right = refs[:count], refs[count : 2 * count]
    block_ref, live_ref, out_ref = refs[2 * count :]
    half = out_ref.shape[1] // 2
    live = live_ref[...] > 0.0
    for at, pieces in ((0, left), (half, right)):
        cols = slice(at, at + half)
        total = jnp.where(live, added(pieces), 0.0)
        out_ref[:, cols] = (block_ref[:, cols].astype(F32) + total).astype(BF16)


def d_input_kernel(eps, count, *refs):
    left, right = refs[:count], refs[count : 2 * count]
    block_ref, cot_ref, gain_ref, out_ref = refs[2 * count :]
    model = out_ref.shape[1]
    half = model // 2
    rows = block_ref[...].astype(F32)
    inv = lax.rsqrt(jnp.sum(rows * rows, axis=1, keepdims=True) / model + eps)
    unit = rows * inv
    parts = [
        added(pieces) * gain_ref[0:1, at : at + half]
        for at, pieces in ((0, left), (half, right))
    ]
    mean = (
        jnp.sum(parts[0] * unit[:, :half], axis=1, keepdims=True)
        + jnp.sum(parts[1] * unit[:, half:], axis=1, keepdims=True)
    ) / model
    for at, scaled in ((0, parts[0]), (half, parts[1])):
        cols = slice(at, at + half)
        d_block = inv * (scaled - unit[:, cols] * mean)
        out_ref[:, cols] = (cot_ref[:, cols].astype(F32) + d_block).astype(BF16)


def finish(kernel, name, left, right, ins, length, model, rows=128):
    half = model // 2

    def piece(first):
        return pl.BlockSpec((rows, half), lambda m: (m + first // rows, 0))

    pieces = list(left) + list(right)
    return pl.pallas_call(
        functools.partial(kernel, len(left)),
        grid=(length // rows,),
        out_shape=jax.ShapeDtypeStruct((length, model), BF16),
        in_specs=[piece(first) for _, first in pieces]
        + [
            pl.BlockSpec((rows, array.shape[1]), lambda m: (m, 0))
            if array.shape[0] == length
            else full_spec(array.shape)
            for array in ins
        ],
        out_specs=pl.BlockSpec((rows, model), lambda m: (m, 0)),
        compiler_params=pltpu.CompilerParams(vmem_limit_bytes=VMEM_CAP),
        cost_estimate=time_like(1e-7),
        name=name,
    )(*[array for array, _ in pieces], *ins)

DI = 5120
STEP = 3
NORM_EPS = 1e-05
BETA_ONE = 0.9
BETA_TWO = 0.95
LEARN_RATE = 0.004
LEARN_SMALL = 0.15
WEIGHT_DECAY = 0.1
ADAM_EPS = 1e-08


def by_rows(value):
    return with_layout_constraint(value, Layout(major_to_minor=(0, 1)))


def silu_act(values):
    return values * jax.nn.sigmoid(values)


def later(row, offset):
    return jnp.pad(row, ((0, 0), (offset, 0)))[:, : row.shape[1]]


def state_act(raw_cols, conv_taps, doc_masks):
    conv = conv_taps[4][:, None] + conv_taps[3][:, None] * raw_cols
    for offset in range(1, 4):
        conv = conv + conv_taps[3 - offset][:, None] * (
            doc_masks[offset - 1][None, :] * later(raw_cols, offset)
        )
    return silu_act(conv)


def contract_rows(left_mat, right_mat):
    return lax.dot_general(
        left_mat, right_mat, (((0,), (0,)), ((), ())), preferred_element_type=F32
    )


def adamw_step(weight, gradient, first_moment, second_moment, decay_factor, learn_rate):
    new_first = BETA_ONE * first_moment + (1.0 - BETA_ONE) * gradient
    new_second = BETA_TWO * second_moment + (1.0 - BETA_TWO) * gradient * gradient
    first_hat = new_first / (1.0 - BETA_ONE**STEP)
    second_hat = new_second / (1.0 - BETA_TWO**STEP)
    weight_f = weight.astype(F32)
    updated = weight_f - learn_rate * (
        first_hat / (jnp.sqrt(second_hat) + ADAM_EPS) + decay_factor * weight_f
    )
    return (updated.astype(weight.dtype), new_first, new_second)


def swap(value, distance, size):
    return lax.ppermute(value, "tp", [(at, at ^ distance) for at in range(size)])


def tied(*values):
    return lax.optimization_barrier(values)


def gather_parts(value, size, near_done):
    if size != 4:
        one, *others = near_done(swap(value, 1, size))
        return [value, one] + [swap(value, k, size) for k in range(2, size)], *others
    half = value.shape[0] // 2
    one, two = swap(value, 1, size), swap(value, 2, size)
    one, *others = near_done(one)
    far = jnp.concatenate([swap(two[:half], 1, size), swap(one[half:], 2, size)], axis=0)
    return [value, one, two, far], *others


def scatter_start(left, right, rows, index, size):
    def block(value, distance):
        return lax.dynamic_slice_in_dim(value, (index ^ distance) * rows, rows, 0)

    sent, kept = [], []
    for half, near in ((left, 1), (right, 2)):
        if size == 4:
            pair = jnp.concatenate([block(half, 3), block(half, near)], axis=0)
            sent.append(swap(pair, near, size))
            kept.append((block(half, 3 - near), (block(half, 0), 0)))
        else:
            sent.append([swap(block(half, k), k, size) for k in range(1, size)])
            kept.append(block(half, 0))
    return sent, kept


def scatter_middle(sent, kept, rows, size):
    if size != 4:
        return sent, [[(one, 0)] for one in kept]
    passed = [
        (kept[at][0].astype(F32) + sent[at][:rows].astype(F32)).astype(BF16) for at in range(2)
    ]
    return passed, [[kept[at][1], (sent[at], rows)] for at in range(2)]


def scatter_last(passed, size):
    if size != 4:
        return passed[0] + passed[1]
    return [swap(passed[0], 2, size), swap(passed[1], 1, size)]


def scatter_end(own, last):
    each = len(last) // 2
    return [
        own[at] + [(piece, 0) for piece in last[at * each : (at + 1) * each]] for at in range(2)
    ]


def row_sum(value, size):
    total = value
    for distance in range(1, size):
        total = total + swap(value, distance, size)
    return total


def all_sum(value, index, size):
    terms = jnp.zeros((size,) + value.shape, value.dtype)
    for distance in range(size):
        piece = value if distance == 0 else swap(value, distance, size)
        terms = lax.dynamic_update_slice(terms, piece[None], (index ^ distance, jnp.int32(0)))
    return jnp.sum(terms, axis=0)


def fsdp_swap(value, distance, size):
    return lax.ppermute(value, "fsdp", [(at, at ^ distance) for at in range(size)])


def gather_by_swaps(value, index, size):
    whole = jnp.zeros((size,) + value.shape, value.dtype)
    for distance in range(size):
        piece = value if distance == 0 else fsdp_swap(value, distance, size)
        whole = lax.dynamic_update_slice(whole, piece[None], (index ^ distance, jnp.int32(0)))
    return whole


def pair_sum(value, index, size):
    blocks = value.reshape(size // 2, 2, value.shape[0] // size, value.shape[1])
    core = index % 2
    away = lax.dynamic_slice_in_dim(blocks, 1 - core, 1, 1)[:, 0]
    own = lax.dynamic_slice_in_dim(blocks, core, 1, 1)[:, 0]
    return (own.astype(F32) + fsdp_swap(away, 1, size).astype(F32)).astype(value.dtype)


def chip_scatter(value, size):
    groups = [list(range(core, size, 2)) for core in range(2)]
    flat = value.reshape(value.shape[0] * value.shape[1], value.shape[2])
    return lax.psum_scatter(
        flat, "fsdp", scatter_dimension=0, axis_index_groups=groups, tiled=True
    )


def chip_sum(value, index, size, after):
    chip = index // 2

    def block(distance):
        return lax.dynamic_slice_in_dim(value, chip ^ distance, 1, 0)[0]

    pieces = [fsdp_swap(block(k), 2 * k, size) for k in range(1, size // 2)]
    pieces, after = tied(pieces, after)
    return sum(pieces, block(0)), after


def pad_cols(value, width):
    return jnp.pad(value, ((0, 0), (0, width - value.shape[1])))


def body(
    block_in,
    cotangent,
    segment_ids,
    group_fill,
    input_gain,
    proj_inner,
    proj_step,
    proj_state,
    conv_inner,
    conv_state,
    head_params,
    mixer_gain,
    proj_output,
    *moments,
):
    tp_size = lax.axis_size("tp")
    fsdp_size = lax.axis_size("fsdp")
    tp_index = lax.axis_index("tp")
    fsdp_index = lax.axis_index("fsdp")
    own_rows, model = block_in.shape
    group_rows = own_rows * tp_size
    shard, _, width = proj_inner.shape
    heads = proj_step.shape[1]
    state_cols = proj_state.shape[1]
    segment = segment_ids[0]
    filled = group_fill[0]

    small_values = jnp.concatenate(
        [input_gain, conv_inner.reshape(-1), conv_state.reshape(-1), mixer_gain], axis=0
    )
    inner_n, state_n = conv_inner.size, conv_state.size
    small_count = inner_n + state_n + mixer_gain.size
    small_cols = -(-(small_count + 3 * heads) // shard)
    used = heads + state_cols
    side = pad_cols(jnp.concatenate([proj_step, proj_state], axis=1), LANE)
    (inner_halves,) = tied(proj_inner.transpose(1, 0, 2))
    x_local = jnp.concatenate([inner_halves[1], side], axis=1)
    x_all = lax.all_gather(x_local, "fsdp", axis=0, tiled=True)
    gate_all = lax.all_gather(inner_halves[0], "fsdp", axis=0, tiled=True)
    small_all = lax.dynamic_update_slice(
        jnp.zeros((fsdp_size, small_values.size), BF16),
        small_values[None],
        (fsdp_index, jnp.int32(0)),
    )
    distance = 1
    while distance < fsdp_size:
        small_all = small_all + fsdp_swap(small_all, distance, fsdp_size)
        distance *= 2
    gain_f = small_all[:, :shard].reshape(model).astype(F32)
    extras = small_all[:, shard:]

    def from_owners(flat, rows):
        return flat.reshape(fsdp_size, rows, -1).transpose(1, 0, 2).reshape(rows, -1).astype(F32)

    taps_inner = from_owners(extras[:, :inner_n], 5)
    taps_state = from_owners(extras[:, inner_n : inner_n + state_n], 5)
    mixer_f = from_owners(extras[:, inner_n + state_n : small_count], 1)[0]
    taps8 = jnp.pad(taps_inner, ((0, 3), (0, 0)))
    mixer8 = jnp.broadcast_to(mixer_f[None, :], (8, width))
    spread = head_tables(heads)
    tables = segment_tables(segment)
    doc_masks = tables[0]
    hp8 = head_columns(head_params)
    skip8 = jnp.broadcast_to(jnp.repeat(head_params[2], LANE // 2)[None, :], (8, width))
    positions = tp_index * own_rows + jnp.arange(own_rows, dtype=jnp.int32)
    live_rows = (positions < filled)[:, None]
    block_f = block_in.astype(F32)
    cot_f = cotangent.astype(F32)
    own_grad = jnp.where(live_rows, cot_f, 0.0).astype(BF16)
    blank = jnp.zeros((group_rows, model), BF16)

    def unit_of(rows):
        rows_f = rows.astype(F32)
        scale = lax.rsqrt(jnp.mean(rows_f * rows_f, axis=1, keepdims=True) + NORM_EPS)
        return rows_f * scale, scale

    def normed_of(rows):
        return (unit_of(rows)[0] * gain_f[None, :]).astype(BF16)

    def put(whole, part, distance):
        return lax.dynamic_update_slice(
            whole, part, ((tp_index ^ distance) * own_rows, jnp.int32(0))
        )

    started = put(blank, normed_of(block_in), 0)

    def near_done(one):
        return tied(one, started, own_grad, taps8, taps_state, mixer8, hp8, skip8, *tables[1:])

    row_parts, started, own_grad, taps8, taps_state, mixer8, hp8, skip8, *late = gather_parts(
        block_in, tp_size, near_done
    )
    tables = (doc_masks, *late)
    row_parts = [by_rows(part) for part in row_parts]
    own_grad, *row_parts = tied(own_grad, *row_parts)
    near = min(3, tp_size)
    grad_parts = [by_rows(own_grad)] + [swap(own_grad, k, tp_size) for k in range(1, near)]

    side_all = x_all[:, width:]
    normed = started
    for distance in range(1, tp_size - 1):
        normed = put(normed, normed_of(row_parts[distance]), distance)
    far_rows, normed = tied(row_parts[-1], normed)
    normed = by_rows(put(normed, normed_of(far_rows), tp_size - 1))
    small = lax.dot_general(
        side_all, normed, (((0,), (1,)), ((), ())), preferred_element_type=F32
    )
    raw = inner_product(normed, x_all, width)
    state_vals, state_back = jax.vjp(
        lambda raw_cols, conv_taps: state_act(raw_cols, conv_taps, doc_masks),
        small[heads:used],
        taps_state,
    )
    state_local = state_vals.astype(BF16)
    bc = jnp.zeros((tp_size * state_cols, group_rows), BF16)
    for k in range(tp_size):
        piece = state_local if k == 0 else swap(state_local, k, tp_size)
        bc = lax.dynamic_update_slice(bc, piece, ((tp_index ^ k) * state_cols, jnp.int32(0)))
    own_grad, bc, out_local = tied(own_grad, bc, proj_output.T)
    out_all = lax.all_gather(out_local, "fsdp", axis=0, tiled=True)
    grad_parts += [swap(own_grad, k, tp_size) for k in range(near, tp_size)]
    mixed, states = ssd_forward(raw, small, bc, tables, taps8, hp8, skip8, spread, heads)

    z_raw, gated, square_sum = gate_product(normed, gate_all, mixed)
    square_sum, *grad_parts = tied(square_sum, *grad_parts)
    square_sum = row_sum(square_sum, tp_size)
    group_grad = jnp.zeros((group_rows, model), BF16)
    for distance in range(tp_size):
        group_grad = put(group_grad, grad_parts[distance], distance)
    group_grad = by_rows(group_grad)
    inv_gate = lax.rsqrt(square_sum / DI + NORM_EPS)[:, None]
    normed_gated = (gated * inv_gate * mixer8[0:1]).astype(BF16)
    sum_out = pair_sum(
        contract_rows(group_grad, normed_gated).astype(BF16), fsdp_index, fsdp_size
    )
    half = model // 2
    normed_gated, sum_out = tied(normed_gated, sum_out)
    grad_out = chip_scatter(sum_out, fsdp_size)
    mixed_left, mixed_right, inner_sum = output_product(normed_gated, out_all, group_grad)
    inner_sum = row_sum(inner_sum, tp_size)
    mixed_sent, mixed_kept = scatter_start(mixed_left, mixed_right, own_rows, tp_index, tp_size)

    inner_mean = inner_sum[:, None] / DI
    d_mixed, d_z, grad_mixer = gate_gradient(
        group_grad, out_all, z_raw, mixed, mixer8, inv_gate, inner_mean
    )
    grad_mixer = grad_mixer[0]
    part_gate, mixed_sent = tied(contract_rows(normed, d_z).astype(BF16), mixed_sent)
    sum_gate = pair_sum(part_gate, fsdp_index, fsdp_size)
    mixed_passed, mixed_kept = scatter_middle(mixed_sent, mixed_kept, own_rows, tp_size)
    sum_gate, grad_out = tied(sum_gate, grad_out)

    d_mixed, sum_gate, mixed_passed = tied(d_mixed, sum_gate, mixed_passed)
    mixed_last = scatter_last(mixed_passed, tp_size)
    grad_gate = chip_scatter(sum_gate, fsdp_size)
    d_x, d_dt, d_bc, d_taps, d_heads, d_skip = ssd_backward(
        raw, small, bc, tables, taps8, hp8, skip8, spread, mixed, d_mixed, states, heads
    )
    def state_block(distance):
        return lax.dynamic_slice_in_dim(d_bc, (tp_index ^ distance) * state_cols, state_cols, 0)

    state_parts = [state_block(0)]
    state_parts += [swap(state_block(k), k, tp_size) for k in range(1, tp_size)]
    part_x, mixed_last, grad_gate, *state_parts = tied(
        contract_rows(normed, d_x).astype(BF16), mixed_last, grad_gate, *state_parts
    )
    sum_x = pair_sum(part_x, fsdp_index, fsdp_size)

    d_state_raw, grad_conv_state = state_back(sum(state_parts[1:], state_parts[0]).astype(F32))
    d_side = jnp.concatenate([d_dt[:heads], d_state_raw], axis=0)
    d_side = jnp.pad(d_side, ((0, LANE - used), (0, 0)))

    four = tp_size == 4
    side_part = lax.dot_general(
        normed, d_side.astype(BF16), (((0,), (1,)), ((), ())), preferred_element_type=F32
    )

    def side_gradient(side_part, d_taps, d_skip, d_heads, grad_conv_state, gain_sums, after):
        grad_head = jnp.stack(
            [
                d_heads[:heads, 0],
                hp8[:heads, 1] * d_heads[:heads, 1],
                jnp.sum(d_skip[0].reshape(heads, LANE // 2), axis=1),
            ],
            axis=0,
        )

        def by_owner(value):
            rows = value.shape[0]
            return value.reshape(rows, fsdp_size, -1).transpose(1, 0, 2).reshape(fsdp_size, -1)

        grad_extras = jnp.concatenate(
            [
                by_owner(d_taps[:5]),
                by_owner(grad_conv_state),
                by_owner(grad_mixer[None, :]),
                jnp.broadcast_to(grad_head.reshape(1, -1), (fsdp_size, 3 * heads)),
            ],
            axis=1,
        )
        grad_extras = pad_cols(grad_extras, small_cols * shard).reshape(fsdp_size * shard, small_cols)
        grad_extras = jnp.concatenate([gain_sums[:, None], grad_extras], axis=1)
        side_part = side_part + jnp.pad(
            grad_extras, ((0, 0), (used, LANE - used - 1 - small_cols))
        )
        side_part = pair_sum(side_part, fsdp_index, fsdp_size)
        return chip_sum(side_part, fsdp_index, fsdp_size, after)

    def d_normed_of(distances, which):
        return d_normed_blocks(
            d_z, d_x, d_side, gate_all, x_all, normed, tp_index ^ jnp.array(distances), which, own_rows
        )

    if four:
        left_away, gains_one = d_normed_of([3, 1], 0)
        gains_one, sum_x = tied(gains_one, sum_x)
        right_away, gains_two = d_normed_of([3, 2], 1)
        gains_two, mixed_last, d_taps, d_skip, d_heads, grad_conv_state = tied(
            gains_two, mixed_last, d_taps, d_skip, d_heads, grad_conv_state
        )
        sent = [swap(left_away, 1, 4), swap(right_away, 2, 4)]
        left_kept, gains_three = d_normed_of([2, 0], 0)
        block_out = finish(
            block_out_kernel,
            "block_out",
            *scatter_end(mixed_kept, mixed_last),
            [block_in, live_rows.astype(F32)],
            own_rows,
            model,
        )
        sent[0], d_side_late, side_part, grad_out = tied(sent[0], d_side, side_part, grad_out)
        right_kept, gains_four = d_normed_blocks(
            d_z, d_x, d_side_late, gate_all, x_all, normed, tp_index ^ jnp.array([1, 0]), 1, own_rows
        )
        kept = [
            (left_kept[:own_rows], (left_kept, own_rows)),
            (right_kept[:own_rows], (right_kept, own_rows)),
        ]
        gain_sums = jnp.concatenate([gains_one + gains_three, gains_two + gains_four], axis=1)[0]
    else:
        block_out = finish(
            block_out_kernel,
            "block_out",
            *scatter_end(mixed_kept, mixed_last),
            [block_in, live_rows.astype(F32)],
            own_rows,
            model,
        )
        left, gains_one = d_normed_of(list(range(tp_size)), 0)
        right, gains_two = d_normed_of(list(range(tp_size)), 1)
        sent = [
            [
                swap(part[k * own_rows : (k + 1) * own_rows], k, tp_size)
                for k in range(1, tp_size)
            ]
            for part in (left, right)
        ]
        kept = [left[:own_rows], right[:own_rows]]
        gain_sums = jnp.concatenate([gains_one, gains_two], axis=1)[0]
    grad_x = chip_scatter(sum_x, fsdp_size)
    passed, kept = scatter_middle(sent, kept, own_rows, tp_size)
    grad_x, passed = tied(grad_x, passed)
    last = scatter_last(passed, tp_size)
    pair = adam_pair(
        lambda w, g, m, v: adamw_step(w, g, m, v, WEIGHT_DECAY, LEARN_RATE),
        grad_gate,
        grad_x,
        proj_inner,
        moments[1],
        moments[10],
    )
    grad_side, pair = side_gradient(
        side_part, d_taps, d_skip, d_heads, grad_conv_state, gain_sums, pair
    )
    grad_side, last[0] = tied(grad_side, last[0])
    grad_input_gain = all_sum(grad_side[:, used], tp_index, tp_size) / input_gain.astype(F32)
    d_input = finish(
        functools.partial(d_input_kernel, NORM_EPS),
        "d_input",
        *scatter_end(kept, last),
        [block_in, cotangent, gain_f[None, :]],
        own_rows,
        model,
    )

    own_extras = grad_side[:, used + 1 : used + 1 + small_cols].reshape(-1)
    grads = (
        grad_input_gain,
        None,
        grad_side[:, :heads],
        grad_side[:, heads:used],
        own_extras[:inner_n].reshape(conv_inner.shape),
        own_extras[inner_n : inner_n + state_n].reshape(conv_state.shape),
        own_extras[small_count : small_count + 3 * heads].reshape(3, heads),
        own_extras[inner_n + state_n : small_count],
        grad_out.astype(F32).T,
    )
    weights = (
        input_gain,
        proj_inner,
        proj_step,
        proj_state,
        conv_inner,
        conv_state,
        head_params,
        mixer_gain,
        proj_output,
    )
    large = (1, 2, 3, 8)
    grads = list(grads)
    updated = [None] * 9
    for at in range(9):
        decay = WEIGHT_DECAY if at in large else 0.0
        rate = LEARN_RATE if at in large else LEARN_SMALL
        if at == 1:
            grads[1], *updated[1] = pair
        else:
            updated[at] = adamw_step(
                weights[at], grads[at], moments[at], moments[9 + at], decay, rate
            )
    return (
        block_out,
        d_input,
        *grads,
        *[entry[0] for entry in updated],
        *[entry[1] for entry in updated],
        *[entry[2] for entry in updated],
    )


def weight_specs():
    return (
        P("fsdp"),
        P("fsdp", None, "tp"),
        P("fsdp", "tp"),
        P("fsdp", "tp"),
        P(None, ("tp", "fsdp")),
        P(None, ("tp", "fsdp")),
        P(None, "tp"),
        P(("tp", "fsdp")),
        P("tp", "fsdp"),
    )


def solution(mesh):
    rows = P(("fsdp", "tp"), None)
    return jax.shard_map(
        body,
        mesh=mesh,
        in_specs=(rows, rows, P("fsdp", None), P("fsdp")) + weight_specs() * 3,
        out_specs=(rows, rows) + weight_specs() * 4,
        check_vma=False,
    )
```
